32 devices in a mesh: dp: 8 (over z, x), blk: 4 (over y, core).
Axes of the slice: x: 2, y: 2, z: 4, core: 2. Of those that a mesh axis runs over, the one named last changes fastest.
Arguments:
- tokens: bfloat16 [8, 512, 1280], P('dp', 'blk')
- first_gain: float32 [1280], replicated, may hold values from 0.5 to 1.5
- first_shift: float32 [1280], replicated, may hold values from -3 to 3
- w_qkv: bfloat16 [1280, 3840], replicated, may hold values from -0.15625 to 0.15625
- w_out: bfloat16 [1280, 1280], replicated, may hold values from -2 to 2
- second_gain: float32 [1280], replicated, may hold values from 0.5 to 1.5
- second_shift: float32 [1280], replicated, may hold values from -3 to 3
- w_in: bfloat16 [1280, 5120], replicated, may hold values from -0.15625 to 0.15625
- w_down: bfloat16 [5120, 1280], replicated, may hold values from -0.078125 to 0.078125
- segment_ids: int32 [8, 512], P('dp', 'blk'), may hold values from 0 to 3, as said below
- cls_positions: int32 [8, 4], P('dp'), may hold values from 0 to 511, as said below
- out_grad: bfloat16 [8, 512, 1280], P('dp', 'blk'), may hold values from -6 to 6
Outputs:
- layer_out: bfloat16 [8, 512, 1280], P('dp', 'blk')
- tokens_grad: bfloat16 [8, 512, 1280], P('dp', 'blk')
- grad_qkv: float32 [1280, 3840], P(('dp', 'blk'))
- grad_out: float32 [1280, 1280], P(('dp', 'blk'))
- grad_in: float32 [1280, 5120], P(('dp', 'blk'))
- grad_down: float32 [5120, 1280], P(('dp', 'blk'))
- first_gain_grad: float32 [1280], P(('dp', 'blk'))
- first_shift_grad: float32 [1280], P(('dp', 'blk'))
- second_gain_grad: float32 [1280], P(('dp', 'blk'))
- second_shift_grad: float32 [1280], P(('dp', 'blk'))
- cls_mean: float32 [1280], P(('dp', 'blk'))
- cls_variance: float32 [1280], P(('dp', 'blk'))
The draws below stay inside these ranges and needn't reach their ends.
Inputs may be any that keep to these rules, and one draw needn't show every extreme that they name: `segment_ids`: in each row the numbers never fall, every cell number has at least one token, and one cell of every row has exactly 256 tokens. `cls_positions`: the first position of each cell of the row, in cell order, consistent with segment_ids.
All inputs are finite; a program needn't handle non-finite values.
Results may differ from the reference program's by a relative error of at most 0.013.
Values may be sent and summed in bfloat16 or wider, within the bound.
A program may use at most 320 MiB of HBM per device.

```python
import math
import jax
import jax.numpy as jnp
from jax import lax

D = 1280
H = 20
HD = 64
FF = 5120
CELLS = 4
LEN = 512
ROWS_ALL = 8


def draw_tokens(key, part):
    first, second = jax.random.split(key)
    rows = jnp.arange(ROWS_ALL, dtype=jnp.float32)[:, None]
    places = jnp.arange(LEN, dtype=jnp.float32)[None, :]
    fraction = (rows * LEN + places) / (ROWS_ALL * LEN)
    scale = jnp.exp(fraction * math.log(3.0))
    noise = jax.random.truncated_normal(first, -4.0, 4.0, (ROWS_ALL, LEN, D), jnp.float32)
    center = jax.random.uniform(second, (D,), jnp.float32, -1.0, 1.0)
    return (scale[:, :, None] * (noise + center[None, None, :])).astype(jnp.bfloat16)


def cell_layout(key):
    key = jax.random.fold_in(key, 7)
    first, second, third = jax.random.split(key, 3)
    half = LEN // 2
    cut_one = jax.random.randint(first, (ROWS_ALL,), 1, half)
    cut_two = jax.random.randint(second, (ROWS_ALL,), 1, half - 1)
    cut_two = cut_two + (cut_two >= cut_one).astype(jnp.int32)
    lower = jnp.minimum(cut_one, cut_two)
    upper = jnp.maximum(cut_one, cut_two)
    first_row = jnp.arange(ROWS_ALL, dtype=jnp.int32) == 0
    upper = jnp.where(first_row, jnp.int32(half - 1), upper)
    lower = jnp.where(first_row, jnp.minimum(lower, jnp.int32(half - 2)), lower)
    smalls = jnp.stack([lower, upper - lower, half - upper], axis=-1).astype(jnp.int32)
    place = jax.random.randint(third, (ROWS_ALL, 1), 0, CELLS)
    place = jnp.where(first_row[:, None], jnp.int32(0), place)
    slots = jnp.arange(CELLS, dtype=jnp.int32)[None, :]
    zeros_col = jnp.zeros((ROWS_ALL, 1), jnp.int32)
    early_pick = jnp.concatenate([smalls, zeros_col], axis=-1)
    later_pick = jnp.concatenate([zeros_col, smalls], axis=-1)
    lengths = jnp.where(slots < place, early_pick, jnp.where(slots == place, jnp.int32(half), later_pick))
    return (jnp.cumsum(lengths, axis=-1) - lengths).astype(jnp.int32)


def draw_segment_ids(key, part):
    starts = cell_layout(key)
    places = jnp.arange(LEN, dtype=jnp.int32)[None, None, :]
    return (jnp.sum((places >= starts[:, :, None]).astype(jnp.int32), axis=1) - 1).astype(jnp.int32)


def draw_cls_positions(key, part):
    return cell_layout(key)


def level_of(key, extent, cuts, smallest, largest):
    def one(dim, parts):
        heights = jax.random.uniform(jax.random.fold_in(jax.random.fold_in(key, 6), dim), (parts,), jnp.float32, smallest / len(cuts), largest / len(cuts))
        return jnp.repeat(jnp.exp(heights), extent[dim] // parts).reshape((-1,) + (1,) * (len(extent) - dim - 1))

    level = one(*cuts[0])
    for cut in cuts[1:]:
        level = level * one(*cut)
    return level


def centred(own_key, dims, scale, reach, cuts=(), kind=jnp.bfloat16):
    array = jax.random.normal(own_key, dims, jnp.float32) * scale
    if len(cuts) > 0:
        array = level_of(own_key, dims, cuts, -0.22, 0.18) * array
    return jnp.clip(array, min=-reach, max=reach).astype(kind)


def setup_inputs(seed: int = 0) -> dict:
    streams_of = jax.random.split(jax.random.key(seed), 13)
    return {
        "tokens": draw_tokens(jax.random.fold_in(streams_of[12], 71), 0),
        "first_gain": jnp.clip(1.0 + 0.1 * jax.random.normal(streams_of[1], (D,), jnp.float32), 0.5, 1.5),
        "first_shift": centred(streams_of[2], (D,), 0.2, 3.0, (), jnp.float32),
        "w_qkv": centred(streams_of[3], (D, 3 * D), D ** -0.5, 0.15625),
        "w_out": centred(streams_of[4], (D, D), (D // 128) ** -0.5, 2.0),
        "second_gain": jnp.clip(1.0 + 0.1 * jax.random.normal(streams_of[5], (D,), jnp.float32), 0.5, 1.5),
        "second_shift": centred(streams_of[6], (D,), 0.2, 3.0, (), jnp.float32),
        "w_in": centred(streams_of[7], (D, FF), D ** -0.5, 0.15625),
        "w_down": centred(streams_of[8], (FF, D), FF ** -0.5, 0.078125),
        "segment_ids": draw_segment_ids(jax.random.fold_in(streams_of[12], 71), 0),
        "cls_positions": draw_cls_positions(jax.random.fold_in(streams_of[12], 71), 0),
        "out_grad": centred(streams_of[11], (ROWS_ALL, LEN, D), 1.0, 6.0, ((0, 8), (1, 4))),
    }


@jax.custom_vjp
def low(v):
    return lax.optimization_barrier(v.astype(jnp.bfloat16)).astype(jnp.float32)

@jax.custom_vjp
def low_back(v):
    return v

def low_keep(v):
    return (low(v), None)

def low_pass(kept, grad):
    return (grad,)

def back_keep(v):
    return (v, None)

def back_low(kept, grad):
    return (low(grad),)
low.defvjp(low_keep, low_pass)
low_back.defvjp(back_keep, back_low)
EPSILON = 1e-05
HIGHEST_PRECISION = lax.Precision.HIGHEST

def layer_norm(values, gain, shift):
    center = values - lax.optimization_barrier(jnp.mean(values, axis=-1, keepdims=True))
    spread = lax.optimization_barrier(jnp.mean(center * center, axis=-1, keepdims=True))
    return center * lax.rsqrt(spread + EPSILON) * gain + shift

def matmul(left, right):
    return jnp.dot(left, right, precision=HIGHEST_PRECISION, preferred_element_type=jnp.float32)

def attend(item):
    queries, key_part, value_part, segment = item
    scores = low_back(matmul(queries, key_part.T))
    same = segment[:, None] == segment[None, :]
    exp_scores = jnp.where(same, jnp.exp(scores), jnp.float32(0.0))
    weights = lax.optimization_barrier(jnp.sum(exp_scores, axis=-1, keepdims=True))
    totals = low_back(matmul(low(exp_scores), value_part))
    return totals / weights

def split_heads(values):
    return values.reshape(ROWS_ALL, LEN, H, HD).transpose(0, 2, 1, 3).reshape(ROWS_ALL * H, LEN, HD)

def forward(wide, first_gain, first_shift, w_qkv, w_out, second_gain, second_shift, w_in, w_down, segment_rep):
    normed_low = low(layer_norm(wide, first_gain, first_shift))
    projected = low_back(matmul(normed_low, w_qkv))
    queries = low(projected[:, :D] * 0.125)
    key_part = low(projected[:, D:2 * D])
    value_part = low(projected[:, 2 * D:])
    attended = lax.map(jax.checkpoint(attend), (split_heads(queries), split_heads(key_part), split_heads(value_part), segment_rep))
    attended = attended.reshape(ROWS_ALL, H, LEN, HD).transpose(0, 2, 1, 3).reshape(ROWS_ALL * LEN, D)
    residual = wide + low_back(matmul(low(attended), w_out))
    normed_two_low = low(layer_norm(residual, second_gain, second_shift))
    hidden_pre = low_back(matmul(normed_two_low, w_in))
    hidden_low = low(jax.nn.gelu(hidden_pre, approximate=False))
    return residual + low_back(matmul(hidden_low, w_down))

def reference(tokens, first_gain, first_shift, w_qkv, w_out, second_gain, second_shift, w_in, w_down, segment_ids, cls_positions, out_grad):
    wide = tokens.astype(jnp.float32).reshape(ROWS_ALL * LEN, D)
    segment_rep = jnp.repeat(segment_ids, H, axis=0)

    def apply(wide_in, gain_one, shift_one, qkv_w, out_w, gain_two, shift_two, in_w, down_w):
        return forward(wide_in, gain_one, shift_one, qkv_w, out_w, gain_two, shift_two, in_w, down_w, segment_rep)
    layer, pull = jax.vjp(apply, wide, first_gain.astype(jnp.float32), first_shift.astype(jnp.float32), w_qkv.astype(jnp.float32), w_out.astype(jnp.float32), second_gain.astype(jnp.float32), second_shift.astype(jnp.float32), w_in.astype(jnp.float32), w_down.astype(jnp.float32))
    grads = pull(out_grad.astype(jnp.float32).reshape(ROWS_ALL * LEN, D))
    layer_rows = layer.reshape(ROWS_ALL, LEN, D)
    embedded = jnp.take_along_axis(layer_rows, cls_positions.astype(jnp.int32)[:, :, None], axis=1)
    count = ROWS_ALL * CELLS
    cls_mean = lax.optimization_barrier(jnp.sum(embedded, axis=(0, 1))) / count
    cls_variance = lax.optimization_barrier(jnp.sum(embedded * embedded, axis=(0, 1))) / count - cls_mean * cls_mean
    return (layer_rows.astype(jnp.bfloat16), grads[0].reshape(ROWS_ALL, LEN, D).astype(jnp.bfloat16), grads[3], grads[4], grads[7], grads[8], grads[1], grads[2], grads[5], grads[6], cls_mean, cls_variance)
```

```python
import jax
import jax.numpy as jnp
from jax import lax
from jax.experimental import pallas as pl
from jax.experimental.pallas import tpu as pltpu
from jax.sharding import PartitionSpec as P

H = 20


EPSILON = 1e-05


def shifted(block, axis, distance):
    devices = range(lax.axis_size(axis))
    route = [((i - distance) % len(devices), i) for i in devices]
    return lax.ppermute(block, axis, route)


def layer_norm(values, gain, shift):
    center = values - jnp.mean(values, axis=-1, keepdims=True)
    spread = jnp.mean(center * center, axis=-1, keepdims=True)
    return center * lax.rsqrt(spread + EPSILON) * gain + shift


def exact_gelu(values):
    return jax.nn.gelu(values, approximate=False)


def same_cells(query_cells, key_cells):
    return query_cells[:, :, None] == key_cells[:, None, :]


def forward_block(queries, key_part, value_part, query_cells, key_cells, totals, weights):
    scores = jnp.einsum("sqhd,skhd->shqk", queries, key_part, preferred_element_type=jnp.float32)
    exp_scores = jnp.where(same_cells(query_cells, key_cells)[:, None], jnp.exp(scores), 0.0)
    weights = weights + jnp.sum(exp_scores, axis=-1)
    totals = totals + jnp.einsum(
        "shqk,skhd->sqhd",
        exp_scores.astype(jnp.bfloat16),
        value_part,
        preferred_element_type=jnp.float32,
    )
    return (totals, weights)


def backward_block(queries, scaled, deltas, query_cells, key_part, value_part, key_cells):
    scores = jnp.einsum("sqhd,skhd->shqk", queries, key_part, preferred_element_type=jnp.float32)
    exp_scores = jnp.where(same_cells(query_cells, key_cells)[:, None], jnp.exp(scores), 0.0)
    grad_exp = jnp.einsum("sqhd,skhd->shqk", scaled, value_part, preferred_element_type=jnp.float32)
    grad_scores = (exp_scores * (grad_exp - deltas[..., None])).astype(jnp.bfloat16)
    grad_queries = jnp.einsum(
        "shqk,skhd->sqhd", grad_scores, key_part, preferred_element_type=jnp.float32
    )
    grad_keys = jnp.einsum(
        "shqk,sqhd->skhd", grad_scores, queries, preferred_element_type=jnp.float32
    )
    grad_values = jnp.einsum(
        "shqk,sqhd->skhd",
        exp_scores.astype(jnp.bfloat16),
        scaled,
        preferred_element_type=jnp.float32,
    )
    return (grad_queries, grad_keys, grad_values)


MESH = pl.DeviceIdType.MESH
F32 = jnp.float32
BF16 = jnp.bfloat16
NN = (((1,), (0,)), ((), ()))
NT = (((1,), (1,)), ((), ()))


def mm(left, right, dims=NN):
    return lax.dot_general(left, right, dims, preferred_element_type=F32)


def remote(src, dst, send, recv, target):
    return pltpu.make_async_remote_copy(
        src_ref=src, dst_ref=dst, send_sem=send, recv_sem=recv, device_id=target, device_id_type=MESH
    )


def greet(targets):
    barrier = pltpu.get_barrier_semaphore()
    for target in targets:
        pl.semaphore_signal(barrier, inc=1, device_id=target, device_id_type=MESH)
    pl.semaphore_wait(barrier, len(targets))


def place():
    dp, blk = lax.axis_index("dp"), lax.axis_index("blk")
    return dp, blk, dp // 2, lax.rem(dp, 2), blk // 2, lax.rem(blk, 2)


def ffn_grads_kernel(
    x_ref, g_ref, win_ref, wdown_ref, down_ref, in_ref,
    gx, gg, wi, wd, xt, gp, ht, part_in, part_dn, sib_in, sib_dn, ysend_in, ysend_dn, yrecv_in, yrecv_dn, slab, slab_in,
    wsem, gsend, grecv, ssend, srecv, ysend, yrecv, qsend, qrecv,
):
    dp, blk, z, x, y, c = place()
    width = x_ref.shape[1]
    tokens = x_ref.shape[0]
    cut = wi.shape[1]
    owned = down_ref.shape[0]
    rows = in_ref.shape[0]
    load_in = pltpu.make_async_copy(win_ref.at[:, pl.ds(pl.multiple_of(dp * cut, cut), cut)], wi, wsem.at[0])
    load_dn = pltpu.make_async_copy(wdown_ref.at[pl.ds(pl.multiple_of(dp * cut, cut), cut), :], wd, wsem.at[1])
    load_in.start()
    load_dn.start()
    gx[0] = x_ref[...]
    gg[0] = g_ref[...]
    sibling = (dp, 2 * y + (1 - c))
    ypeer = (dp, 2 * (1 - y) + c)
    xpeer = (2 * z + (1 - x), blk)
    greet([(lax.rem(dp + k, 8), blk) for k in range(1, 8)] + [sibling, ypeer])

    def gather(slot, target_slot, target):
        return (
            remote(gx.at[slot], gx.at[target_slot], gsend.at[0, target_slot], grecv.at[0, target_slot], target),
            remote(gg.at[slot], gg.at[target_slot], gsend.at[1, target_slot], grecv.at[1, target_slot], target),
        )

    for k in range(1, 4):
        for copy in gather(0, k, (2 * lax.rem(z + k, 4) + x, blk)):
            copy.start()
    for copy in gather(0, 4, xpeer):
        copy.start()
    load_in.wait()
    load_dn.wait()

    def make(slot):
        xs = gx[slot]
        place_at = pl.ds(pl.multiple_of(slot * tokens, tokens), tokens)
        xt[:, place_at] = xs.T
        pre = mm(xs, wi[...])
        cdf = 0.5 * (1.0 + lax.erf(pre * 0.7071067811865476))
        ht[:, place_at] = (pre * cdf).astype(BF16).T
        slope = cdf + pre * (0.3989422804014327 * jnp.exp(-0.5 * pre * pre))
        gp[place_at, :] = (mm(gg[slot], wd[...], NT) * slope).astype(BF16)

    make(0)

    @pl.loop(1, 4)
    def _(slot):
        for copy in gather(slot, slot, xpeer):
            copy.wait_recv()
        for copy in gather(slot, slot + 4, xpeer):
            copy.start()
        make(slot)

    @pl.loop(4, 8)
    def _(slot):
        for copy in gather(slot, slot, xpeer):
            copy.wait_recv()
        make(slot)

    @pl.loop(0, 4)
    def _(pair):
        made = mm(xt[pl.ds(pl.multiple_of(pair * 2 * owned, 2 * owned), 2 * owned), :], gp[...])
        for half in range(2):
            for q in range(4):
                at = half * owned + q * rows
                part_in[q, 2 * pair + half] = made[at : at + rows].astype(BF16)

    to_sibling = []
    for kind, part, landing in ((0, part_in, sib_in), (1, part_dn, sib_dn)):
        for yy in range(2):
            away = part.at[2 * yy + (1 - c)]
            to_sibling.append(remote(away, landing.at[yy], ssend.at[kind, yy], srecv.at[kind, yy], sibling))
    to_sibling[0].start()
    to_sibling[1].start()
    every = gg[...].reshape(8 * tokens, width)

    @pl.loop(0, 4)
    def _(q):
        part_dn[q] = mm(ht[pl.ds(pl.multiple_of(q * owned, owned), owned), :], every).astype(BF16)

    to_sibling[2].start()
    to_sibling[3].start()
    over = 2 * (1 - y) + c
    mine = 2 * y + c
    for copy in to_sibling:
        copy.wait()
    ysend_in[...] = (part_in[over].astype(F32) + sib_in[1 - y].astype(F32)).astype(BF16)
    ysend_dn[...] = (part_dn[over].astype(F32) + sib_dn[1 - y].astype(F32)).astype(BF16)
    to_y = (
        remote(ysend_in, yrecv_in, ysend.at[0], yrecv.at[0], ypeer),
        remote(ysend_dn, yrecv_dn, ysend.at[1], yrecv.at[1], ypeer),
    )
    for copy in to_y:
        copy.start()
    to_y[0].wait()
    slab[...] = (part_in[mine].astype(F32) + sib_in[y].astype(F32) + yrecv_in[...].astype(F32)).astype(BF16)
    to_q = []
    for k in range(1, 8):
        target = lax.rem(dp + k, 8)
        to_q.append(remote(slab.at[target], slab_in.at[dp], qsend.at[k], qrecv.at[k], (target, blk)))
        to_q[-1].start()
    slab_in[dp] = slab[dp]
    to_y[1].wait()
    down_ref[...] = part_dn[mine].astype(F32) + sib_dn[y].astype(F32) + yrecv_dn[...].astype(F32)
    for copy in to_q:
        copy.wait()
    for s in range(8):
        in_ref[:, s * cut : (s + 1) * cut] = slab_in[s].astype(F32)
    for k in range(1, 4):
        for copy in gather(0, k, xpeer):
            copy.wait_send()
    for k in range(0, 4):
        for copy in gather(k, 4 + k, xpeer):
            copy.wait_send()


def ffn_grads(normed, grad, w_in, w_down):
    tokens, width = normed.shape
    inner = w_in.shape[1]
    cut, owned, rows = inner // 8, inner // 32, width // 32
    v = pltpu.VMEM
    dma = pltpu.SemaphoreType.DMA
    flops = 2 * 8 * tokens * width * cut * 4
    return pl.pallas_call(
        ffn_grads_kernel,
        out_shape=(jax.ShapeDtypeStruct((owned, width), F32), jax.ShapeDtypeStruct((rows, inner), F32)),
        in_specs=[pl.BlockSpec(memory_space=v)] * 2 + [pl.BlockSpec(memory_space=pl.ANY)] * 2,
        out_specs=(pl.BlockSpec(memory_space=v),) * 2,
        scratch_shapes=[
            v((8, tokens, width), BF16), v((8, tokens, width), BF16),
            v((width, cut), BF16), v((cut, width), BF16),
            v((width, 8 * tokens), BF16), v((8 * tokens, cut), BF16), v((cut, 8 * tokens), BF16),
            v((4, 8, rows, cut), BF16), v((4, owned, width), BF16),
            v((2, 8, rows, cut), BF16), v((2, owned, width), BF16),
            v((8, rows, cut), BF16), v((owned, width), BF16),
            v((8, rows, cut), BF16), v((owned, width), BF16),
            v((8, rows, cut), BF16), v((8, rows, cut), BF16),
            dma((2,)), dma((2, 8)), dma((2, 8)), dma((2, 2)), dma((2, 2)), dma((2,)), dma((2,)), dma((8,)), dma((8,)),
        ],
        compiler_params=pltpu.CompilerParams(collective_id=1, has_side_effects=True, vmem_limit_bytes=60 * 2**20),
        cost_estimate=pl.CostEstimate(flops=flops, bytes_accessed=8 * 2**20, transcendentals=0),
    )(normed, grad, w_in, w_down)


def on_device(
    tokens,
    first_gain,
    first_shift,
    w_qkv,
    w_out,
    second_gain,
    second_shift,
    w_in,
    w_down,
    segment_ids,
    cls_positions,
    out_grad,
):
    seqs_here, block_len, width = tokens.shape
    head_count = H
    head_size = width // head_count
    blocks = lax.axis_size("blk")
    head_shape = (seqs_here, block_len, head_count, head_size)
    flat_shape = (seqs_here, block_len, width)
    tokens_wide = tokens.astype(jnp.float32)
    normed_low = layer_norm(tokens_wide, first_gain, first_shift).astype(jnp.bfloat16)
    projected = jnp.dot(normed_low, w_qkv, preferred_element_type=jnp.float32)
    queries = (projected[..., :width] * 0.125).astype(jnp.bfloat16).reshape(head_shape)
    key_part = projected[..., width : 2 * width].astype(jnp.bfloat16).reshape(head_shape)
    value_part = projected[..., 2 * width :].astype(jnp.bfloat16).reshape(head_shape)
    totals = jnp.zeros(head_shape, jnp.float32)
    weights = jnp.zeros((seqs_here, head_count, block_len), jnp.float32)
    totals, weights = forward_block(
        queries, key_part, value_part, segment_ids, segment_ids, totals, weights
    )

    def forward_step(position, loop_state):
        moving, totals_in, weights_in = loop_state
        moving = shifted((moving[0], moving[1], moving[2]), "blk", 1)
        totals_out, weights_out = forward_block(
            queries, moving[0], moving[1], segment_ids, moving[2], totals_in, weights_in
        )
        return (moving, totals_out, weights_out)

    moved_state, totals, weights = lax.fori_loop(
        0, blocks - 1, forward_step, ((key_part, value_part, segment_ids), totals, weights)
    )
    weights_rows = jnp.swapaxes(weights, 1, 2)[..., None]
    attended = totals / weights_rows
    attended_low = attended.reshape(flat_shape).astype(jnp.bfloat16)
    residual = tokens_wide + jnp.dot(attended_low, w_out, preferred_element_type=jnp.float32)
    normed_two_low = layer_norm(residual, second_gain, second_shift).astype(jnp.bfloat16)
    hidden_pre = jnp.dot(normed_two_low, w_in, preferred_element_type=jnp.float32)
    hidden_low = exact_gelu(hidden_pre).astype(jnp.bfloat16)
    layer = residual + jnp.dot(hidden_low, w_down, preferred_element_type=jnp.float32)
    offset = lax.axis_index("blk") * block_len
    places = (
        lax.broadcasted_iota(jnp.int32, (seqs_here, cls_positions.shape[1], block_len), 2) + offset
    )
    chosen = jnp.sum((places == cls_positions[:, :, None]).astype(jnp.float32), axis=1)
    cell_sums = jnp.sum(chosen[..., None] * layer, axis=(0, 1))
    cell_squares = jnp.sum(chosen[..., None] * layer * layer, axis=(0, 1))
    count = cls_positions.shape[0] * cls_positions.shape[1] * lax.axis_size("dp")
    share = width // (lax.axis_size("dp") * blocks)
    moment_sums = lax.psum((cell_sums, cell_squares), ("dp", "blk"))
    rank = lax.axis_index("dp") * blocks + lax.axis_index("blk")
    sum_share = lax.dynamic_slice_in_dim(moment_sums[0], rank * share, share)
    square_share = lax.dynamic_slice_in_dim(moment_sums[1], rank * share, share)
    grad_layer = out_grad.astype(jnp.float32)
    grad_hidden = jnp.einsum("sbd,fd->sbf", out_grad, w_down, preferred_element_type=jnp.float32)
    grad_pre = jax.vjp(exact_gelu, hidden_pre)[1](grad_hidden)[0].astype(jnp.bfloat16)
    if lax.axis_size("dp") == 8 and blocks == 4 and seqs_here == 1:
        grad_down, grad_in = ffn_grads(normed_two_low[0], out_grad[0], w_in, w_down)
    else:
        grad_down = jnp.einsum("sbf,sbd->fd", hidden_low, out_grad, preferred_element_type=jnp.float32)
        grad_in = jnp.einsum(
            "sbd,sbf->df", normed_two_low, grad_pre, preferred_element_type=jnp.float32
        )
        grad_in = lax.psum_scatter(grad_in, ("dp", "blk"), scatter_dimension=0, tiled=True)
        grad_down = lax.psum_scatter(grad_down, ("dp", "blk"), scatter_dimension=0, tiled=True)
    grad_normed_two = jnp.einsum("sbf,df->sbd", grad_pre, w_in, preferred_element_type=jnp.float32)
    unused_two, pull_two = jax.vjp(layer_norm, residual, second_gain, second_shift)
    residual_part, second_gain_grad, second_shift_grad = pull_two(grad_normed_two)
    grad_residual = grad_layer + residual_part
    grad_proj = grad_residual.astype(jnp.bfloat16)
    grad_out = jnp.einsum(
        "sbd,sbe->de", attended_low, grad_proj, preferred_element_type=jnp.float32
    )
    grad_attended = jnp.einsum(
        "sbe,de->sbd", grad_proj, w_out, preferred_element_type=jnp.float32
    ).reshape(head_shape)
    scaled = (grad_attended / weights_rows).astype(jnp.bfloat16)
    deltas = jnp.swapaxes(jnp.sum(grad_attended * attended, axis=-1), 1, 2) / weights

    def key_step(position, loop_state):
        moving, key_sums, query_sum = loop_state
        grad_queries, grad_keys, grad_values = backward_block(
            queries, scaled, deltas, segment_ids, moving[0], moving[1], moving[2]
        )
        query_next = query_sum + grad_queries
        keys_next = key_sums[0] + grad_keys
        values_next = key_sums[1] + grad_values
        moving = shifted((moving[0], moving[1], moving[2]), "blk", 1)
        key_sums = (
            shifted(keys_next.astype(jnp.bfloat16), "blk", 1).astype(keys_next.dtype),
            shifted(values_next.astype(jnp.bfloat16), "blk", 1).astype(values_next.dtype),
        )
        return (moving, key_sums, query_next)

    zero_heads = jnp.zeros(head_shape, jnp.float32)
    moved_back, key_sums, query_total = lax.fori_loop(
        0,
        blocks,
        key_step,
        ((key_part, value_part, segment_ids), (zero_heads, zero_heads), zero_heads),
    )
    keys_total, values_total = (key_sums[0], key_sums[1])
    grad_qkv_low = jnp.concatenate(
        [
            (query_total * 0.125).reshape(flat_shape),
            keys_total.reshape(flat_shape),
            values_total.reshape(flat_shape),
        ],
        axis=-1,
    ).astype(jnp.bfloat16)
    grad_qkv = jnp.einsum(
        "sbd,sbe->de", normed_low, grad_qkv_low, preferred_element_type=jnp.float32
    )
    grad_normed_one = jnp.einsum(
        "sbe,de->sbd", grad_qkv_low, w_qkv, preferred_element_type=jnp.float32
    )
    unused_one, pull_one = jax.vjp(layer_norm, tokens_wide, first_gain, first_shift)
    tokens_part, first_gain_grad, first_shift_grad = pull_one(grad_normed_one)
    tokens_grad = (grad_residual + tokens_part).astype(jnp.bfloat16)
    summed = (
        lax.psum_scatter(grad_qkv, ("dp", "blk"), scatter_dimension=0, tiled=True),
        lax.psum_scatter(grad_out, ("dp", "blk"), scatter_dimension=0, tiled=True),
        grad_in,
        grad_down,
        lax.psum_scatter(first_gain_grad, ("dp", "blk"), scatter_dimension=0, tiled=True),
        lax.psum_scatter(first_shift_grad, ("dp", "blk"), scatter_dimension=0, tiled=True),
        lax.psum_scatter(second_gain_grad, ("dp", "blk"), scatter_dimension=0, tiled=True),
        lax.psum_scatter(second_shift_grad, ("dp", "blk"), scatter_dimension=0, tiled=True),
    )
    cls_mean = sum_share / count
    cls_variance = square_share / count - cls_mean * cls_mean
    return (
        layer.astype(jnp.bfloat16),
        tokens_grad,
        summed[0],
        summed[1],
        summed[2],
        summed[3],
        summed[4],
        summed[5],
        summed[6],
        summed[7],
        cls_mean,
        cls_variance,
    )


def solution(mesh):
    placed = (
        P("dp", "blk", None),
        P(),
        P(),
        P(),
        P(),
        P(),
        P(),
        P(),
        P(),
        P("dp", "blk"),
        P("dp", None),
        P("dp", "blk", None),
    )
    return jax.shard_map(
        on_device,
        mesh=mesh,
        in_specs=placed,
        out_specs=(
            P("dp", "blk", None),
            P("dp", "blk", None),
            P(("dp", "blk"), None),
            P(("dp", "blk"), None),
            P(("dp", "blk"), None),
            P(("dp", "blk"), None),
            P(("dp", "blk")),
            P(("dp", "blk")),
            P(("dp", "blk")),
            P(("dp", "blk")),
            P(("dp", "blk")),
            P(("dp", "blk")),
        ),
        check_vma=False,
    )
```

```python
import jax
import jax.numpy as jnp
from jax import lax
from jax.experimental import pallas as pl
from jax.experimental.pallas import tpu as pltpu
from jax.sharding import PartitionSpec as P

H = 20


EPSILON = 1e-05


def shifted(block, axis, distance):
    devices = range(lax.axis_size(axis))
    route = [((i - distance) % len(devices), i) for i in devices]
    return lax.ppermute(block, axis, route)


def layer_norm(values, gain, shift):
    center = values - jnp.mean(values, axis=-1, keepdims=True)
    spread = jnp.mean(center * center, axis=-1, keepdims=True)
    return center * lax.rsqrt(spread + EPSILON) * gain + shift


def exact_gelu(values):
    return jax.nn.gelu(values, approximate=False)


def same_cells(query_cells, key_cells):
    return query_cells[:, :, None] == key_cells[:, None, :]


def forward_block(queries, key_part, value_part, query_cells, key_cells, totals, weights):
    scores = jnp.einsum("sqhd,skhd->shqk", queries, key_part, preferred_element_type=jnp.float32)
    exp_scores = jnp.where(same_cells(query_cells, key_cells)[:, None], jnp.exp(scores), 0.0)
    weights = weights + jnp.sum(exp_scores, axis=-1)
    totals = totals + jnp.einsum(
        "shqk,skhd->sqhd",
        exp_scores.astype(jnp.bfloat16),
        value_part,
        preferred_element_type=jnp.float32,
    )
    return (totals, weights)


def backward_block(queries, scaled, deltas, query_cells, key_part, value_part, key_cells):
    scores = jnp.einsum("sqhd,skhd->shqk", queries, key_part, preferred_element_type=jnp.float32)
    exp_scores = jnp.where(same_cells(query_cells, key_cells)[:, None], jnp.exp(scores), 0.0)
    grad_exp = jnp.einsum("sqhd,skhd->shqk", scaled, value_part, preferred_element_type=jnp.float32)
    grad_scores = (exp_scores * (grad_exp - deltas[..., None])).astype(jnp.bfloat16)
    grad_queries = jnp.einsum(
        "shqk,skhd->sqhd", grad_scores, key_part, preferred_element_type=jnp.float32
    )
    grad_keys = jnp.einsum(
        "shqk,sqhd->skhd", grad_scores, queries, preferred_element_type=jnp.float32
    )
    grad_values = jnp.einsum(
        "shqk,sqhd->skhd",
        exp_scores.astype(jnp.bfloat16),
        scaled,
        preferred_element_type=jnp.float32,
    )
    return (grad_queries, grad_keys, grad_values)


def on_device_general(
    tokens,
    first_gain,
    first_shift,
    w_qkv,
    w_out,
    second_gain,
    second_shift,
    w_in,
    w_down,
    segment_ids,
    cls_positions,
    out_grad,
):
    seqs_here, block_len, width = tokens.shape
    head_count = H
    head_size = width // head_count
    blocks = lax.axis_size("blk")
    head_shape = (seqs_here, block_len, head_count, head_size)
    flat_shape = (seqs_here, block_len, width)
    tokens_wide = tokens.astype(jnp.float32)
    normed_low = layer_norm(tokens_wide, first_gain, first_shift).astype(jnp.bfloat16)
    projected = jnp.dot(normed_low, w_qkv, preferred_element_type=jnp.float32)
    queries = (projected[..., :width] * 0.125).astype(jnp.bfloat16).reshape(head_shape)
    key_part = projected[..., width : 2 * width].astype(jnp.bfloat16).reshape(head_shape)
    value_part = projected[..., 2 * width :].astype(jnp.bfloat16).reshape(head_shape)
    totals = jnp.zeros(head_shape, jnp.float32)
    weights = jnp.zeros((seqs_here, head_count, block_len), jnp.float32)
    totals, weights = forward_block(
        queries, key_part, value_part, segment_ids, segment_ids, totals, weights
    )

    def forward_step(position, loop_state):
        moving, totals_in, weights_in = loop_state
        moving = shifted((moving[0], moving[1], moving[2]), "blk", 1)
        totals_out, weights_out = forward_block(
            queries, moving[0], moving[1], segment_ids, moving[2], totals_in, weights_in
        )
        return (moving, totals_out, weights_out)

    moved_state, totals, weights = lax.fori_loop(
        0, blocks - 1, forward_step, ((key_part, value_part, segment_ids), totals, weights)
    )
    weights_rows = jnp.swapaxes(weights, 1, 2)[..., None]
    attended = totals / weights_rows
    attended_low = attended.reshape(flat_shape).astype(jnp.bfloat16)
    residual = tokens_wide + jnp.dot(attended_low, w_out, preferred_element_type=jnp.float32)
    normed_two_low = layer_norm(residual, second_gain, second_shift).astype(jnp.bfloat16)
    hidden_pre = jnp.dot(normed_two_low, w_in, preferred_element_type=jnp.float32)
    hidden_low = exact_gelu(hidden_pre).astype(jnp.bfloat16)
    layer = residual + jnp.dot(hidden_low, w_down, preferred_element_type=jnp.float32)
    offset = lax.axis_index("blk") * block_len
    places = (
        lax.broadcasted_iota(jnp.int32, (seqs_here, cls_positions.shape[1], block_len), 2) + offset
    )
    chosen = jnp.sum((places == cls_positions[:, :, None]).astype(jnp.float32), axis=1)
    cell_sums = jnp.sum(chosen[..., None] * layer, axis=(0, 1))
    cell_squares = jnp.sum(chosen[..., None] * layer * layer, axis=(0, 1))
    count = cls_positions.shape[0] * cls_positions.shape[1] * lax.axis_size("dp")
    share = width // (lax.axis_size("dp") * blocks)
    moment_sums = lax.psum((cell_sums, cell_squares), ("dp", "blk"))
    rank = lax.axis_index("dp") * blocks + lax.axis_index("blk")
    sum_share = lax.dynamic_slice_in_dim(moment_sums[0], rank * share, share)
    square_share = lax.dynamic_slice_in_dim(moment_sums[1], rank * share, share)
    grad_layer = out_grad.astype(jnp.float32)
    grad_down = jnp.einsum("sbf,sbd->fd", hidden_low, out_grad, preferred_element_type=jnp.float32)
    grad_hidden = jnp.einsum("sbd,fd->sbf", out_grad, w_down, preferred_element_type=jnp.float32)
    grad_pre = jax.vjp(exact_gelu, hidden_pre)[1](grad_hidden)[0].astype(jnp.bfloat16)
    grad_in = jnp.einsum(
        "sbd,sbf->df", normed_two_low, grad_pre, preferred_element_type=jnp.float32
    )
    grad_normed_two = jnp.einsum("sbf,df->sbd", grad_pre, w_in, preferred_element_type=jnp.float32)
    unused_two, pull_two = jax.vjp(layer_norm, residual, second_gain, second_shift)
    residual_part, second_gain_grad, second_shift_grad = pull_two(grad_normed_two)
    grad_residual = grad_layer + residual_part
    grad_proj = grad_residual.astype(jnp.bfloat16)
    grad_out = jnp.einsum(
        "sbd,sbe->de", attended_low, grad_proj, preferred_element_type=jnp.float32
    )
    grad_attended = jnp.einsum(
        "sbe,de->sbd", grad_proj, w_out, preferred_element_type=jnp.float32
    ).reshape(head_shape)
    scaled = (grad_attended / weights_rows).astype(jnp.bfloat16)
    deltas = jnp.swapaxes(jnp.sum(grad_attended * attended, axis=-1), 1, 2) / weights

    def key_step(position, loop_state):
        moving, key_sums, query_sum = loop_state
        grad_queries, grad_keys, grad_values = backward_block(
            queries, scaled, deltas, segment_ids, moving[0], moving[1], moving[2]
        )
        query_next = query_sum + grad_queries
        keys_next = key_sums[0] + grad_keys
        values_next = key_sums[1] + grad_values
        moving = shifted((moving[0], moving[1], moving[2]), "blk", 1)
        key_sums = (
            shifted(keys_next.astype(jnp.bfloat16), "blk", 1).astype(keys_next.dtype),
            shifted(values_next.astype(jnp.bfloat16), "blk", 1).astype(values_next.dtype),
        )
        return (moving, key_sums, query_next)

    zero_heads = jnp.zeros(head_shape, jnp.float32)
    moved_back, key_sums, query_total = lax.fori_loop(
        0,
        blocks,
        key_step,
        ((key_part, value_part, segment_ids), (zero_heads, zero_heads), zero_heads),
    )
    keys_total, values_total = (key_sums[0], key_sums[1])
    grad_qkv_low = jnp.concatenate(
        [
            (query_total * 0.125).reshape(flat_shape),
            keys_total.reshape(flat_shape),
            values_total.reshape(flat_shape),
        ],
        axis=-1,
    ).astype(jnp.bfloat16)
    grad_qkv = jnp.einsum(
        "sbd,sbe->de", normed_low, grad_qkv_low, preferred_element_type=jnp.float32
    )
    grad_normed_one = jnp.einsum(
        "sbe,de->sbd", grad_qkv_low, w_qkv, preferred_element_type=jnp.float32
    )
    unused_one, pull_one = jax.vjp(layer_norm, tokens_wide, first_gain, first_shift)
    tokens_part, first_gain_grad, first_shift_grad = pull_one(grad_normed_one)
    tokens_grad = (grad_residual + tokens_part).astype(jnp.bfloat16)
    summed = (
        lax.psum_scatter(grad_qkv, ("dp", "blk"), scatter_dimension=0, tiled=True),
        lax.psum_scatter(grad_out, ("dp", "blk"), scatter_dimension=0, tiled=True),
        lax.psum_scatter(grad_in, ("dp", "blk"), scatter_dimension=0, tiled=True),
        lax.psum_scatter(grad_down, ("dp", "blk"), scatter_dimension=0, tiled=True),
        lax.psum_scatter(first_gain_grad, ("dp", "blk"), scatter_dimension=0, tiled=True),
        lax.psum_scatter(first_shift_grad, ("dp", "blk"), scatter_dimension=0, tiled=True),
        lax.psum_scatter(second_gain_grad, ("dp", "blk"), scatter_dimension=0, tiled=True),
        lax.psum_scatter(second_shift_grad, ("dp", "blk"), scatter_dimension=0, tiled=True),
    )
    cls_mean = sum_share / count
    cls_variance = square_share / count - cls_mean * cls_mean
    return (
        layer.astype(jnp.bfloat16),
        tokens_grad,
        summed[0],
        summed[1],
        summed[2],
        summed[3],
        summed[4],
        summed[5],
        summed[6],
        summed[7],
        cls_mean,
        cls_variance,
    )


MESH = pl.DeviceIdType.MESH
F32 = jnp.float32
BF16 = jnp.bfloat16
NN = (((1,), (0,)), ((), ()))
NT = (((1,), (1,)), ((), ()))


def mm(left, right, dims=NN):
    return lax.dot_general(left, right, dims, preferred_element_type=F32)


def remote(src, dst, send, recv, target):
    return pltpu.make_async_remote_copy(
        src_ref=src, dst_ref=dst, send_sem=send, recv_sem=recv, device_id=target, device_id_type=MESH
    )


def greet(targets):
    barrier = pltpu.get_barrier_semaphore()
    for target in targets:
        pl.semaphore_signal(barrier, inc=1, device_id=target, device_id_type=MESH)
    pl.semaphore_wait(barrier, len(targets))


def place():
    dp, blk = lax.axis_index("dp"), lax.axis_index("blk")
    return dp, blk, dp // 2, lax.rem(dp, 2), blk // 2, lax.rem(blk, 2)


def ffn_grads_kernel(
    x_ref, g_ref, win_ref, wdown_ref, down_ref, in_ref,
    gx, gg, wi, wd, xt, gp, ht, part_in, part_dn, sib_in, sib_dn, ysend_in, ysend_dn, yrecv_in, yrecv_dn, slab, slab_in,
    wsem, gsend, grecv, ssend, srecv, ysend, yrecv, qsend, qrecv,
):
    dp, blk, z, x, y, c = place()
    width = x_ref.shape[1]
    tokens = x_ref.shape[0]
    cut = wi.shape[1]
    owned = down_ref.shape[0]
    rows = in_ref.shape[0]
    load_in = pltpu.make_async_copy(win_ref.at[:, pl.ds(pl.multiple_of(dp * cut, cut), cut)], wi, wsem.at[0])
    load_dn = pltpu.make_async_copy(wdown_ref.at[pl.ds(pl.multiple_of(dp * cut, cut), cut), :], wd, wsem.at[1])
    load_in.start()
    load_dn.start()
    gx[0] = x_ref[...]
    gg[0] = g_ref[...]
    sibling = (dp, 2 * y + (1 - c))
    ypeer = (dp, 2 * (1 - y) + c)
    xpeer = (2 * z + (1 - x), blk)
    greet([(lax.rem(dp + k, 8), blk) for k in range(1, 8)] + [sibling, ypeer])

    def gather(slot, target_slot, target):
        return (
            remote(gx.at[slot], gx.at[target_slot], gsend.at[0, target_slot], grecv.at[0, target_slot], target),
            remote(gg.at[slot], gg.at[target_slot], gsend.at[1, target_slot], grecv.at[1, target_slot], target),
        )

    for k in range(1, 4):
        for copy in gather(0, k, (2 * lax.rem(z + k, 4) + x, blk)):
            copy.start()
    for copy in gather(0, 4, xpeer):
        copy.start()
    load_in.wait()
    load_dn.wait()

    def make(slot):
        xs = gx[slot]
        place_at = pl.ds(pl.multiple_of(slot * tokens, tokens), tokens)
        xt[:, place_at] = xs.T
        pre = mm(xs, wi[...])
        cdf = 0.5 * (1.0 + lax.erf(pre * 0.7071067811865476))
        ht[:, place_at] = (pre * cdf).astype(BF16).T
        slope = cdf + pre * (0.3989422804014327 * jnp.exp(-0.5 * pre * pre))
        gp[place_at, :] = (mm(gg[slot], wd[...], NT) * slope).astype(BF16)

    make(0)

    @pl.loop(1, 4)
    def _(slot):
        for copy in gather(slot, slot, xpeer):
            copy.wait_recv()
        for copy in gather(slot, slot + 4, xpeer):
            copy.start()
        make(slot)

    @pl.loop(4, 8)
    def _(slot):
        for copy in gather(slot, slot, xpeer):
            copy.wait_recv()
        make(slot)

    @pl.loop(0, 4)
    def _(pair):
        made = mm(xt[pl.ds(pl.multiple_of(pair * 2 * owned, 2 * owned), 2 * owned), :], gp[...])
        for half in range(2):
            for q in range(4):
                at = half * owned + q * rows
                part_in[q, 2 * pair + half] = made[at : at + rows].astype(BF16)

    to_sibling = []
    for kind, part, landing in ((0, part_in, sib_in), (1, part_dn, sib_dn)):
        for yy in range(2):
            away = part.at[2 * yy + (1 - c)]
            to_sibling.append(remote(away, landing.at[yy], ssend.at[kind, yy], srecv.at[kind, yy], sibling))
    to_sibling[0].start()
    to_sibling[1].start()
    every = gg[...].reshape(8 * tokens, width)

    @pl.loop(0, 4)
    def _(q):
        part_dn[q] = mm(ht[pl.ds(pl.multiple_of(q * owned, owned), owned), :], every).astype(BF16)

    to_sibling[2].start()
    to_sibling[3].start()
    over = 2 * (1 - y) + c
    mine = 2 * y + c
    for copy in to_sibling:
        copy.wait()
    ysend_in[...] = (part_in[over].astype(F32) + sib_in[1 - y].astype(F32)).astype(BF16)
    ysend_dn[...] = (part_dn[over].astype(F32) + sib_dn[1 - y].astype(F32)).astype(BF16)
    to_y = (
        remote(ysend_in, yrecv_in, ysend.at[0], yrecv.at[0], ypeer),
        remote(ysend_dn, yrecv_dn, ysend.at[1], yrecv.at[1], ypeer),
    )
    for copy in to_y:
        copy.start()
    to_y[0].wait()
    slab[...] = (part_in[mine].astype(F32) + sib_in[y].astype(F32) + yrecv_in[...].astype(F32)).astype(BF16)
    to_q = []
    for k in range(1, 8):
        target = lax.rem(dp + k, 8)
        to_q.append(remote(slab.at[target], slab_in.at[dp], qsend.at[k], qrecv.at[k], (target, blk)))
        to_q[-1].start()
    slab_in[dp] = slab[dp]
    to_y[1].wait()
    down_ref[...] = part_dn[mine].astype(F32) + sib_dn[y].astype(F32) + yrecv_dn[...].astype(F32)
    for copy in to_q:
        copy.wait()
    for s in range(8):
        in_ref[:, s * cut : (s + 1) * cut] = slab_in[s].astype(F32)
    for k in range(1, 4):
        for copy in gather(0, k, xpeer):
            copy.wait_send()
    for k in range(0, 4):
        for copy in gather(k, 4 + k, xpeer):
            copy.wait_send()


def ffn_grads(normed, grad, w_in, w_down):
    tokens, width = normed.shape
    inner = w_in.shape[1]
    cut, owned, rows = inner // 8, inner // 32, width // 32
    v = pltpu.VMEM
    dma = pltpu.SemaphoreType.DMA
    flops = 2 * 8 * tokens * width * cut * 4
    return pl.pallas_call(
        ffn_grads_kernel,
        out_shape=(jax.ShapeDtypeStruct((owned, width), F32), jax.ShapeDtypeStruct((rows, inner), F32)),
        in_specs=[pl.BlockSpec(memory_space=v)] * 2 + [pl.BlockSpec(memory_space=pl.ANY)] * 2,
        out_specs=(pl.BlockSpec(memory_space=v),) * 2,
        scratch_shapes=[
            v((8, tokens, width), BF16), v((8, tokens, width), BF16),
            v((width, cut), BF16), v((cut, width), BF16),
            v((width, 8 * tokens), BF16), v((8 * tokens, cut), BF16), v((cut, 8 * tokens), BF16),
            v((4, 8, rows, cut), BF16), v((4, owned, width), BF16),
            v((2, 8, rows, cut), BF16), v((2, owned, width), BF16),
            v((8, rows, cut), BF16), v((owned, width), BF16),
            v((8, rows, cut), BF16), v((owned, width), BF16),
            v((8, rows, cut), BF16), v((8, rows, cut), BF16),
            dma((2,)), dma((2, 8)), dma((2, 8)), dma((2, 2)), dma((2, 2)), dma((2,)), dma((2,)), dma((8,)), dma((8,)),
        ],
        compiler_params=pltpu.CompilerParams(collective_id=1, has_side_effects=True, vmem_limit_bytes=60 * 2**20),
        cost_estimate=pl.CostEstimate(flops=flops, bytes_accessed=8 * 2**20, transcendentals=0),
    )(normed, grad, w_in, w_down)


TN = (((0,), (0,)), ((), ()))


def neighbours(dp, y, c):
    return (dp, 2 * y + (1 - c)), (dp, 2 * (1 - y) + c), (dp, 2 * (1 - y) + (1 - c))


def row_gather(kind, mine, rows, y, c, sibling, ypeer, send, recv):
    at = rows.at[y, pl.ds(pl.multiple_of(c * mine, mine), mine), :]
    over = rows.at[1 - y, pl.ds(pl.multiple_of(c * mine, mine), mine), :]
    return (
        remote(at, at, send.at[kind, 0], recv.at[kind, 0], sibling),
        remote(at, at, send.at[kind, 1], recv.at[kind, 1], ypeer),
        remote(over, over, send.at[kind, 2], recv.at[kind, 2], sibling),
    )


def norm_rows(values, gain, shift):
    center = values - jnp.mean(values, axis=-1, keepdims=True)
    spread = jnp.mean(center * center, axis=-1, keepdims=True)
    return center * lax.rsqrt(spread + EPSILON) * gain + shift


def half_of(pair, head):
    lanes = lax.broadcasted_iota(jnp.int32, pair.shape, 1) // 64
    return jnp.where(lanes == head, pair, jnp.zeros_like(pair))


def attend_kernel(
    tok_ref, gain_ref, shift_ref, segq_ref, segk_ref, wqkv_ref, row_ref, qkv_ref, att_ref, own_ref,
    rows, wbuf, low, landing, wsem, gsend, grecv, asend, arecv,
):
    dp, blk, z, x, y, c = place()
    tokens, width = tok_ref.shape
    row_len = 4 * tokens
    first = 5 * y + 3 * c
    pairs = 3 - c

    def load(j, t):
        source = wqkv_ref.at[:, pl.ds(pl.multiple_of(t * width + (first + j) * 128, 128), 128)]
        return pltpu.make_async_copy(source, wbuf.at[j, :, pl.ds(t * 128, 128)], wsem.at[j, t])

    @pl.loop(0, pairs)
    def _(j):
        for t in range(3):
            load(j, t).start()

    rows[y, pl.ds(pl.multiple_of(c * tokens, tokens), tokens), :] = tok_ref[...]
    sibling, ypeer, diag = neighbours(dp, y, c)
    greet([sibling, ypeer, diag])
    moves = row_gather(0, tokens, rows, y, c, sibling, ypeer, gsend, grecv)
    moves[0].start()
    moves[1].start()

    @pl.loop(0, pairs)
    def _(j):
        for t in range(3):
            load(j, t).wait()

    def project(chip):
        at = pl.ds(pl.multiple_of(chip * 2 * tokens, 2 * tokens), 2 * tokens)
        row_ref[at, :] = norm_rows(rows[chip].astype(F32), gain_ref[...], shift_ref[...]).astype(BF16)

        @pl.loop(0, pairs)
        def _(j):
            made = mm(row_ref[at, :], wbuf[j])
            qkv_ref[j, at, 0:128] = (made[:, 0:128] * 0.125).astype(BF16)
            qkv_ref[j, at, 128:384] = made[:, 128:384].astype(BF16)

    @pl.loop(0, 2)
    def _(step):
        @pl.when(step == 0)
        def _():
            moves[0].wait_recv()

        @pl.when(step == 1)
        def _():
            moves[1].wait_recv()
            moves[2].start()
            moves[2].wait_recv()

        project(y + step - 2 * y * step)

    @pl.when(c == 1)
    def _():
        low[2] = jnp.zeros_like(low[2])
        qkv_ref[2] = jnp.zeros_like(qkv_ref[2])
        att_ref[2] = jnp.zeros_like(att_ref[2])

    @pl.loop(0, pairs)
    def _(j):
        @pl.loop(0, 2)
        def _(part):
            at = pl.ds(pl.multiple_of(part * 2 * tokens, 2 * tokens), 2 * tokens)
            same = segq_ref[at, :] == segk_ref[...]
            pair = jnp.zeros((2 * tokens, 128), F32)
            for head in range(2):
                scores = mm(half_of(qkv_ref[j, at, 0:128], head), qkv_ref[j, :, 128:256], NT)
                weigh = jnp.where(same, jnp.exp(scores), 0.0)
                total = jnp.sum(weigh, axis=-1, keepdims=True)
                pair = pair + half_of(mm(weigh.astype(BF16), qkv_ref[j, :, 256:384]) / total, head)
            att_ref[j, at, :] = pair
            low[j, at, :] = pair.astype(BF16)

    def rows_of(b):
        return pl.ds(pl.multiple_of(b * tokens, tokens), tokens)

    out = []
    for r, target in ((1, sibling), (2, ypeer), (3, diag)):
        out.append(remote(low.at[:, rows_of(target[1]), :], landing.at[r], asend.at[r], arecv.at[r], target))
        out[-1].start()
    landing[0] = low[:, rows_of(blk), :]
    for copy in out:
        copy.wait()
    spread_pairs(landing, own_ref, y, c, 1)
    for move in moves:
        move.wait_send()


def spread_pairs(landing, out, y, c, kinds):
    for yy in range(2):
        for cc in range(2):
            slot = 2 * (y + yy - 2 * y * yy) + (c + cc - 2 * c * cc)
            for j in range(3 - cc):
                p = 5 * yy + 3 * cc + j
                for t in range(kinds):
                    at = t * (out.shape[1] // kinds) + 128 * p
                    out[:, at : at + 128] = landing[slot, j, :, 128 * t : 128 * t + 128].astype(out.dtype)


def attend(tokens, gain, shift, segq, segk, w_qkv):
    count, width = tokens.shape
    row_len = 4 * count
    v = pltpu.VMEM
    dma = pltpu.SemaphoreType.DMA
    return pl.pallas_call(
        attend_kernel,
        out_shape=(
            jax.ShapeDtypeStruct((row_len, width), BF16),
            jax.ShapeDtypeStruct((3, row_len, 384), BF16),
            jax.ShapeDtypeStruct((3, row_len, 128), F32),
            jax.ShapeDtypeStruct((count, width), BF16),
        ),
        in_specs=[pl.BlockSpec(memory_space=v)] * 5 + [pl.BlockSpec(memory_space=pl.ANY)],
        out_specs=(pl.BlockSpec(memory_space=v),) * 4,
        scratch_shapes=[
            v((2, 2 * count, width), BF16), v((3, width, 384), BF16),
            v((3, row_len, 128), BF16), v((4, 3, count, 128), BF16),
            dma((3, 3)), dma((1, 3)), dma((1, 3)), dma((4,)), dma((4,)),
        ],
        compiler_params=pltpu.CompilerParams(collective_id=2, has_side_effects=True, vmem_limit_bytes=48 * 2**20),
        cost_estimate=pl.CostEstimate(flops=2 * row_len * width * 1152, bytes_accessed=8 * 2**20, transcendentals=0),
    )(tokens, gain, shift, segq, segk, w_qkv)


def attend_back_kernel(
    proj_ref, mine_ref, row_ref, qkv_ref, att_ref, segq_ref, segk_ref, wout_ref, gqkv_ref, gout_ref, low_ref,
    grow, arow, wo, turned, aturned, gatt, low, keys, values, part, xin, zout, zin, full, fin, landing,
    wsem, gsend, grecv, xsend, xrecv, zsend, zrecv, fsend, frecv, asend, arecv,
):
    dp, blk, z, x, y, c = place()
    tokens, width = proj_ref.shape
    row_len = 4 * tokens
    first = 5 * y + 3 * c
    pairs = 3 - c
    share = width // 8
    cut = share // 4

    @pl.loop(0, pairs)
    def _(j):
        source = wout_ref.at[pl.ds(pl.multiple_of((first + j) * 128, 128), 128), :]
        pltpu.make_async_copy(source, wo.at[j], wsem.at[j]).start()

    own_rows = pl.ds(pl.multiple_of(c * tokens, tokens), tokens)
    grow[y, own_rows, :] = proj_ref[...]
    arow[y, own_rows, :] = mine_ref[...]
    sibling, ypeer, diag = neighbours(dp, y, c)
    xpeer = (2 * z + (1 - x), blk)
    zpeers = [(2 * lax.rem(z + k, 4) + x, blk) for k in range(1, 4)]
    greet([sibling, ypeer, diag, xpeer] + zpeers)
    moves = row_gather(0, tokens, grow, y, c, sibling, ypeer, gsend, grecv)
    amoves = row_gather(1, tokens, arow, y, c, sibling, ypeer, gsend, grecv)
    for copy in (moves[0], moves[1], amoves[0], amoves[1]):
        copy.start()
    for b in range(4):
        turned[:, b * tokens : (b + 1) * tokens] = row_ref[b * tokens : (b + 1) * tokens, :].T
    moves[1].wait_recv()
    moves[2].start()

    @pl.loop(0, pairs)
    def _(j):
        source = wout_ref.at[pl.ds(pl.multiple_of((first + j) * 128, 128), 128), :]
        pltpu.make_async_copy(source, wo.at[j], wsem.at[j]).wait()

    moves[0].wait_recv()
    moves[2].wait_recv()
    every = grow[...].reshape(row_len, width)

    @pl.loop(0, pairs)
    def _(j):
        gatt[j] = mm(grow[...].reshape(row_len, width), wo[j], NT)

    amoves[1].wait_recv()
    amoves[2].start()
    amoves[0].wait_recv()
    amoves[2].wait_recv()
    for b in range(4):
        aturned[:, b * tokens : (b + 1) * tokens] = arow[b // 2, (b % 2) * tokens : (b % 2 + 1) * tokens, :].T

    def to_x(s):
        return remote(part.at[s, 1 - x], xin.at[s], xsend.at[s], xrecv.at[s], xpeer)

    def to_z(s, k):
        target = lax.rem(z + k, 4)
        return remote(zout.at[s, target], zin.at[s, k - 1], zsend.at[s, k - 1], zrecv.at[s, k - 1], zpeers[k - 1])

    def to_blk(s, r, target):
        return remote(full.at[s, target[1]], fin.at[r, s], fsend.at[r, s], frecv.at[r, s], target)

    def to_low(j, r, target):
        there = pl.ds(pl.multiple_of(target[1] * tokens, tokens), tokens)
        return remote(low.at[j, there, :], landing.at[r, j], asend.at[r, j], arecv.at[r, j], target)

    others = ((1, sibling), (2, ypeer), (3, diag))

    def add_x(s):
        to_x(s).wait()
        for k in range(4):
            zout[s, k] = (part[s, x, k].astype(F32) + xin[s, k].astype(F32)).astype(BF16)
        for k in range(1, 4):
            to_z(s, k).start()

    def add_z(s):
        for k in range(1, 4):
            to_z(s, k).wait()
        total = zout[s, z].astype(F32)
        for k in range(3):
            total = total + zin[s, k].astype(F32)
        for b in range(4):
            full[s, b] = total[b * cut : (b + 1) * cut]
        for r, target in others:
            to_blk(s, r, target).start()
        fin[0, s] = full[s, blk]

    def weight_part(s, left, right):
        @pl.loop(0, 4)
        def _(zz):
            at = pl.ds(pl.multiple_of(zz * 2 * share, 2 * share), 2 * share)
            made = mm(left[at, :], right)
            part[s, 0, zz] = made[:share].astype(BF16)
            part[s, 1, zz] = made[share:].astype(BF16)

    @pl.when(c == 0)
    def _():
        weight_part(0, aturned, grow[:, :, pl.ds(pl.multiple_of(first * 128, 128), 384)].reshape(row_len, 384))

    @pl.when(c == 1)
    def _():
        right = grow[:, :, pl.ds(pl.multiple_of(first * 128, 128), 256)].reshape(row_len, 256)
        weight_part(0, aturned, jnp.concatenate([right, jnp.zeros((row_len, 128), BF16)], axis=1))

    to_x(0).start()

    @pl.loop(0, pairs)
    def _(j):
        keys[...] = jnp.zeros_like(keys)
        values[...] = jnp.zeros_like(values)

        @pl.loop(0, 2)
        def _(half):
            at = pl.ds(pl.multiple_of(half * 2 * tokens, 2 * tokens), 2 * tokens)
            same = segq_ref[at, :] == segk_ref[...]
            queries_grad = jnp.zeros((2 * tokens, 128), F32)
            for head in range(2):
                query = half_of(qkv_ref[j, at, 0:128], head)
                key = half_of(qkv_ref[j, :, 128:256], head)
                grad = half_of(gatt[j, at, :], head)
                weigh = jnp.where(same, jnp.exp(mm(query, key, NT)), 0.0)
                total = jnp.sum(weigh, axis=-1, keepdims=True)
                scaled = (grad / total).astype(BF16)
                delta = jnp.sum(grad * att_ref[j, at, :], axis=-1, keepdims=True) / total
                spread = mm(scaled, qkv_ref[j, :, 256:384], NT)
                score = (weigh * (spread - delta)).astype(BF16)
                queries_grad = queries_grad + mm(score, key)
                keys[...] += mm(score, query, TN)
                values[...] += mm(weigh.astype(BF16), scaled, TN)
            low[j, at, 0:128] = (queries_grad * 0.125).astype(BF16)

        low[j, :, 128:256] = keys[...].astype(BF16)
        low[j, :, 256:384] = values[...].astype(BF16)
        for r, target in others:
            to_low(j, r, target).start()
        weight_part(j + 1, turned, low[j])
        to_x(j + 1).start()
        add_x(j)

        @pl.when(j > 0)
        def _():
            add_z(j - 1)

    add_x(pairs)
    add_z(pairs - 1)
    add_z(pairs)

    @pl.loop(0, pairs)
    def _(j):
        landing[0, j] = low[j, pl.ds(pl.multiple_of(blk * tokens, tokens), tokens), :]
        for r, target in others:
            to_low(j, r, target).wait_send()

    @pl.loop(0, pairs + 1)
    def _(s):
        for r, target in others:
            to_blk(s, r, target).wait_send()

    for r, target, count in ((1, sibling, 2 + c), (2, ypeer, 3 - c), (3, diag, 2 + c)):
        @pl.loop(0, count)
        def _(j):
            to_low(j, r, target).wait_recv()

        @pl.loop(0, count + 1)
        def _(s):
            to_blk(s, r, target).wait_recv()

    spread_pairs(landing, low_ref, y, c, 3)
    for yy in range(2):
        for cc in range(2):
            slot = 2 * (y + yy - 2 * y * yy) + (c + cc - 2 * c * cc)
            p = 5 * yy + 3 * cc
            wide = 128 * (3 - cc)
            gout_ref[:, 128 * p : 128 * p + wide] = fin[slot, 0, :, :wide]
            for j in range(3 - cc):
                for t in range(3):
                    at = t * width + 128 * (p + j)
                    gqkv_ref[:, at : at + 128] = fin[slot, j + 1, :, 128 * t : 128 * t + 128]
    for move in moves + amoves:
        move.wait_send()


def attend_back(proj, mine, rows, qkv, att, segq, segk, w_out):
    count, width = proj.shape
    row_len, share = 4 * count, width // 8
    v = pltpu.VMEM
    dma = pltpu.SemaphoreType.DMA
    return pl.pallas_call(
        attend_back_kernel,
        out_shape=(
            jax.ShapeDtypeStruct((share // 4, 3 * width), F32),
            jax.ShapeDtypeStruct((share // 4, width), F32),
            jax.ShapeDtypeStruct((count, 3 * width), BF16),
        ),
        in_specs=[pl.BlockSpec(memory_space=v)] * 7 + [pl.BlockSpec(memory_space=pl.ANY)],
        out_specs=(pl.BlockSpec(memory_space=v),) * 3,
        scratch_shapes=[
            v((2, 2 * count, width), BF16), v((2, 2 * count, width), BF16), v((3, 128, width), BF16),
            v((width, row_len), BF16), v((width, row_len), BF16), v((3, row_len, 128), F32),
            v((3, row_len, 384), BF16), v((row_len, 128), F32), v((row_len, 128), F32),
            v((4, 2, 4, share, 384), BF16), v((4, 4, share, 384), BF16), v((4, 4, share, 384), BF16),
            v((4, 3, share, 384), BF16), v((4, 4, share // 4, 384), F32), v((4, 4, share // 4, 384), F32),
            v((4, 3, count, 384), BF16),
            dma((3,)), dma((2, 3)), dma((2, 3)), dma((4,)), dma((4,)), dma((4, 3)), dma((4, 3)),
            dma((4, 4)), dma((4, 4)), dma((4, 3)), dma((4, 3)),
        ],
        compiler_params=pltpu.CompilerParams(collective_id=3, has_side_effects=True, vmem_limit_bytes=60 * 2**20),
        cost_estimate=pl.CostEstimate(flops=20 * 2**30, bytes_accessed=16 * 2**20, transcendentals=0),
    )(proj, mine, rows, qkv, att, segq, segk, w_out)


def on_device(
    tokens,
    first_gain,
    first_shift,
    w_qkv,
    w_out,
    second_gain,
    second_shift,
    w_in,
    w_down,
    segment_ids,
    cls_positions,
    out_grad,
):
    tokens, out_grad = tokens[0], out_grad[0]
    block_len, width = tokens.shape
    blocks = lax.axis_size("blk")
    row_len = block_len * blocks
    tokens_wide = tokens.astype(F32)
    places = lax.broadcasted_iota(jnp.int32, (row_len, cls_positions.shape[1]), 0)
    row_cells = jnp.sum((places >= cls_positions).astype(jnp.int32), axis=1)
    segq, segk = row_cells[:, None], row_cells[None, :]
    rows, qkv, att, attended_low = attend(
        tokens, first_gain[None], first_shift[None], segq, segk, w_qkv
    )
    residual = tokens_wide + jnp.dot(attended_low, w_out, preferred_element_type=F32)
    normed_two_low = layer_norm(residual, second_gain, second_shift).astype(BF16)
    hidden_pre = jnp.dot(normed_two_low, w_in, preferred_element_type=F32)
    hidden_low = exact_gelu(hidden_pre).astype(BF16)
    layer = residual + jnp.dot(hidden_low, w_down, preferred_element_type=F32)
    offset = lax.axis_index("blk") * block_len
    spots = lax.broadcasted_iota(jnp.int32, (cls_positions.shape[1], block_len), 1) + offset
    chosen = jnp.sum((spots == cls_positions[0][:, None]).astype(F32), axis=0)
    cell_sums = jnp.sum(chosen[:, None] * layer, axis=0)
    cell_squares = jnp.sum(chosen[:, None] * layer * layer, axis=0)
    count = cls_positions.shape[0] * cls_positions.shape[1] * lax.axis_size("dp")
    grad_hidden = mm(out_grad, w_down, NT)
    grad_pre = jax.vjp(exact_gelu, hidden_pre)[1](grad_hidden)[0].astype(BF16)
    grad_down, grad_in = ffn_grads(normed_two_low, out_grad, w_in, w_down)
    grad_normed_two = mm(grad_pre, w_in, NT)
    unused_two, pull_two = jax.vjp(layer_norm, residual, second_gain, second_shift)
    residual_part, second_gain_grad, second_shift_grad = pull_two(grad_normed_two)
    grad_residual = out_grad.astype(F32) + residual_part
    grad_proj = grad_residual.astype(BF16)
    grad_qkv, grad_out, grad_qkv_low = attend_back(
        grad_proj, attended_low, rows, qkv, att, segq, segk, w_out
    )
    grad_normed_one = mm(grad_qkv_low, w_qkv, NT)
    unused_one, pull_one = jax.vjp(layer_norm, tokens_wide, first_gain, first_shift)
    tokens_part, first_gain_grad, first_shift_grad = pull_one(grad_normed_one)
    tokens_grad = (grad_residual + tokens_part).astype(BF16)
    sums = lax.psum(
        jnp.stack([first_gain_grad, first_shift_grad, second_gain_grad, second_shift_grad, cell_sums, cell_squares]),
        ("dp", "blk"),
    )
    share = width // (lax.axis_size("dp") * blocks)
    rank = lax.axis_index("dp") * blocks + lax.axis_index("blk")
    mine = lax.dynamic_slice_in_dim(sums, rank * share, share, axis=1)
    cls_mean = mine[4] / count
    cls_variance = mine[5] / count - cls_mean * cls_mean
    return (
        layer.astype(BF16)[None],
        tokens_grad[None],
        grad_qkv,
        grad_out,
        grad_in,
        grad_down,
        mine[0],
        mine[1],
        mine[2],
        mine[3],
        cls_mean,
        cls_variance,
    )


def solution(mesh):
    placed = (
        P("dp", "blk", None),
        P(),
        P(),
        P(),
        P(),
        P(),
        P(),
        P(),
        P(),
        P("dp", "blk"),
        P("dp", None),
        P("dp", "blk", None),
    )
    small = mesh.shape["dp"] == 8 and mesh.shape["blk"] == 4
    return jax.shard_map(
        on_device if small else on_device_general,
        mesh=mesh,
        in_specs=placed,
        out_specs=(
            P("dp", "blk", None),
            P("dp", "blk", None),
            P(("dp", "blk"), None),
            P(("dp", "blk"), None),
            P(("dp", "blk"), None),
            P(("dp", "blk"), None),
            P(("dp", "blk")),
            P(("dp", "blk")),
            P(("dp", "blk")),
            P(("dp", "blk")),
            P(("dp", "blk")),
            P(("dp", "blk")),
        ),
        check_vma=False,
    )
```

```python
import jax
import jax.numpy as jnp
from jax import lax
from jax.experimental import pallas as pl
from jax.experimental.pallas import tpu as pltpu
from jax.sharding import PartitionSpec as P

H = 20


EPSILON = 1e-05


def shifted(block, axis, distance):
    devices = range(lax.axis_size(axis))
    route = [((i - distance) % len(devices), i) for i in devices]
    return lax.ppermute(block, axis, route)


def layer_norm(values, gain, shift):
    center = values - jnp.mean(values, axis=-1, keepdims=True)
    spread = jnp.mean(center * center, axis=-1, keepdims=True)
    return center * lax.rsqrt(spread + EPSILON) * gain + shift


def exact_gelu(values):
    return jax.nn.gelu(values, approximate=False)


def same_cells(query_cells, key_cells):
    return query_cells[:, :, None] == key_cells[:, None, :]


def forward_block(queries, key_part, value_part, query_cells, key_cells, totals, weights):
    scores = jnp.einsum("sqhd,skhd->shqk", queries, key_part, preferred_element_type=jnp.float32)
    exp_scores = jnp.where(same_cells(query_cells, key_cells)[:, None], jnp.exp(scores), 0.0)
    weights = weights + jnp.sum(exp_scores, axis=-1)
    totals = totals + jnp.einsum(
        "shqk,skhd->sqhd",
        exp_scores.astype(jnp.bfloat16),
        value_part,
        preferred_element_type=jnp.float32,
    )
    return (totals, weights)


def backward_block(queries, scaled, deltas, query_cells, key_part, value_part, key_cells):
    scores = jnp.einsum("sqhd,skhd->shqk", queries, key_part, preferred_element_type=jnp.float32)
    exp_scores = jnp.where(same_cells(query_cells, key_cells)[:, None], jnp.exp(scores), 0.0)
    grad_exp = jnp.einsum("sqhd,skhd->shqk", scaled, value_part, preferred_element_type=jnp.float32)
    grad_scores = (exp_scores * (grad_exp - deltas[..., None])).astype(jnp.bfloat16)
    grad_queries = jnp.einsum(
        "shqk,skhd->sqhd", grad_scores, key_part, preferred_element_type=jnp.float32
    )
    grad_keys = jnp.einsum(
        "shqk,sqhd->skhd", grad_scores, queries, preferred_element_type=jnp.float32
    )
    grad_values = jnp.einsum(
        "shqk,sqhd->skhd",
        exp_scores.astype(jnp.bfloat16),
        scaled,
        preferred_element_type=jnp.float32,
    )
    return (grad_queries, grad_keys, grad_values)


def on_device_general(
    tokens,
    first_gain,
    first_shift,
    w_qkv,
    w_out,
    second_gain,
    second_shift,
    w_in,
    w_down,
    segment_ids,
    cls_positions,
    out_grad,
):
    seqs_here, block_len, width = tokens.shape
    head_count = H
    head_size = width // head_count
    blocks = lax.axis_size("blk")
    head_shape = (seqs_here, block_len, head_count, head_size)
    flat_shape = (seqs_here, block_len, width)
    tokens_wide = tokens.astype(jnp.float32)
    normed_low = layer_norm(tokens_wide, first_gain, first_shift).astype(jnp.bfloat16)
    projected = jnp.dot(normed_low, w_qkv, preferred_element_type=jnp.float32)
    queries = (projected[..., :width] * 0.125).astype(jnp.bfloat16).reshape(head_shape)
    key_part = projected[..., width : 2 * width].astype(jnp.bfloat16).reshape(head_shape)
    value_part = projected[..., 2 * width :].astype(jnp.bfloat16).reshape(head_shape)
    totals = jnp.zeros(head_shape, jnp.float32)
    weights = jnp.zeros((seqs_here, head_count, block_len), jnp.float32)
    totals, weights = forward_block(
        queries, key_part, value_part, segment_ids, segment_ids, totals, weights
    )

    def forward_step(position, loop_state):
        moving, totals_in, weights_in = loop_state
        moving = shifted((moving[0], moving[1], moving[2]), "blk", 1)
        totals_out, weights_out = forward_block(
            queries, moving[0], moving[1], segment_ids, moving[2], totals_in, weights_in
        )
        return (moving, totals_out, weights_out)

    moved_state, totals, weights = lax.fori_loop(
        0, blocks - 1, forward_step, ((key_part, value_part, segment_ids), totals, weights)
    )
    weights_rows = jnp.swapaxes(weights, 1, 2)[..., None]
    attended = totals / weights_rows
    attended_low = attended.reshape(flat_shape).astype(jnp.bfloat16)
    residual = tokens_wide + jnp.dot(attended_low, w_out, preferred_element_type=jnp.float32)
    normed_two_low = layer_norm(residual, second_gain, second_shift).astype(jnp.bfloat16)
    hidden_pre = jnp.dot(normed_two_low, w_in, preferred_element_type=jnp.float32)
    hidden_low = exact_gelu(hidden_pre).astype(jnp.bfloat16)
    layer = residual + jnp.dot(hidden_low, w_down, preferred_element_type=jnp.float32)
    offset = lax.axis_index("blk") * block_len
    places = (
        lax.broadcasted_iota(jnp.int32, (seqs_here, cls_positions.shape[1], block_len), 2) + offset
    )
    chosen = jnp.sum((places == cls_positions[:, :, None]).astype(jnp.float32), axis=1)
    cell_sums = jnp.sum(chosen[..., None] * layer, axis=(0, 1))
    cell_squares = jnp.sum(chosen[..., None] * layer * layer, axis=(0, 1))
    count = cls_positions.shape[0] * cls_positions.shape[1] * lax.axis_size("dp")
    share = width // (lax.axis_size("dp") * blocks)
    moment_sums = lax.psum((cell_sums, cell_squares), ("dp", "blk"))
    rank = lax.axis_index("dp") * blocks + lax.axis_index("blk")
    sum_share = lax.dynamic_slice_in_dim(moment_sums[0], rank * share, share)
    square_share = lax.dynamic_slice_in_dim(moment_sums[1], rank * share, share)
    grad_layer = out_grad.astype(jnp.float32)
    grad_down = jnp.einsum("sbf,sbd->fd", hidden_low, out_grad, preferred_element_type=jnp.float32)
    grad_hidden = jnp.einsum("sbd,fd->sbf", out_grad, w_down, preferred_element_type=jnp.float32)
    grad_pre = jax.vjp(exact_gelu, hidden_pre)[1](grad_hidden)[0].astype(jnp.bfloat16)
    grad_in = jnp.einsum(
        "sbd,sbf->df", normed_two_low, grad_pre, preferred_element_type=jnp.float32
    )
    grad_normed_two = jnp.einsum("sbf,df->sbd", grad_pre, w_in, preferred_element_type=jnp.float32)
    unused_two, pull_two = jax.vjp(layer_norm, residual, second_gain, second_shift)
    residual_part, second_gain_grad, second_shift_grad = pull_two(grad_normed_two)
    grad_residual = grad_layer + residual_part
    grad_proj = grad_residual.astype(jnp.bfloat16)
    grad_out = jnp.einsum(
        "sbd,sbe->de", attended_low, grad_proj, preferred_element_type=jnp.float32
    )
    grad_attended = jnp.einsum(
        "sbe,de->sbd", grad_proj, w_out, preferred_element_type=jnp.float32
    ).reshape(head_shape)
    scaled = (grad_attended / weights_rows).astype(jnp.bfloat16)
    deltas = jnp.swapaxes(jnp.sum(grad_attended * attended, axis=-1), 1, 2) / weights

    def key_step(position, loop_state):
        moving, key_sums, query_sum = loop_state
        grad_queries, grad_keys, grad_values = backward_block(
            queries, scaled, deltas, segment_ids, moving[0], moving[1], moving[2]
        )
        query_next = query_sum + grad_queries
        keys_next = key_sums[0] + grad_keys
        values_next = key_sums[1] + grad_values
        moving = shifted((moving[0], moving[1], moving[2]), "blk", 1)
        key_sums = (
            shifted(keys_next.astype(jnp.bfloat16), "blk", 1).astype(keys_next.dtype),
            shifted(values_next.astype(jnp.bfloat16), "blk", 1).astype(values_next.dtype),
        )
        return (moving, key_sums, query_next)

    zero_heads = jnp.zeros(head_shape, jnp.float32)
    moved_back, key_sums, query_total = lax.fori_loop(
        0,
        blocks,
        key_step,
        ((key_part, value_part, segment_ids), (zero_heads, zero_heads), zero_heads),
    )
    keys_total, values_total = (key_sums[0], key_sums[1])
    grad_qkv_low = jnp.concatenate(
        [
            (query_total * 0.125).reshape(flat_shape),
            keys_total.reshape(flat_shape),
            values_total.reshape(flat_shape),
        ],
        axis=-1,
    ).astype(jnp.bfloat16)
    grad_qkv = jnp.einsum(
        "sbd,sbe->de", normed_low, grad_qkv_low, preferred_element_type=jnp.float32
    )
    grad_normed_one = jnp.einsum(
        "sbe,de->sbd", grad_qkv_low, w_qkv, preferred_element_type=jnp.float32
    )
    unused_one, pull_one = jax.vjp(layer_norm, tokens_wide, first_gain, first_shift)
    tokens_part, first_gain_grad, first_shift_grad = pull_one(grad_normed_one)
    tokens_grad = (grad_residual + tokens_part).astype(jnp.bfloat16)
    summed = (
        lax.psum_scatter(grad_qkv, ("dp", "blk"), scatter_dimension=0, tiled=True),
        lax.psum_scatter(grad_out, ("dp", "blk"), scatter_dimension=0, tiled=True),
        lax.psum_scatter(grad_in, ("dp", "blk"), scatter_dimension=0, tiled=True),
        lax.psum_scatter(grad_down, ("dp", "blk"), scatter_dimension=0, tiled=True),
        lax.psum_scatter(first_gain_grad, ("dp", "blk"), scatter_dimension=0, tiled=True),
        lax.psum_scatter(first_shift_grad, ("dp", "blk"), scatter_dimension=0, tiled=True),
        lax.psum_scatter(second_gain_grad, ("dp", "blk"), scatter_dimension=0, tiled=True),
        lax.psum_scatter(second_shift_grad, ("dp", "blk"), scatter_dimension=0, tiled=True),
    )
    cls_mean = sum_share / count
    cls_variance = square_share / count - cls_mean * cls_mean
    return (
        layer.astype(jnp.bfloat16),
        tokens_grad,
        summed[0],
        summed[1],
        summed[2],
        summed[3],
        summed[4],
        summed[5],
        summed[6],
        summed[7],
        cls_mean,
        cls_variance,
    )


MESH = pl.DeviceIdType.MESH
F32 = jnp.float32
BF16 = jnp.bfloat16
NN = (((1,), (0,)), ((), ()))
NT = (((1,), (1,)), ((), ()))
TN = (((0,), (0,)), ((), ()))


def mm(left, right, dims=NN):
    return lax.dot_general(left, right, dims, preferred_element_type=F32)


def remote(src, dst, send, recv, target):
    return pltpu.make_async_remote_copy(
        src_ref=src, dst_ref=dst, send_sem=send, recv_sem=recv, device_id=target, device_id_type=MESH
    )


def greet(targets):
    barrier = pltpu.get_barrier_semaphore()
    for target in targets:
        pl.semaphore_signal(barrier, inc=1, device_id=target, device_id_type=MESH)
    pl.semaphore_wait(barrier, len(targets))


def place():
    dp, blk = lax.axis_index("dp"), lax.axis_index("blk")
    return dp, blk, dp // 2, lax.rem(dp, 2), blk // 2, lax.rem(blk, 2)


def piece(index, size):
    return pl.ds(pl.multiple_of(index * size, size), size)


def flip(mine, other):
    return mine + other - 2 * mine * other


class RowGather:
    def __init__(self, rows, size, y, c, sibling, ypeer, send, recv):
        near, far = rows.at[y, piece(c, size)], rows.at[1 - y, piece(c, size)]
        self.core = remote(near, near, send.at[0], recv.at[0], sibling)
        self.over = remote(near, near, send.at[1], recv.at[1], ypeer)
        self.last = remote(far, far, send.at[2], recv.at[2], sibling)

    def start(self):
        self.over.start()
        self.core.start()

    def forward(self):
        self.over.wait_recv()
        self.last.start()

    def arrive(self):
        self.core.wait_recv()
        self.last.wait_recv()

    def drain(self):
        for copy in (self.core, self.over, self.last):
            copy.wait_send()


class DpGather:
    def __init__(self, slots, z, x, blk, send, recv):
        self.slots, self.z, self.x, self.send, self.recv = slots, z, x, send, recv
        self.targets = ((2 * (z + 1) + x, blk), (2 * (z - 1) + x, blk), (2 * z + 1 - x, blk))

    def hop(self, kind, zz):
        slot = self.slots.at[self.x, zz]
        return remote(slot, slot, self.send.at[kind, zz], self.recv.at[self.x, zz], self.targets[kind])

    def up(self, zz):
        @pl.when(self.z < 3)
        def _():
            self.hop(0, zz).start()

        self.hop(2, zz).start()

    def down(self, zz):
        @pl.when(self.z > 0)
        def _():
            self.hop(1, zz).start()

    def start(self):
        self.up(self.z)
        self.down(self.z)

    def forward(self, step):
        below, above = self.z - step, self.z + step

        @pl.when(below >= 0)
        def _():
            self.hop(0, below).wait_recv()
            self.up(below)

        @pl.when(above <= 3)
        def _():
            self.hop(1, above).wait_recv()
            self.down(above)
            self.hop(2, above).start()

    def arrive(self):
        for zz in range(4):
            slot = self.slots.at[1 - self.x, zz]
            remote(slot, slot, self.send.at[2, zz], self.recv.at[1 - self.x, zz], self.targets[2]).wait_recv()

    def drain(self):
        for zz in range(4):
            self.hop(2, zz).wait_send()

            @pl.when((self.z < 3) & (zz <= self.z))
            def _():
                self.hop(0, zz).wait_send()

            @pl.when((self.z > 0) & (zz >= self.z))
            def _():
                self.hop(1, zz).wait_send()


def centered(values):
    center = values - jnp.mean(values, axis=-1, keepdims=True)
    spread = jnp.mean(center * center, axis=-1, keepdims=True)
    scale = lax.rsqrt(spread + EPSILON)
    return center * scale, scale


def norm_back(grad, unit, scale):
    return scale * (
        grad - jnp.mean(grad, axis=-1, keepdims=True) - unit * jnp.mean(grad * unit, axis=-1, keepdims=True)
    )


def half_of(pair, head):
    lanes = lax.broadcasted_iota(jnp.int32, pair.shape, 1) // 64
    return jnp.where(lanes == head, pair, jnp.zeros_like(pair))


def cells_at(cls_ref, places):
    found = jnp.zeros(places.shape, jnp.int32)
    for n in range(cls_ref.shape[1]):
        found = found + (places >= cls_ref[0, n]).astype(jnp.int32)
    return found


def same_cell(cls_ref, start, count, row_len):
    mine = lax.broadcasted_iota(jnp.int32, (count, 1), 0) + start
    other = lax.broadcasted_iota(jnp.int32, (1, row_len), 1)
    return cells_at(cls_ref, mine) == cells_at(cls_ref, other)


def gelu_parts(pre):
    cdf = 0.5 * (1.0 + lax.erf(pre * 0.7071067811865476))
    return cdf, cdf + pre * (0.3989422804014327 * jnp.exp(-0.5 * pre * pre))


def attend_kernel(
    cls_ref, tok_ref, grad_ref, gain_ref, shift_ref, wqkv_ref,
    turned_ref, qkv_ref, att_ref, aturned_ref, own_ref, grads_ref,
    rows, normed, wbuf, low, wsem, gsend, grecv, asend, arecv, dsend, drecv,
):
    dp, blk, z, x, y, c = place()
    tokens, width = tok_ref.shape
    row_len = 4 * tokens
    first = 5 * y + 3 * c
    pairs = 3 - c
    both = 2 * tokens

    def load(j, t):
        source = wqkv_ref.at[:, pl.ds(pl.multiple_of(t * width + (first + j) * 128, 128), 128)]
        return pltpu.make_async_copy(source, wbuf.at[j, :, pl.ds(t * 128, 128)], wsem.at[j, t])

    @pl.loop(0, pairs)
    def _(j):
        for t in range(3):
            load(j, t).start()

    rows[y, piece(c, tokens), :] = tok_ref[...]
    grads_ref[x, z] = grad_ref[...]
    sibling, ypeer, diag = (dp, 2 * y + 1 - c), (dp, 2 * (1 - y) + c), (dp, 2 * (1 - y) + 1 - c)
    greet([sibling, ypeer, diag] + [(2 * lax.rem(z + k, 4) + x, blk) for k in (1, 3)] + [(2 * z + 1 - x, blk)])
    row = RowGather(rows, tokens, y, c, sibling, ypeer, gsend, grecv)
    row.start()
    grads = DpGather(grads_ref, z, x, blk, dsend, drecv)
    grads.start()

    @pl.loop(0, pairs)
    def _(j):
        for t in range(3):
            load(j, t).wait()

    @pl.loop(0, 2)
    def _(step):
        @pl.when(step == 0)
        def _():
            row.core.wait_recv()

        @pl.when(step == 1)
        def _():
            row.forward()
            row.last.wait_recv()
            grads.forward(1)

        chip = flip(y, step)
        at = piece(chip, both)
        normed[at, :] = (centered(rows[chip].astype(F32))[0] * gain_ref[...] + shift_ref[...]).astype(BF16)

        @pl.loop(0, pairs)
        def _(j):
            made = mm(normed[at, :], wbuf[j])
            qkv_ref[j, at, 0:128] = (made[:, 0:128] * 0.125).astype(BF16)
            qkv_ref[j, at, 128:384] = made[:, 128:384].astype(BF16)

    @pl.when(c == 1)
    def _():
        qkv_ref[2] = jnp.zeros_like(qkv_ref[2])
        att_ref[2] = jnp.zeros_like(att_ref[2])

    def to_blk(j, r, target):
        return remote(low.at[0, j], low.at[r, j], asend.at[r, j], arecv.at[r, j], target)

    others = ((1, sibling), (2, ypeer), (3, diag))

    @pl.loop(0, pairs)
    def _(j):
        @pl.loop(0, 2)
        def _(part):
            at = piece(part, both)
            same = same_cell(cls_ref, part * both, both, row_len)
            pair = jnp.zeros((both, 128), F32)
            for head in range(2):
                scores = mm(half_of(qkv_ref[j, at, 0:128], head), qkv_ref[j, :, 128:256], NT)
                weigh = jnp.where(same, jnp.exp(scores), 0.0)
                total = jnp.sum(weigh, axis=-1, keepdims=True)
                pair = pair + half_of(mm(weigh.astype(BF16), qkv_ref[j, :, 256:384]) / total, head)
            att_ref[j, at, :] = pair
            low[0, j, at, :] = pair.astype(BF16)

        for r, target in others:
            to_blk(j, r, target).start()

        @pl.when(j == 0)
        def _():
            grads.forward(2)

    for b in range(4):
        at = slice(b * tokens, (b + 1) * tokens)
        turned_ref[:, at] = normed[at, :].T
    grads.forward(3)

    @pl.loop(0, pairs)
    def _(j):
        for r, target in others:
            to_blk(j, r, target).wait_send()

    for r, target, count in ((1, sibling, 2 + c), (2, ypeer, pairs), (3, diag, 2 + c)):

        @pl.loop(0, count)
        def _(j):
            to_blk(j, r, target).wait_recv()

    for p in range(10):
        yy, cc = p // 5, (p % 5) // 3
        j = p % 5 - 3 * cc
        slot = 2 * flip(y, yy) + flip(c, cc)
        aturned_ref[128 * p : 128 * p + 128, :] = low[slot, j].T
        own_ref[:, 128 * p : 128 * p + 128] = low[slot, j, piece(blk, tokens), :]
    row.drain()
    grads.arrive()
    grads.drain()


def attend(cls_positions, tokens, grad, gain, shift, w_qkv):
    count, width = tokens.shape
    row_len = 4 * count
    v = pltpu.VMEM
    dma = pltpu.SemaphoreType.DMA
    return pl.pallas_call(
        attend_kernel,
        out_shape=(
            jax.ShapeDtypeStruct((width, row_len), BF16),
            jax.ShapeDtypeStruct((3, row_len, 384), BF16),
            jax.ShapeDtypeStruct((3, row_len, 128), F32),
            jax.ShapeDtypeStruct((width, row_len), BF16),
            jax.ShapeDtypeStruct((count, width), BF16),
            jax.ShapeDtypeStruct((2, 4, count, width), BF16),
        ),
        in_specs=[pl.BlockSpec(memory_space=pltpu.SMEM)]
        + [pl.BlockSpec(memory_space=v)] * 4
        + [pl.BlockSpec(memory_space=pl.ANY)],
        out_specs=(pl.BlockSpec(memory_space=v),) * 6,
        scratch_shapes=[
            v((2, 2 * count, width), BF16), v((row_len, width), BF16), v((3, width, 384), BF16),
            v((4, 3, row_len, 128), BF16),
            dma((3, 3)), dma((3,)), dma((3,)), dma((4, 3)), dma((4, 3)), dma((3, 4)), dma((2, 4)),
        ],
        compiler_params=pltpu.CompilerParams(collective_id=1, has_side_effects=True, vmem_limit_bytes=48 * 2**20),
        cost_estimate=pl.CostEstimate(flops=2 * row_len * width * 1152, bytes_accessed=8 * 2**20, transcendentals=0),
    )(cls_positions, tokens, grad, gain, shift, w_qkv)


def rest_kernel(
    cls_ref, tok_ref, own_ref, qkv_ref, att_ref, turned_ref, aturned_ref, gg,
    gain1_ref, gain2_ref, shift2_ref, wout_ref, win_ref, wdown_ref, wqkv_ref,
    layer_ref, tgrad_ref, gqkv_ref, gout_ref, in_ref, down_ref, sums_ref,
    st_in, st_dn, wi, wd, wo, gx, gp, ht, part_in, part_dn, sib_in, sib_dn, ysend_in, ysend_dn, yrecv_in, yrecv_dn,
    slab, slab_in, residual, unit, gnorm, grow, gatt, low, keys, values, part, xin, zout, zin, full, fin, landing,
    sums, sbuf, sbox, tbox,
    wsem, ssem, osem, gsend, grecv, dsend, drecv, sibs, sibr, ysend, yrecv, qsend, qrecv,
    xsend, xrecv, zsend, zrecv, fsend, frecv, asend, arecv, usend, urecv, tsend, trecv,
):
    dp, blk, z, x, y, c = place()
    tokens, width = tok_ref.shape
    row_len, both = 4 * tokens, 2 * tokens
    first, pairs = 5 * y + 3 * c, 3 - c
    cut, owned, rows = wi.shape[1], down_ref.shape[0], in_ref.shape[0]
    share = width // 8
    block = st_in.shape[2]
    steps = win_ref.shape[1] // block
    depth = st_in.shape[0]
    sibling, ypeer, diag = (dp, 2 * y + 1 - c), (dp, 2 * (1 - y) + c), (dp, 2 * (1 - y) + 1 - c)
    xpeer = (2 * z + 1 - x, blk)
    zpeers = [(2 * lax.rem(z + k, 4) + x, blk) for k in range(1, 4)]
    others = ((1, sibling), (2, ypeer), (3, diag))

    def stream_in(i):
        slot = lax.rem(i, depth)
        return pltpu.make_async_copy(win_ref.at[:, piece(i, block)], st_in.at[slot], ssem.at[0, slot])

    def stream_dn(i):
        slot = lax.rem(i, depth)
        return pltpu.make_async_copy(wdown_ref.at[piece(i, block), :], st_dn.at[slot], ssem.at[1, slot])

    tails = ((0, block), (1, block), (2, width - 2 * block))

    def load_out(i, size):
        return pltpu.make_async_copy(
            wout_ref.at[pl.ds(i * block, size), :], st_dn.at[i, pl.ds(0, size), :], ssem.at[1, i]
        )

    for i, size in tails:
        load_out(i, size).start()
    for i in range(depth - 1):
        stream_in(i).start()

    def load_rows(j):
        return pltpu.make_async_copy(wout_ref.at[piece(first + j, 128), :], wo.at[j], osem.at[j])

    @pl.loop(0, pairs)
    def _(j):
        load_rows(j).start()

    greet([sibling, ypeer, diag] + [(lax.rem(dp + k, 8), blk) for k in range(1, 8)])

    made = tok_ref[...].astype(F32)
    for i, size in tails:
        load_out(i, size).wait()
        made = made + mm(own_ref[:, i * block : i * block + size], st_dn[i, :size, :])
    for i in range(depth - 1):
        stream_dn(i).start()
    residual[...] = made
    made, scale2 = centered(made)
    unit[...] = made
    gx[x, z] = (made * gain2_ref[...] + shift2_ref[...]).astype(BF16)
    normed = DpGather(gx, z, x, blk, dsend, drecv)
    normed.start()
    gnorm[...] = jnp.zeros_like(gnorm)

    @pl.loop(0, steps)
    def _(i):
        slot = lax.rem(i, depth)

        @pl.when(i + depth - 1 < steps)
        def _():
            stream_in(i + depth - 1).start()
            stream_dn(i + depth - 1).start()

        stream_in(i).wait()
        stream_dn(i).wait()
        pre = mm(gx[x, z], st_in[slot])
        cdf, slope = gelu_parts(pre)
        grad = (mm(gg[x, z], st_dn[slot], NT) * slope).astype(BF16)
        residual[...] += mm((pre * cdf).astype(BF16), st_dn[slot])
        gnorm[...] += mm(grad, st_in[slot], NT)

        @pl.when(i == 4)
        def _():
            normed.forward(1)

        @pl.when(i == 8)
        def _():
            normed.forward(2)

    load_in = pltpu.make_async_copy(win_ref.at[:, piece(dp, cut)], wi, wsem.at[0])
    load_dn = pltpu.make_async_copy(wdown_ref.at[piece(dp, cut), :], wd, wsem.at[1])
    load_in.start()
    load_dn.start()
    layer = residual[...]
    layer_ref[...] = layer.astype(BF16)
    sums[...] = jnp.zeros_like(sums)
    spots = lax.broadcasted_iota(jnp.int32, (tokens, 1), 0) + blk * tokens
    chosen = jnp.zeros((tokens, 1), F32)
    for n in range(cls_ref.shape[1]):
        chosen = chosen + (spots == cls_ref[0, n]).astype(F32)
    sums[4:5, :] = jnp.sum(chosen * layer, axis=0, keepdims=True)
    sums[5:6, :] = jnp.sum(chosen * layer * layer, axis=0, keepdims=True)
    grad = gnorm[...]
    sums[2:3, :] = jnp.sum(grad * unit[...], axis=0, keepdims=True)
    sums[3:4, :] = jnp.sum(grad, axis=0, keepdims=True)
    made = gg[x, z].astype(F32) + norm_back(grad * gain2_ref[...], unit[...], scale2)
    residual[...] = made
    grow[y, piece(c, tokens), :] = made.astype(BF16)
    row = RowGather(grow, tokens, y, c, sibling, ypeer, gsend, grecv)
    row.start()
    load_in.wait()
    load_dn.wait()

    def make(xx):
        @pl.loop(0, 2)
        def _(half):
            at = piece(2 * xx + half, both)
            pre = mm(gx[xx, piece(half, 2)].reshape(both, width), wi[...])
            cdf, slope = gelu_parts(pre)
            ht[:, at] = (pre * cdf).astype(BF16).T
            gp[at, :] = (mm(gg[xx, piece(half, 2)].reshape(both, width), wd[...], NT) * slope).astype(BF16)

    normed.forward(3)
    row.forward()
    make(x)
    row.arrive()

    @pl.loop(0, pairs)
    def _(j):
        load_rows(j).wait()
        gatt[j] = mm(grow[...].reshape(row_len, width), wo[j], NT)

    def to_x(s):
        return remote(part.at[s, 1 - x], xin.at[s], xsend.at[s], xrecv.at[s], xpeer)

    def to_z(s, k):
        target = lax.rem(z + k, 4)
        return remote(zout.at[s, target], zin.at[s, k - 1], zsend.at[s, k - 1], zrecv.at[s, k - 1], zpeers[k - 1])

    def to_blk(s, r, target):
        return remote(full.at[s, target[1]], fin.at[r, s], fsend.at[r, s], frecv.at[r, s], target)

    def to_low(j, r, target):
        return remote(low.at[j, piece(target[1], tokens), :], landing.at[r, j], asend.at[r, j], arecv.at[r, j], target)

    def add_x(s):
        to_x(s).wait()
        for k in range(4):
            zout[s, k] = (part[s, x, k].astype(F32) + xin[s, k].astype(F32)).astype(BF16)
        for k in range(1, 4):
            to_z(s, k).start()

    def add_z(s):
        for k in range(1, 4):
            to_z(s, k).wait()
        total = zout[s, z].astype(F32)
        for k in range(3):
            total = total + zin[s, k].astype(F32)
        for b in range(4):
            full[s, b] = total[b * rows : (b + 1) * rows]
        for r, target in others:
            to_blk(s, r, target).start()
        fin[0, s] = full[s, blk]

    def weight_part(s, left, right):
        @pl.loop(0, 4)
        def _(zz):
            made = mm(left[piece(zz, 2 * share), :], right)
            part[s, 0, zz] = made[:share].astype(BF16)
            part[s, 1, zz] = made[share:].astype(BF16)

    @pl.when(c == 0)
    def _():
        weight_part(0, aturned_ref, grow[:, :, pl.ds(pl.multiple_of(first * 128, 128), 384)].reshape(row_len, 384))

    @pl.when(c == 1)
    def _():
        right = grow[:, :, pl.ds(pl.multiple_of(first * 128, 128), 256)].reshape(row_len, 256)
        weight_part(0, aturned_ref, jnp.concatenate([right, jnp.zeros((row_len, 128), BF16)], axis=1))

    to_x(0).start()

    to_sibling = []
    for kind, source, box in ((0, part_in, sib_in), (1, part_dn, sib_dn)):
        for yy in range(2):
            away = source.at[2 * yy + (1 - c)]
            to_sibling.append(remote(away, box.at[yy], sibs.at[kind, yy], sibr.at[kind, yy], sibling))
    to_y = (
        remote(ysend_in, yrecv_in, ysend.at[0], yrecv.at[0], ypeer),
        remote(ysend_dn, yrecv_dn, ysend.at[1], yrecv.at[1], ypeer),
    )

    @pl.loop(0, pairs)
    def _(j):
        keys[...] = jnp.zeros_like(keys)
        values[...] = jnp.zeros_like(values)

        @pl.loop(0, 2)
        def _(half):
            at = piece(half, both)
            same = same_cell(cls_ref, half * both, both, row_len)
            queries_grad = jnp.zeros((both, 128), F32)
            for head in range(2):
                query = half_of(qkv_ref[j, at, 0:128], head)
                key = half_of(qkv_ref[j, :, 128:256], head)
                grad = half_of(gatt[j, at, :], head)
                weigh = jnp.where(same, jnp.exp(mm(query, key, NT)), 0.0)
                total = jnp.sum(weigh, axis=-1, keepdims=True)
                scaled = (grad / total).astype(BF16)
                delta = jnp.sum(grad * att_ref[j, at, :], axis=-1, keepdims=True) / total
                spread = mm(scaled, qkv_ref[j, :, 256:384], NT)
                score = (weigh * (spread - delta)).astype(BF16)
                queries_grad = queries_grad + mm(score, key)
                keys[...] += mm(score, query, TN)
                values[...] += mm(weigh.astype(BF16), scaled, TN)
            low[j, at, 0:128] = (queries_grad * 0.125).astype(BF16)

        low[j, :, 128:256] = keys[...].astype(BF16)
        low[j, :, 256:384] = values[...].astype(BF16)
        for r, target in others:
            to_low(j, r, target).start()
        weight_part(j + 1, turned_ref, low[j])
        to_x(j + 1).start()

        @pl.when(j == 0)
        def _():
            normed.arrive()
            make(1 - x)

            @pl.loop(0, 2)
            def _(half):
                left = gx[:, :, :, piece(half, width // 2)].reshape(8 * tokens, width // 2)
                made = mm(left, gp[...], TN)
                for n in range(4):
                    for q in range(4):
                        at = n * share + q * rows
                        part_in[q, 4 * half + n] = made[at : at + rows].astype(BF16)

            to_sibling[0].start()
            to_sibling[1].start()
            every = gg[...].reshape(8 * tokens, width)

            @pl.loop(0, 4)
            def _(q):
                part_dn[q] = mm(ht[piece(q, owned), :], every).astype(BF16)

            to_sibling[2].start()
            to_sibling[3].start()

        add_x(j)

        @pl.when(j > 0)
        def _():
            add_z(j - 1)

        @pl.when(j == 1)
        def _():
            for copy in to_sibling:
                copy.wait()
            over = 2 * (1 - y) + c
            ysend_in[...] = (part_in[over].astype(F32) + sib_in[1 - y].astype(F32)).astype(BF16)
            to_y[0].start()
            ysend_dn[...] = (part_dn[over].astype(F32) + sib_dn[1 - y].astype(F32)).astype(BF16)
            to_y[1].start()

    @pl.loop(0, pairs)
    def _(j):
        landing[0, j] = low[j, piece(blk, tokens), :]
        for r, target in others:
            to_low(j, r, target).wait_send()

    for r, target, count in ((1, sibling, 2 + c), (2, ypeer, pairs), (3, diag, 2 + c)):

        @pl.loop(0, count)
        def _(j):
            to_low(j, r, target).wait_recv()

    def stream_qkv(p, t):
        slot = lax.rem(p, depth)
        source = wqkv_ref.at[:, pl.ds(pl.multiple_of(t * width + p * 128, 128), 128)]
        return pltpu.make_async_copy(source, st_in.at[slot, :, pl.ds(t * 128, 128)], wsem.at[2 + 3 * slot + t])

    for p in range(depth - 1):
        for t in range(3):
            stream_qkv(p, t).start()
    gnorm[...] = jnp.zeros_like(gnorm)
    mine = 2 * y + c
    to_q = []
    for k in range(1, 8):
        target = lax.rem(dp + k, 8)
        to_q.append(remote(slab.at[target], slab_in.at[dp], qsend.at[k], qrecv.at[k], (target, blk)))

    @pl.loop(0, 10)
    def _(p):
        @pl.when(p + depth - 1 < 10)
        def _():
            for t in range(3):
                stream_qkv(p + depth - 1, t).start()

        for t in range(3):
            stream_qkv(p, t).wait()
        yy, pp = p // 5, lax.rem(p, 5)
        cc = pp // 3
        slot = 2 * flip(y, yy) + flip(c, cc)
        gnorm[...] += mm(landing[slot, pp - 3 * cc], st_in[lax.rem(p, depth), :, 0:384], NT)

        @pl.when(p == 3)
        def _():
            add_x(pairs)

        @pl.when(p == 6)
        def _():
            to_y[0].wait()
            total = part_in[mine].astype(F32) + sib_in[y].astype(F32) + yrecv_in[...].astype(F32)
            slab[...] = total.astype(BF16)
            for copy in to_q:
                copy.start()
            slab_in[dp] = slab[dp]

    grad = gnorm[...]
    made, scale1 = centered(tok_ref[...].astype(F32))
    sums[0:1, :] = jnp.sum(grad * made, axis=0, keepdims=True)
    sums[1:2, :] = jnp.sum(grad, axis=0, keepdims=True)
    sbuf[...] = jnp.zeros_like(sbuf)
    for k in range(8):
        sbuf[k, :, 0:share] = sums[:, k * share : (k + 1) * share]
    to_u = []
    for k in range(1, 8):
        target = lax.rem(dp + k, 8)
        to_u.append(remote(sbuf.at[target], sbox.at[dp], usend.at[k], urecv.at[k], (target, blk)))
        to_u[-1].start()
    sbox[dp] = sbuf[dp]
    tgrad_ref[...] = (residual[...] + norm_back(grad * gain1_ref[...], made, scale1)).astype(BF16)
    add_z(pairs - 1)
    for copy in to_u:
        copy.wait()
    tbox[0] = jnp.sum(sbox[...], axis=0)
    to_t = [remote(tbox.at[0], tbox.at[r], tsend.at[r], trecv.at[r], target) for r, target in others]
    for copy in to_t:
        copy.start()
    to_y[1].wait()
    down_ref[...] = part_dn[mine].astype(F32) + sib_dn[y].astype(F32) + yrecv_dn[...].astype(F32)
    for copy in to_q:
        copy.wait()
    for s in range(8):
        in_ref[:, s * cut : (s + 1) * cut] = slab_in[s].astype(F32)
    add_z(pairs)
    for copy in to_t:
        copy.wait()
    sums_ref[...] = (tbox[0] + tbox[1]) + (tbox[2] + tbox[3])

    @pl.loop(0, pairs + 1)
    def _(s):
        for r, target in others:
            to_blk(s, r, target).wait_send()

    for r, target, count in ((1, sibling, 2 + c), (2, ypeer, pairs), (3, diag, 2 + c)):

        @pl.loop(0, count + 1)
        def _(s):
            to_blk(s, r, target).wait_recv()

    for yy in range(2):
        for cc in range(2):
            slot = 2 * flip(y, yy) + flip(c, cc)
            p = 5 * yy + 3 * cc
            wide = 128 * (3 - cc)
            gout_ref[:, 128 * p : 128 * p + wide] = fin[slot, 0, :, :wide]
            for j in range(3 - cc):
                for t in range(3):
                    at = t * width + 128 * (p + j)
                    gqkv_ref[:, at : at + 128] = fin[slot, j + 1, :, 128 * t : 128 * t + 128]
    row.drain()
    normed.drain()


def rest(cls_positions, tokens, own, qkv, att, turned, aturned, grads, gain1, gain2, shift2, w_out, w_in, w_down, w_qkv):
    count, width = tokens.shape
    inner = w_in.shape[1]
    row_len, share = 4 * count, width // 8
    cut, owned, rows = inner // 8, inner // 32, width // 32
    block, depth = 512, 3
    v = pltpu.VMEM
    dma = pltpu.SemaphoreType.DMA
    return pl.pallas_call(
        rest_kernel,
        out_shape=(
            jax.ShapeDtypeStruct((count, width), BF16),
            jax.ShapeDtypeStruct((count, width), BF16),
            jax.ShapeDtypeStruct((rows, 3 * width), F32),
            jax.ShapeDtypeStruct((rows, width), F32),
            jax.ShapeDtypeStruct((rows, inner), F32),
            jax.ShapeDtypeStruct((owned, width), F32),
            jax.ShapeDtypeStruct((8, 256), F32),
        ),
        in_specs=[pl.BlockSpec(memory_space=pltpu.SMEM)]
        + [pl.BlockSpec(memory_space=v)] * 10
        + [pl.BlockSpec(memory_space=pl.ANY)] * 4,
        out_specs=(pl.BlockSpec(memory_space=v),) * 7,
        scratch_shapes=[
            v((depth, width, block), BF16), v((depth, block, width), BF16),
            v((width, cut), BF16), v((cut, width), BF16), v((3, 128, width), BF16),
            v((2, 4, count, width), BF16), v((8 * count, cut), BF16), v((cut, 8 * count), BF16),
            v((4, 8, rows, cut), BF16), v((4, owned, width), BF16),
            v((2, 8, rows, cut), BF16), v((2, owned, width), BF16),
            v((8, rows, cut), BF16), v((owned, width), BF16), v((8, rows, cut), BF16), v((owned, width), BF16),
            v((8, rows, cut), BF16), v((8, rows, cut), BF16),
            v((count, width), F32), v((count, width), F32), v((count, width), F32),
            v((2, 2 * count, width), BF16), v((3, row_len, 128), F32), v((3, row_len, 384), BF16),
            v((row_len, 128), F32), v((row_len, 128), F32),
            v((4, 2, 4, share, 384), BF16), v((4, 4, share, 384), BF16), v((4, 4, share, 384), BF16),
            v((4, 3, share, 384), BF16), v((4, 4, share // 4, 384), F32), v((4, 4, share // 4, 384), F32),
            v((4, 3, count, 384), BF16),
            v((8, width), F32), v((8, 8, 256), F32), v((8, 8, 256), F32), v((4, 8, 256), F32),
            dma((2 + 3 * depth,)), dma((2, depth)), dma((3,)), dma((3,)), dma((3,)), dma((3, 4)), dma((2, 4)),
            dma((2, 2)), dma((2, 2)), dma((2,)), dma((2,)), dma((8,)), dma((8,)),
            dma((4,)), dma((4,)), dma((4, 3)), dma((4, 3)), dma((4, 4)), dma((4, 4)), dma((4, 3)), dma((4, 3)),
            dma((8,)), dma((8,)), dma((4,)), dma((4,)),
        ],
        compiler_params=pltpu.CompilerParams(collective_id=2, has_side_effects=True, vmem_limit_bytes=64 * 2**20),
        cost_estimate=pl.CostEstimate(flops=40 * 2**30, bytes_accessed=50 * 2**20, transcendentals=0),
    )(cls_positions, tokens, own, qkv, att, turned, aturned, grads, gain1, gain2, shift2, w_out, w_in, w_down, w_qkv)


def on_device(
    tokens,
    first_gain,
    first_shift,
    w_qkv,
    w_out,
    second_gain,
    second_shift,
    w_in,
    w_down,
    segment_ids,
    cls_positions,
    out_grad,
):
    tokens, out_grad = tokens[0], out_grad[0]
    turned, qkv, att, aturned, own, grads = attend(
        cls_positions, tokens, out_grad, first_gain[None], first_shift[None], w_qkv
    )
    layer, tokens_grad, grad_qkv, grad_out, grad_in, grad_down, sums = rest(
        cls_positions, tokens, own, qkv, att, turned, aturned, grads,
        first_gain[None], second_gain[None], second_shift[None], w_out, w_in, w_down, w_qkv,
    )
    count = cls_positions.shape[0] * cls_positions.shape[1] * lax.axis_size("dp")
    share = tokens.shape[1] // (lax.axis_size("dp") * lax.axis_size("blk"))
    mine = lax.dynamic_slice_in_dim(sums, lax.axis_index("blk") * share, share, axis=1)
    cls_mean = mine[4] / count
    cls_variance = mine[5] / count - cls_mean * cls_mean
    return (
        layer[None],
        tokens_grad[None],
        grad_qkv,
        grad_out,
        grad_in,
        grad_down,
        mine[0],
        mine[1],
        mine[2],
        mine[3],
        cls_mean,
        cls_variance,
    )


def solution(mesh):
    placed = (
        P("dp", "blk", None),
        P(),
        P(),
        P(),
        P(),
        P(),
        P(),
        P(),
        P(),
        P("dp", "blk"),
        P("dp", None),
        P("dp", "blk", None),
    )
    small = mesh.shape["dp"] == 8 and mesh.shape["blk"] == 4
    return jax.shard_map(
        on_device if small else on_device_general,
        mesh=mesh,
        in_specs=placed,
        out_specs=(
            P("dp", "blk", None),
            P("dp", "blk", None),
            P(("dp", "blk"), None),
            P(("dp", "blk"), None),
            P(("dp", "blk"), None),
            P(("dp", "blk"), None),
            P(("dp", "blk")),
            P(("dp", "blk")),
            P(("dp", "blk")),
            P(("dp", "blk")),
            P(("dp", "blk")),
            P(("dp", "blk")),
        ),
        check_vma=False,
    )
```

```python
import functools

import jax
import jax.numpy as jnp
from jax import lax
from jax.experimental import pallas as pl
from jax.experimental.pallas import tpu as pltpu
from jax.sharding import PartitionSpec as P

H = 20


EPSILON = 1e-05


def shifted(block, axis, distance):
    devices = range(lax.axis_size(axis))
    route = [((i - distance) % len(devices), i) for i in devices]
    return lax.ppermute(block, axis, route)


def layer_norm(values, gain, shift):
    center = values - jnp.mean(values, axis=-1, keepdims=True)
    spread = jnp.mean(center * center, axis=-1, keepdims=True)
    return center * lax.rsqrt(spread + EPSILON) * gain + shift


def exact_gelu(values):
    return jax.nn.gelu(values, approximate=False)


def same_cells(query_cells, key_cells):
    return query_cells[:, :, None] == key_cells[:, None, :]


def forward_block(queries, key_part, value_part, query_cells, key_cells, totals, weights):
    scores = jnp.einsum("sqhd,skhd->shqk", queries, key_part, preferred_element_type=jnp.float32)
    exp_scores = jnp.where(same_cells(query_cells, key_cells)[:, None], jnp.exp(scores), 0.0)
    weights = weights + jnp.sum(exp_scores, axis=-1)
    totals = totals + jnp.einsum(
        "shqk,skhd->sqhd",
        exp_scores.astype(jnp.bfloat16),
        value_part,
        preferred_element_type=jnp.float32,
    )
    return (totals, weights)


def backward_block(queries, scaled, deltas, query_cells, key_part, value_part, key_cells):
    scores = jnp.einsum("sqhd,skhd->shqk", queries, key_part, preferred_element_type=jnp.float32)
    exp_scores = jnp.where(same_cells(query_cells, key_cells)[:, None], jnp.exp(scores), 0.0)
    grad_exp = jnp.einsum("sqhd,skhd->shqk", scaled, value_part, preferred_element_type=jnp.float32)
    grad_scores = (exp_scores * (grad_exp - deltas[..., None])).astype(jnp.bfloat16)
    grad_queries = jnp.einsum(
        "shqk,skhd->sqhd", grad_scores, key_part, preferred_element_type=jnp.float32
    )
    grad_keys = jnp.einsum(
        "shqk,sqhd->skhd", grad_scores, queries, preferred_element_type=jnp.float32
    )
    grad_values = jnp.einsum(
        "shqk,sqhd->skhd",
        exp_scores.astype(jnp.bfloat16),
        scaled,
        preferred_element_type=jnp.float32,
    )
    return (grad_queries, grad_keys, grad_values)


def on_device_general(
    tokens,
    first_gain,
    first_shift,
    w_qkv,
    w_out,
    second_gain,
    second_shift,
    w_in,
    w_down,
    segment_ids,
    cls_positions,
    out_grad,
):
    seqs_here, block_len, width = tokens.shape
    head_count = H
    head_size = width // head_count
    blocks = lax.axis_size("blk")
    head_shape = (seqs_here, block_len, head_count, head_size)
    flat_shape = (seqs_here, block_len, width)
    tokens_wide = tokens.astype(jnp.float32)
    normed_low = layer_norm(tokens_wide, first_gain, first_shift).astype(jnp.bfloat16)
    projected = jnp.dot(normed_low, w_qkv, preferred_element_type=jnp.float32)
    queries = (projected[..., :width] * 0.125).astype(jnp.bfloat16).reshape(head_shape)
    key_part = projected[..., width : 2 * width].astype(jnp.bfloat16).reshape(head_shape)
    value_part = projected[..., 2 * width :].astype(jnp.bfloat16).reshape(head_shape)
    totals = jnp.zeros(head_shape, jnp.float32)
    weights = jnp.zeros((seqs_here, head_count, block_len), jnp.float32)
    totals, weights = forward_block(
        queries, key_part, value_part, segment_ids, segment_ids, totals, weights
    )

    def forward_step(position, loop_state):
        moving, totals_in, weights_in = loop_state
        moving = shifted((moving[0], moving[1], moving[2]), "blk", 1)
        totals_out, weights_out = forward_block(
            queries, moving[0], moving[1], segment_ids, moving[2], totals_in, weights_in
        )
        return (moving, totals_out, weights_out)

    moved_state, totals, weights = lax.fori_loop(
        0, blocks - 1, forward_step, ((key_part, value_part, segment_ids), totals, weights)
    )
    weights_rows = jnp.swapaxes(weights, 1, 2)[..., None]
    attended = totals / weights_rows
    attended_low = attended.reshape(flat_shape).astype(jnp.bfloat16)
    residual = tokens_wide + jnp.dot(attended_low, w_out, preferred_element_type=jnp.float32)
    normed_two_low = layer_norm(residual, second_gain, second_shift).astype(jnp.bfloat16)
    hidden_pre = jnp.dot(normed_two_low, w_in, preferred_element_type=jnp.float32)
    hidden_low = exact_gelu(hidden_pre).astype(jnp.bfloat16)
    layer = residual + jnp.dot(hidden_low, w_down, preferred_element_type=jnp.float32)
    offset = lax.axis_index("blk") * block_len
    places = (
        lax.broadcasted_iota(jnp.int32, (seqs_here, cls_positions.shape[1], block_len), 2) + offset
    )
    chosen = jnp.sum((places == cls_positions[:, :, None]).astype(jnp.float32), axis=1)
    cell_sums = jnp.sum(chosen[..., None] * layer, axis=(0, 1))
    cell_squares = jnp.sum(chosen[..., None] * layer * layer, axis=(0, 1))
    count = cls_positions.shape[0] * cls_positions.shape[1] * lax.axis_size("dp")
    share = width // (lax.axis_size("dp") * blocks)
    moment_sums = lax.psum((cell_sums, cell_squares), ("dp", "blk"))
    rank = lax.axis_index("dp") * blocks + lax.axis_index("blk")
    sum_share = lax.dynamic_slice_in_dim(moment_sums[0], rank * share, share)
    square_share = lax.dynamic_slice_in_dim(moment_sums[1], rank * share, share)
    grad_layer = out_grad.astype(jnp.float32)
    grad_down = jnp.einsum("sbf,sbd->fd", hidden_low, out_grad, preferred_element_type=jnp.float32)
    grad_hidden = jnp.einsum("sbd,fd->sbf", out_grad, w_down, preferred_element_type=jnp.float32)
    grad_pre = jax.vjp(exact_gelu, hidden_pre)[1](grad_hidden)[0].astype(jnp.bfloat16)
    grad_in = jnp.einsum(
        "sbd,sbf->df", normed_two_low, grad_pre, preferred_element_type=jnp.float32
    )
    grad_normed_two = jnp.einsum("sbf,df->sbd", grad_pre, w_in, preferred_element_type=jnp.float32)
    unused_two, pull_two = jax.vjp(layer_norm, residual, second_gain, second_shift)
    residual_part, second_gain_grad, second_shift_grad = pull_two(grad_normed_two)
    grad_residual = grad_layer + residual_part
    grad_proj = grad_residual.astype(jnp.bfloat16)
    grad_out = jnp.einsum(
        "sbd,sbe->de", attended_low, grad_proj, preferred_element_type=jnp.float32
    )
    grad_attended = jnp.einsum(
        "sbe,de->sbd", grad_proj, w_out, preferred_element_type=jnp.float32
    ).reshape(head_shape)
    scaled = (grad_attended / weights_rows).astype(jnp.bfloat16)
    deltas = jnp.swapaxes(jnp.sum(grad_attended * attended, axis=-1), 1, 2) / weights

    def key_step(position, loop_state):
        moving, key_sums, query_sum = loop_state
        grad_queries, grad_keys, grad_values = backward_block(
            queries, scaled, deltas, segment_ids, moving[0], moving[1], moving[2]
        )
        query_next = query_sum + grad_queries
        keys_next = key_sums[0] + grad_keys
        values_next = key_sums[1] + grad_values
        moving = shifted((moving[0], moving[1], moving[2]), "blk", 1)
        key_sums = (
            shifted(keys_next.astype(jnp.bfloat16), "blk", 1).astype(keys_next.dtype),
            shifted(values_next.astype(jnp.bfloat16), "blk", 1).astype(values_next.dtype),
        )
        return (moving, key_sums, query_next)

    zero_heads = jnp.zeros(head_shape, jnp.float32)
    moved_back, key_sums, query_total = lax.fori_loop(
        0,
        blocks,
        key_step,
        ((key_part, value_part, segment_ids), (zero_heads, zero_heads), zero_heads),
    )
    keys_total, values_total = (key_sums[0], key_sums[1])
    grad_qkv_low = jnp.concatenate(
        [
            (query_total * 0.125).reshape(flat_shape),
            keys_total.reshape(flat_shape),
            values_total.reshape(flat_shape),
        ],
        axis=-1,
    ).astype(jnp.bfloat16)
    grad_qkv = jnp.einsum(
        "sbd,sbe->de", normed_low, grad_qkv_low, preferred_element_type=jnp.float32
    )
    grad_normed_one = jnp.einsum(
        "sbe,de->sbd", grad_qkv_low, w_qkv, preferred_element_type=jnp.float32
    )
    unused_one, pull_one = jax.vjp(layer_norm, tokens_wide, first_gain, first_shift)
    tokens_part, first_gain_grad, first_shift_grad = pull_one(grad_normed_one)
    tokens_grad = (grad_residual + tokens_part).astype(jnp.bfloat16)
    summed = (
        lax.psum_scatter(grad_qkv, ("dp", "blk"), scatter_dimension=0, tiled=True),
        lax.psum_scatter(grad_out, ("dp", "blk"), scatter_dimension=0, tiled=True),
        lax.psum_scatter(grad_in, ("dp", "blk"), scatter_dimension=0, tiled=True),
        lax.psum_scatter(grad_down, ("dp", "blk"), scatter_dimension=0, tiled=True),
        lax.psum_scatter(first_gain_grad, ("dp", "blk"), scatter_dimension=0, tiled=True),
        lax.psum_scatter(first_shift_grad, ("dp", "blk"), scatter_dimension=0, tiled=True),
        lax.psum_scatter(second_gain_grad, ("dp", "blk"), scatter_dimension=0, tiled=True),
        lax.psum_scatter(second_shift_grad, ("dp", "blk"), scatter_dimension=0, tiled=True),
    )
    cls_mean = sum_share / count
    cls_variance = square_share / count - cls_mean * cls_mean
    return (
        layer.astype(jnp.bfloat16),
        tokens_grad,
        summed[0],
        summed[1],
        summed[2],
        summed[3],
        summed[4],
        summed[5],
        summed[6],
        summed[7],
        cls_mean,
        cls_variance,
    )


MESH = pl.DeviceIdType.MESH
F32 = jnp.float32
BF16 = jnp.bfloat16
NN = (((1,), (0,)), ((), ()))
NT = (((1,), (1,)), ((), ()))
TN = (((0,), (0,)), ((), ()))


def mm(left, right, dims=NN):
    return lax.dot_general(left, right, dims, preferred_element_type=F32)


def remote(src, dst, send, recv, target):
    return pltpu.make_async_remote_copy(
        src_ref=src, dst_ref=dst, send_sem=send, recv_sem=recv, device_id=target, device_id_type=MESH
    )


def greet(targets):
    barrier = pltpu.get_barrier_semaphore()
    for target in targets:
        pl.semaphore_signal(barrier, inc=1, device_id=target, device_id_type=MESH)
    pl.semaphore_wait(barrier, len(targets))


def place():
    dp, blk = lax.axis_index("dp"), lax.axis_index("blk")
    return dp, blk, dp // 2, lax.rem(dp, 2), blk // 2, lax.rem(blk, 2)


def piece(index, size):
    return pl.ds(pl.multiple_of(index * size, size), size)


def flip(mine, other):
    return mine + other - 2 * mine * other


class RowGather:
    def __init__(self, rows, size, y, c, sibling, ypeer, send, recv):
        near, far = rows.at[y, piece(c, size)], rows.at[1 - y, piece(c, size)]
        self.core = remote(near, near, send.at[0], recv.at[0], sibling)
        self.over = remote(near, near, send.at[1], recv.at[1], ypeer)
        self.last = remote(far, far, send.at[2], recv.at[2], sibling)

    def start(self):
        self.over.start()
        self.core.start()

    def forward(self):
        self.over.wait_recv()
        self.last.start()

    def arrive(self):
        self.core.wait_recv()
        self.last.wait_recv()

    def drain(self):
        for copy in (self.core, self.over, self.last):
            copy.wait_send()


class DpGather:
    def __init__(self, slots, z, x, blk, send, recv):
        self.slots, self.z, self.x, self.send, self.recv = slots, z, x, send, recv
        self.targets = ((2 * (z + 1) + x, blk), (2 * (z - 1) + x, blk), (2 * z + 1 - x, blk))

    def hop(self, kind, zz):
        slot = self.slots.at[self.x, zz]
        return remote(slot, slot, self.send.at[kind, zz], self.recv.at[self.x, zz], self.targets[kind])

    def up(self, zz):
        @pl.when(self.z < 3)
        def _():
            self.hop(0, zz).start()

        self.hop(2, zz).start()

    def down(self, zz):
        @pl.when(self.z > 0)
        def _():
            self.hop(1, zz).start()

    def start(self):
        self.up(self.z)
        self.down(self.z)

    def forward(self, step):
        below, above = self.z - step, self.z + step

        @pl.when(below >= 0)
        def _():
            self.hop(0, below).wait_recv()
            self.up(below)

        @pl.when(above <= 3)
        def _():
            self.hop(1, above).wait_recv()
            self.down(above)
            self.hop(2, above).start()

    def arrive(self):
        for zz in range(4):
            slot = self.slots.at[1 - self.x, zz]
            remote(slot, slot, self.send.at[2, zz], self.recv.at[1 - self.x, zz], self.targets[2]).wait_recv()

    def drain(self):
        for zz in range(4):
            self.hop(2, zz).wait_send()

            @pl.when((self.z < 3) & (zz <= self.z))
            def _():
                self.hop(0, zz).wait_send()

            @pl.when((self.z > 0) & (zz >= self.z))
            def _():
                self.hop(1, zz).wait_send()


def centered(values):
    center = values - jnp.mean(values, axis=-1, keepdims=True)
    spread = jnp.mean(center * center, axis=-1, keepdims=True)
    scale = lax.rsqrt(spread + EPSILON)
    return center * scale, scale


def norm_back(grad, unit, scale):
    return scale * (
        grad - jnp.mean(grad, axis=-1, keepdims=True) - unit * jnp.mean(grad * unit, axis=-1, keepdims=True)
    )


def half_of(pair, head):
    lanes = lax.broadcasted_iota(jnp.int32, pair.shape, 1) // 64
    return jnp.where(lanes == head, pair, jnp.zeros_like(pair))


def cells_at(cls_ref, places):
    found = jnp.zeros(places.shape, jnp.int32)
    for n in range(cls_ref.shape[1]):
        found = found + (places >= cls_ref[0, n]).astype(jnp.int32)
    return found


def same_cell(cls_ref, start, count, row_len):
    mine = lax.broadcasted_iota(jnp.int32, (count, 1), 0) + start
    other = lax.broadcasted_iota(jnp.int32, (1, row_len), 1)
    return cells_at(cls_ref, mine) == cells_at(cls_ref, other)


def gelu_parts(pre):
    cdf = 0.5 * (1.0 + lax.erf(pre * 0.7071067811865476))
    return cdf, cdf + pre * (0.3989422804014327 * jnp.exp(-0.5 * pre * pre))


def as_row(ref):
    return ref[...].reshape(1, ref.shape[0])


def layer_kernel(
    cls_ref, tok_hbm, grad_hbm, gain1_ref, shift1_ref, gain2_ref, shift2_ref, wqkv_ref, wout_ref, win_ref, wdown_ref,
    layer_out, tgrad_out, gqkv_out, gout_out, in_out, down_out, sums_ref,
    gg, rows_all, qkv_ref, att_ref, turned_ref, aturned_ref, attlow, abox, arow,
    layer_ref, tgrad_ref, gqkv_ref, gout_ref, in_ref, down_ref,
    st_in, st_dn, wi, wd, wo, gx, gp, ht, part_in, part_dn, sib_in, sib_dn, ysend_in, ysend_dn, yrecv_in, yrecv_dn,
    slab, slab_in, residual, unit, gnorm, grow, gatt, low, keys, values, part, xin, zout, zin, full, fin, landing,
    sums, sbuf, sbox, tbox,
    isem, lsem, rsend, rrecv, ogsend, ogrecv, bsend, brecv, arsend, arrecv, outsem,
    wsem, ssem, osem, gsend, grecv, dsend, drecv, sibs, sibr, ysend, yrecv, qsend, qrecv,
    xsend, xrecv, zsend, zrecv, fsend, frecv, asend, arecv, usend, urecv, tsend, trecv,
):
    dp, blk, z, x, y, c = place()
    tokens, width = tok_hbm.shape
    row_len, both = 4 * tokens, 2 * tokens
    first, pairs = 5 * y + 3 * c, 3 - c
    cut, owned, rows = wi.shape[1], down_ref.shape[0], in_ref.shape[0]
    share = width // 8
    block = st_in.shape[2]
    steps = win_ref.shape[1] // block
    depth = st_in.shape[0]
    sibling, ypeer, diag = (dp, 2 * y + 1 - c), (dp, 2 * (1 - y) + c), (dp, 2 * (1 - y) + 1 - c)
    xpeer = (2 * z + 1 - x, blk)
    zpeers = [(2 * lax.rem(z + k, 4) + x, blk) for k in range(1, 4)]
    others = ((1, sibling), (2, ypeer), (3, diag))
    received = ((1, sibling, 2 + c), (2, ypeer, pairs), (3, diag, 2 + c))

    tok_in = pltpu.make_async_copy(tok_hbm, rows_all.at[y, piece(c, tokens), :], isem.at[0])
    grad_in = pltpu.make_async_copy(grad_hbm, gg.at[x, z], isem.at[1])
    tok_in.start()
    grad_in.start()

    def load(j, t):
        source = wqkv_ref.at[:, pl.ds(pl.multiple_of(t * width + (first + j) * 128, 128), 128)]
        return pltpu.make_async_copy(source, st_in.at[j, :, pl.ds(t * 128, 128)], lsem.at[j, t])

    @pl.loop(0, pairs)
    def _(j):
        for t in range(3):
            load(j, t).start()

    def stream_in(i):
        slot = lax.rem(i, depth)
        return pltpu.make_async_copy(win_ref.at[:, piece(i, block)], st_in.at[slot], ssem.at[0, slot])

    def stream_dn(i):
        slot = lax.rem(i, depth)
        return pltpu.make_async_copy(wdown_ref.at[piece(i, block), :], st_dn.at[slot], ssem.at[1, slot])

    tails = ((0, block), (1, block), (2, width - 2 * block))

    def load_out(i, size):
        return pltpu.make_async_copy(
            wout_ref.at[pl.ds(i * block, size), :], st_dn.at[i, pl.ds(0, size), :], ssem.at[1, i]
        )

    def load_rows(j):
        return pltpu.make_async_copy(wout_ref.at[piece(first + j, 128), :], wo.at[j], osem.at[j])

    greet([sibling, ypeer, diag] + [(lax.rem(dp + k, 8), blk) for k in range(1, 8)])
    row_tok = RowGather(rows_all, tokens, y, c, sibling, ypeer, rsend, rrecv)
    grads = DpGather(gg, z, x, blk, ogsend, ogrecv)
    tok_in.wait()
    row_tok.start()
    grad_in.wait()
    grads.start()
    for i, size in tails:
        load_out(i, size).start()

    @pl.loop(0, pairs)
    def _(j):
        load_rows(j).start()
        for t in range(3):
            load(j, t).wait()

    normed_rows = wd

    @pl.loop(0, 2)
    def _(step):
        @pl.when(step == 0)
        def _():
            row_tok.core.wait_recv()

        @pl.when(step == 1)
        def _():
            row_tok.forward()
            row_tok.last.wait_recv()
            grads.forward(1)

        chip = flip(y, step)
        at = piece(chip, both)
        normed_rows[at, :] = (centered(rows_all[chip].astype(F32))[0] * as_row(gain1_ref) + as_row(shift1_ref)).astype(BF16)

        @pl.loop(0, pairs)
        def _(j):
            made = mm(normed_rows[at, :], st_in[j, :, 0:384])
            qkv_ref[j, at, 0:128] = (made[:, 0:128] * 0.125).astype(BF16)
            qkv_ref[j, at, 128:384] = made[:, 128:384].astype(BF16)

    for i in range(depth - 1):
        stream_in(i).start()

    def to_own(j, r, target):
        return remote(attlow.at[j, piece(target[1], tokens), :], abox.at[r, j], bsend.at[r, j], brecv.at[r, j], target)

    @pl.loop(0, pairs)
    def _(j):
        @pl.loop(0, 2)
        def _(part):
            at = piece(part, both)
            same = same_cell(cls_ref, part * both, both, row_len)
            pair = jnp.zeros((both, 128), F32)
            for head in range(2):
                scores = mm(half_of(qkv_ref[j, at, 0:128], head), qkv_ref[j, :, 128:256], NT)
                weigh = jnp.where(same, jnp.exp(scores), 0.0)
                total = jnp.sum(weigh, axis=-1, keepdims=True)
                pair = pair + half_of(mm(weigh.astype(BF16), qkv_ref[j, :, 256:384]) / total, head)
            att_ref[j, at, :] = pair
            attlow[j, at, :] = pair.astype(BF16)

        for r, target in others:
            to_own(j, r, target).start()
        abox[0, j] = attlow[j, piece(blk, tokens), :]

    grads.forward(2)
    for b in range(4):
        at = slice(b * tokens, (b + 1) * tokens)
        turned_ref[:, at] = normed_rows[at, :].T

    for r, target, count in received:

        @pl.loop(0, count)
        def _(j):
            to_own(j, r, target).wait_recv()

    own_at = (y, piece(c, tokens))
    for p in range(10):
        yy, cc = p // 5, (p % 5) // 3
        slot = 2 * flip(y, yy) + flip(c, cc)
        arow[y, piece(c, tokens), 128 * p : 128 * p + 128] = abox[slot, p % 5 - 3 * cc]
    row_att = RowGather(arow, tokens, y, c, sibling, ypeer, arsend, arrecv)

    made = rows_all[y, piece(c, tokens), :].astype(F32)
    for i, size in tails:
        load_out(i, size).wait()
        made = made + mm(arow[y, piece(c, tokens), i * block : i * block + size], st_dn[i, :size, :])
    for i in range(depth - 1):
        stream_dn(i).start()
    residual[...] = made
    made, scale2 = centered(made)
    unit[...] = made
    gx[x, z] = (made * as_row(gain2_ref) + as_row(shift2_ref)).astype(BF16)
    normed = DpGather(gx, z, x, blk, dsend, drecv)
    normed.start()
    row_att.start()
    gnorm[...] = jnp.zeros_like(gnorm)

    @pl.loop(0, steps)
    def _(i):
        slot = lax.rem(i, depth)

        @pl.when(i + depth - 1 < steps)
        def _():
            stream_in(i + depth - 1).start()
            stream_dn(i + depth - 1).start()

        stream_in(i).wait()
        stream_dn(i).wait()
        pre = mm(gx[x, z], st_in[slot])
        cdf, slope = gelu_parts(pre)
        grad = (mm(gg[x, z], st_dn[slot], NT) * slope).astype(BF16)
        residual[...] += mm((pre * cdf).astype(BF16), st_dn[slot])
        gnorm[...] += mm(grad, st_in[slot], NT)

        @pl.when(i == 1)
        def _():
            grads.forward(3)

        @pl.when(i == 4)
        def _():
            row_att.forward()
            normed.forward(1)

        @pl.when(i == 8)
        def _():
            normed.forward(2)

    load_in = pltpu.make_async_copy(win_ref.at[:, piece(dp, cut)], wi, wsem.at[0])
    load_dn = pltpu.make_async_copy(wdown_ref.at[piece(dp, cut), :], wd, wsem.at[1])
    load_in.start()
    load_dn.start()
    layer = residual[...]
    layer_ref[...] = layer.astype(BF16)
    outs = [pltpu.make_async_copy(layer_ref, layer_out, outsem.at[0])]
    outs[0].start()
    sums[...] = jnp.zeros_like(sums)
    spots = lax.broadcasted_iota(jnp.int32, (tokens, 1), 0) + blk * tokens
    chosen = jnp.zeros((tokens, 1), F32)
    for n in range(cls_ref.shape[1]):
        chosen = chosen + (spots == cls_ref[0, n]).astype(F32)
    sums[4:5, :] = jnp.sum(chosen * layer, axis=0, keepdims=True)
    sums[5:6, :] = jnp.sum(chosen * layer * layer, axis=0, keepdims=True)
    grad = gnorm[...]
    sums[2:3, :] = jnp.sum(grad * unit[...], axis=0, keepdims=True)
    sums[3:4, :] = jnp.sum(grad, axis=0, keepdims=True)
    made = gg[x, z].astype(F32) + norm_back(grad * as_row(gain2_ref), unit[...], scale2)
    residual[...] = made
    grow[y, piece(c, tokens), :] = made.astype(BF16)
    row = RowGather(grow, tokens, y, c, sibling, ypeer, gsend, grecv)
    row.start()
    load_in.wait()
    load_dn.wait()

    def make(xx):
        @pl.loop(0, 2)
        def _(half):
            at = piece(2 * xx + half, both)
            pre = mm(gx[xx, piece(half, 2)].reshape(both, width), wi[...])
            cdf, slope = gelu_parts(pre)
            ht[:, at] = (pre * cdf).astype(BF16).T
            gp[at, :] = (mm(gg[xx, piece(half, 2)].reshape(both, width), wd[...], NT) * slope).astype(BF16)

    normed.forward(3)
    row.forward()
    make(x)
    row_att.arrive()
    for b in range(4):
        aturned_ref[:, b * tokens : (b + 1) * tokens] = arow[b // 2, (b % 2) * tokens : (b % 2 + 1) * tokens, :].T
    row.arrive()

    @pl.loop(0, pairs)
    def _(j):
        load_rows(j).wait()
        gatt[j] = mm(grow[...].reshape(row_len, width), wo[j], NT)

    def to_x(s):
        return remote(part.at[s, 1 - x], xin.at[s], xsend.at[s], xrecv.at[s], xpeer)

    def to_z(s, k):
        target = lax.rem(z + k, 4)
        return remote(zout.at[s, target], zin.at[s, k - 1], zsend.at[s, k - 1], zrecv.at[s, k - 1], zpeers[k - 1])

    def to_blk(s, r, target):
        return remote(full.at[s, target[1]], fin.at[r, s], fsend.at[r, s], frecv.at[r, s], target)

    def to_low(j, r, target):
        return remote(low.at[j, piece(target[1], tokens), :], landing.at[r, j], asend.at[r, j], arecv.at[r, j], target)

    def add_x(s):
        to_x(s).wait()
        for k in range(4):
            zout[s, k] = (part[s, x, k].astype(F32) + xin[s, k].astype(F32)).astype(BF16)
        for k in range(1, 4):
            to_z(s, k).start()

    def add_z(s):
        for k in range(1, 4):
            to_z(s, k).wait()
        total = zout[s, z].astype(F32)
        for k in range(3):
            total = total + zin[s, k].astype(F32)
        for b in range(4):
            full[s, b] = total[b * rows : (b + 1) * rows]
        for r, target in others:
            to_blk(s, r, target).start()
        fin[0, s] = full[s, blk]

    def weight_part(s, left, right):
        @pl.loop(0, 4)
        def _(zz):
            made = mm(left[piece(zz, 2 * share), :], right)
            part[s, 0, zz] = made[:share].astype(BF16)
            part[s, 1, zz] = made[share:].astype(BF16)

    @pl.when(c == 0)
    def _():
        weight_part(0, aturned_ref, grow[:, :, pl.ds(pl.multiple_of(first * 128, 128), 384)].reshape(row_len, 384))

    @pl.when(c == 1)
    def _():
        right = grow[:, :, pl.ds(pl.multiple_of(first * 128, 128), 256)].reshape(row_len, 256)
        weight_part(0, aturned_ref, jnp.concatenate([right, jnp.zeros((row_len, 128), BF16)], axis=1))

    to_x(0).start()

    to_sibling = []
    for kind, source, box in ((0, part_in, sib_in), (1, part_dn, sib_dn)):
        for yy in range(2):
            away = source.at[2 * yy + (1 - c)]
            to_sibling.append(remote(away, box.at[yy], sibs.at[kind, yy], sibr.at[kind, yy], sibling))
    to_y = (
        remote(ysend_in, yrecv_in, ysend.at[0], yrecv.at[0], ypeer),
        remote(ysend_dn, yrecv_dn, ysend.at[1], yrecv.at[1], ypeer),
    )

    @pl.loop(0, pairs)
    def _(j):
        keys[...] = jnp.zeros_like(keys)
        values[...] = jnp.zeros_like(values)

        @pl.loop(0, 2)
        def _(half):
            at = piece(half, both)
            same = same_cell(cls_ref, half * both, both, row_len)
            queries_grad = jnp.zeros((both, 128), F32)
            for head in range(2):
                query = half_of(qkv_ref[j, at, 0:128], head)
                key = half_of(qkv_ref[j, :, 128:256], head)
                grad = half_of(gatt[j, at, :], head)
                weigh = jnp.where(same, jnp.exp(mm(query, key, NT)), 0.0)
                total = jnp.sum(weigh, axis=-1, keepdims=True)
                scaled = (grad / total).astype(BF16)
                delta = jnp.sum(grad * att_ref[j, at, :], axis=-1, keepdims=True) / total
                spread = mm(scaled, qkv_ref[j, :, 256:384], NT)
                score = (weigh * (spread - delta)).astype(BF16)
                queries_grad = queries_grad + mm(score, key)
                keys[...] += mm(score, query, TN)
                values[...] += mm(weigh.astype(BF16), scaled, TN)
            low[j, at, 0:128] = (queries_grad * 0.125).astype(BF16)

        low[j, :, 128:256] = keys[...].astype(BF16)
        low[j, :, 256:384] = values[...].astype(BF16)
        for r, target in others:
            to_low(j, r, target).start()
        weight_part(j + 1, turned_ref, low[j])
        to_x(j + 1).start()

        @pl.when(j == 0)
        def _():
            normed.arrive()
            grads.arrive()
            make(1 - x)

            @pl.loop(0, 2)
            def _(half):
                left = gx[:, :, :, piece(half, width // 2)].reshape(8 * tokens, width // 2)
                made = mm(left, gp[...], TN)
                for n in range(4):
                    for q in range(4):
                        at = n * share + q * rows
                        part_in[q, 4 * half + n] = made[at : at + rows].astype(BF16)

            to_sibling[0].start()
            to_sibling[1].start()
            every = gg[...].reshape(8 * tokens, width)

            @pl.loop(0, 4)
            def _(q):
                part_dn[q] = mm(ht[piece(q, owned), :], every).astype(BF16)

            to_sibling[2].start()
            to_sibling[3].start()

        add_x(j)

        @pl.when(j > 0)
        def _():
            add_z(j - 1)

        @pl.when(j == 1)
        def _():
            for copy in to_sibling:
                copy.wait()
            over = 2 * (1 - y) + c
            ysend_in[...] = (part_in[over].astype(F32) + sib_in[1 - y].astype(F32)).astype(BF16)
            to_y[0].start()
            ysend_dn[...] = (part_dn[over].astype(F32) + sib_dn[1 - y].astype(F32)).astype(BF16)
            to_y[1].start()

    @pl.loop(0, pairs)
    def _(j):
        landing[0, j] = low[j, piece(blk, tokens), :]
        for r, target in others:
            to_low(j, r, target).wait_send()

    for r, target, count in received:

        @pl.loop(0, count)
        def _(j):
            to_low(j, r, target).wait_recv()

    def stream_qkv(p, t):
        slot = lax.rem(p, depth)
        source = wqkv_ref.at[:, pl.ds(pl.multiple_of(t * width + p * 128, 128), 128)]
        return pltpu.make_async_copy(source, st_in.at[slot, :, pl.ds(t * 128, 128)], wsem.at[2 + 3 * slot + t])

    for p in range(depth - 1):
        for t in range(3):
            stream_qkv(p, t).start()
    gnorm[...] = jnp.zeros_like(gnorm)
    mine = 2 * y + c
    to_q = []
    for k in range(1, 8):
        target = lax.rem(dp + k, 8)
        to_q.append(remote(slab.at[target], slab_in.at[dp], qsend.at[k], qrecv.at[k], (target, blk)))

    @pl.loop(0, 10)
    def _(p):
        @pl.when(p + depth - 1 < 10)
        def _():
            for t in range(3):
                stream_qkv(p + depth - 1, t).start()

        for t in range(3):
            stream_qkv(p, t).wait()
        yy, pp = p // 5, lax.rem(p, 5)
        cc = pp // 3
        slot = 2 * flip(y, yy) + flip(c, cc)
        gnorm[...] += mm(landing[slot, pp - 3 * cc], st_in[lax.rem(p, depth), :, 0:384], NT)

        @pl.when(p == 3)
        def _():
            add_x(pairs)

        @pl.when(p == 6)
        def _():
            to_y[0].wait()
            total = part_in[mine].astype(F32) + sib_in[y].astype(F32) + yrecv_in[...].astype(F32)
            slab[...] = total.astype(BF16)
            for copy in to_q:
                copy.start()
            slab_in[dp] = slab[dp]

    grad = gnorm[...]
    made, scale1 = centered(rows_all[y, piece(c, tokens), :].astype(F32))
    sums[0:1, :] = jnp.sum(grad * made, axis=0, keepdims=True)
    sums[1:2, :] = jnp.sum(grad, axis=0, keepdims=True)
    sbuf[...] = jnp.zeros_like(sbuf)
    for k in range(8):
        sbuf[k, :, 0:share] = sums[:, k * share : (k + 1) * share]
    to_u = []
    for k in range(1, 8):
        target = lax.rem(dp + k, 8)
        to_u.append(remote(sbuf.at[target], sbox.at[dp], usend.at[k], urecv.at[k], (target, blk)))
        to_u[-1].start()
    sbox[dp] = sbuf[dp]
    tgrad_ref[...] = (residual[...] + norm_back(grad * as_row(gain1_ref), made, scale1)).astype(BF16)
    outs.append(pltpu.make_async_copy(tgrad_ref, tgrad_out, outsem.at[1]))
    outs[-1].start()
    add_z(pairs - 1)
    for copy in to_u:
        copy.wait()
    tbox[0] = jnp.sum(sbox[...], axis=0)
    to_t = [remote(tbox.at[0], tbox.at[r], tsend.at[r], trecv.at[r], target) for r, target in others]
    for copy in to_t:
        copy.start()
    to_y[1].wait()
    down_ref[...] = part_dn[mine].astype(F32) + sib_dn[y].astype(F32) + yrecv_dn[...].astype(F32)
    outs.append(pltpu.make_async_copy(down_ref, down_out, outsem.at[2]))
    outs[-1].start()
    for copy in to_q:
        copy.wait()
    for s in range(8):
        in_ref[:, s * cut : (s + 1) * cut] = slab_in[s].astype(F32)
    outs.append(pltpu.make_async_copy(in_ref, in_out, outsem.at[3]))
    outs[-1].start()
    add_z(pairs)
    for copy in to_t:
        copy.wait()
    total = (tbox[0] + tbox[1]) + (tbox[2] + tbox[3])
    for b in range(4):
        @pl.when(blk == b)
        def _():
            sums_ref[...] = total[:, b * rows : (b + 1) * rows]

    @pl.loop(0, pairs + 1)
    def _(s):
        for r, target in others:
            to_blk(s, r, target).wait_send()

    for r, target, count in received:

        @pl.loop(0, count + 1)
        def _(s):
            to_blk(s, r, target).wait_recv()

    for yy in range(2):
        for cc in range(2):
            slot = 2 * flip(y, yy) + flip(c, cc)
            p = 5 * yy + 3 * cc
            wide = 128 * (3 - cc)
            gout_ref[:, 128 * p : 128 * p + wide] = fin[slot, 0, :, :wide]
            for j in range(3 - cc):
                for t in range(3):
                    at = t * width + 128 * (p + j)
                    gqkv_ref[:, at : at + 128] = fin[slot, j + 1, :, 128 * t : 128 * t + 128]
    outs.append(pltpu.make_async_copy(gqkv_ref, gqkv_out, outsem.at[4]))
    outs[-1].start()
    outs.append(pltpu.make_async_copy(gout_ref, gout_out, outsem.at[5]))
    outs[-1].start()

    @pl.loop(0, pairs)
    def _(j):
        for r, target in others:
            to_own(j, r, target).wait_send()

    for gather in (row_tok, row_att, row, grads, normed):
        gather.drain()
    for copy in outs:
        copy.wait()


def finish_kernel(cells, sums_ref, *refs):
    count = 6
    arrays, (mean_ref, variance_ref, *grads), outs = refs[:count], refs[count : count + 6], refs[count + 6 : 2 * count + 6]
    held, isem, osem = refs[2 * count + 6 : -2], refs[-2], refs[-1]
    loads = [pltpu.make_async_copy(arrays[i], held[i], isem.at[i]) for i in range(count)]
    stores = [pltpu.make_async_copy(held[i], outs[i], osem.at[i]) for i in range(count)]
    for load in loads:
        load.start()
    for load, store in zip(loads, stores):
        load.wait()
        store.start()
    mean = sums_ref[4:5, :] / cells
    mean_ref[...] = mean
    variance_ref[...] = sums_ref[5:6, :] / cells - mean * mean
    for i in range(4):
        grads[i][...] = sums_ref[i : i + 1, :]
    for store in stores:
        store.wait()


def finish(cells, sums, *arrays):
    anywhere, v = pl.BlockSpec(memory_space=pl.ANY), pl.BlockSpec(memory_space=pltpu.VMEM)
    count = len(arrays)
    small = jax.ShapeDtypeStruct((1, sums.shape[1]), F32)
    return pl.pallas_call(
        functools.partial(finish_kernel, cells),
        out_shape=(small,) * 6 + tuple(jax.ShapeDtypeStruct(a.shape, a.dtype) for a in arrays),
        in_specs=[v] + [anywhere] * count,
        out_specs=(v,) * 6 + (anywhere,) * count,
        scratch_shapes=[pltpu.VMEM(a.shape, a.dtype) for a in arrays]
        + [pltpu.SemaphoreType.DMA((count,)), pltpu.SemaphoreType.DMA((count,))],
    )(sums, *arrays)


def whole_layer(cls_positions, tokens, grad, gain1, shift1, gain2, shift2, w_qkv, w_out, w_in, w_down):
    count, width = tokens.shape
    inner = w_in.shape[1]
    row_len, share = 4 * count, width // 8
    cut, owned, rows = inner // 8, inner // 32, width // 32
    block, depth = 512, 3
    v = pltpu.VMEM
    dma = pltpu.SemaphoreType.DMA
    anywhere = pl.BlockSpec(memory_space=pl.ANY)
    return pl.pallas_call(
        layer_kernel,
        out_shape=(
            jax.ShapeDtypeStruct((count, width), BF16),
            jax.ShapeDtypeStruct((count, width), BF16),
            jax.ShapeDtypeStruct((rows, 3 * width), F32),
            jax.ShapeDtypeStruct((rows, width), F32),
            jax.ShapeDtypeStruct((rows, inner), F32),
            jax.ShapeDtypeStruct((owned, width), F32),
            jax.ShapeDtypeStruct((8, rows), F32),
        ),
        in_specs=[pl.BlockSpec(memory_space=pltpu.SMEM)]
        + [anywhere] * 2
        + [pl.BlockSpec(memory_space=v)] * 4
        + [anywhere] * 4,
        out_specs=(anywhere,) * 6 + (pl.BlockSpec(memory_space=v),),
        scratch_shapes=[
            v((2, 4, count, width), BF16), v((2, 2 * count, width), BF16),
            v((3, row_len, 384), BF16), v((3, row_len, 128), F32), v((width, row_len), BF16), v((width, row_len), BF16),
            v((3, row_len, 128), BF16), v((4, 3, count, 128), BF16), v((2, 2 * count, width), BF16),
            v((count, width), BF16), v((count, width), BF16), v((rows, 3 * width), F32), v((rows, width), F32),
            v((rows, inner), F32), v((owned, width), F32),
            v((depth, width, block), BF16), v((depth, block, width), BF16),
            v((width, cut), BF16), v((cut, width), BF16), v((3, 128, width), BF16),
            v((2, 4, count, width), BF16), v((8 * count, cut), BF16), v((cut, 8 * count), BF16),
            v((4, 8, rows, cut), BF16), v((4, owned, width), BF16),
            v((2, 8, rows, cut), BF16), v((2, owned, width), BF16),
            v((8, rows, cut), BF16), v((owned, width), BF16), v((8, rows, cut), BF16), v((owned, width), BF16),
            v((8, rows, cut), BF16), v((8, rows, cut), BF16),
            v((count, width), F32), v((count, width), F32), v((count, width), F32),
            v((2, 2 * count, width), BF16), v((3, row_len, 128), F32), v((3, row_len, 384), BF16),
            v((row_len, 128), F32), v((row_len, 128), F32),
            v((4, 2, 4, share, 384), BF16), v((4, 4, share, 384), BF16), v((4, 4, share, 384), BF16),
            v((4, 3, share, 384), BF16), v((4, 4, share // 4, 384), F32), v((4, 4, share // 4, 384), F32),
            v((4, 3, count, 384), BF16),
            v((8, width), F32), v((8, 8, 256), F32), v((8, 8, 256), F32), v((4, 8, 256), F32),
            dma((2,)), dma((3, 3)), dma((3,)), dma((3,)), dma((3, 4)), dma((2, 4)), dma((4, 3)), dma((4, 3)),
            dma((3,)), dma((3,)), dma((6,)),
            dma((2 + 3 * depth,)), dma((2, depth)), dma((3,)), dma((3,)), dma((3,)), dma((3, 4)), dma((2, 4)),
            dma((2, 2)), dma((2, 2)), dma((2,)), dma((2,)), dma((8,)), dma((8,)),
            dma((4,)), dma((4,)), dma((4, 3)), dma((4, 3)), dma((4, 4)), dma((4, 4)), dma((4, 3)), dma((4, 3)),
            dma((8,)), dma((8,)), dma((4,)), dma((4,)),
        ],
        compiler_params=pltpu.CompilerParams(collective_id=1, has_side_effects=True, vmem_limit_bytes=64 * 2**20),
        cost_estimate=pl.CostEstimate(flops=40 * 2**30, bytes_accessed=50 * 2**20, transcendentals=0),
    )(cls_positions, tokens, grad, gain1, shift1, gain2, shift2, w_qkv, w_out, w_in, w_down)


def on_device(
    tokens,
    first_gain,
    first_shift,
    w_qkv,
    w_out,
    second_gain,
    second_shift,
    w_in,
    w_down,
    segment_ids,
    cls_positions,
    out_grad,
):
    tokens, out_grad = tokens[0], out_grad[0]
    layer, tokens_grad, grad_qkv, grad_out, grad_in, grad_down, sums = whole_layer(
        cls_positions, tokens, out_grad, first_gain, first_shift, second_gain, second_shift, w_qkv, w_out, w_in, w_down
    )
    mean, variance, gain1_grad, shift1_grad, gain2_grad, shift2_grad, *large = finish(
        cls_positions.size * lax.axis_size("dp"), sums, layer, tokens_grad, grad_qkv, grad_out, grad_in, grad_down
    )
    return (
        large[0][None],
        large[1][None],
        *large[2:],
        gain1_grad[0],
        shift1_grad[0],
        gain2_grad[0],
        shift2_grad[0],
        mean[0],
        variance[0],
    )


def solution(mesh):
    placed = (
        P("dp", "blk", None),
        P(),
        P(),
        P(),
        P(),
        P(),
        P(),
        P(),
        P(),
        P("dp", "blk"),
        P("dp", None),
        P("dp", "blk", None),
    )
    small = mesh.shape["dp"] == 8 and mesh.shape["blk"] == 4
    return jax.shard_map(
        on_device if small else on_device_general,
        mesh=mesh,
        in_specs=placed,
        out_specs=(
            P("dp", "blk", None),
            P("dp", "blk", None),
            P(("dp", "blk"), None),
            P(("dp", "blk"), None),
            P(("dp", "blk"), None),
            P(("dp", "blk"), None),
            P(("dp", "blk")),
            P(("dp", "blk")),
            P(("dp", "blk")),
            P(("dp", "blk")),
            P(("dp", "blk")),
            P(("dp", "blk")),
        ),
        check_vma=False,
    )
```

```python
import functools

import jax
import jax.numpy as jnp
from jax import lax
from jax.experimental import pallas as pl
from jax.experimental.pallas import tpu as pltpu
from jax.sharding import PartitionSpec as P

H = 20


EPSILON = 1e-05


def shifted(block, axis, distance):
    devices = range(lax.axis_size(axis))
    route = [((i - distance) % len(devices), i) for i in devices]
    return lax.ppermute(block, axis, route)


def layer_norm(values, gain, shift):
    center = values - jnp.mean(values, axis=-1, keepdims=True)
    spread = jnp.mean(center * center, axis=-1, keepdims=True)
    return center * lax.rsqrt(spread + EPSILON) * gain + shift


def exact_gelu(values):
    return jax.nn.gelu(values, approximate=False)


def same_cells(query_cells, key_cells):
    return query_cells[:, :, None] == key_cells[:, None, :]


def forward_block(queries, key_part, value_part, query_cells, key_cells, totals, weights):
    scores = jnp.einsum("sqhd,skhd->shqk", queries, key_part, preferred_element_type=jnp.float32)
    exp_scores = jnp.where(same_cells(query_cells, key_cells)[:, None], jnp.exp(scores), 0.0)
    weights = weights + jnp.sum(exp_scores, axis=-1)
    totals = totals + jnp.einsum(
        "shqk,skhd->sqhd",
        exp_scores.astype(jnp.bfloat16),
        value_part,
        preferred_element_type=jnp.float32,
    )
    return (totals, weights)


def backward_block(queries, scaled, deltas, query_cells, key_part, value_part, key_cells):
    scores = jnp.einsum("sqhd,skhd->shqk", queries, key_part, preferred_element_type=jnp.float32)
    exp_scores = jnp.where(same_cells(query_cells, key_cells)[:, None], jnp.exp(scores), 0.0)
    grad_exp = jnp.einsum("sqhd,skhd->shqk", scaled, value_part, preferred_element_type=jnp.float32)
    grad_scores = (exp_scores * (grad_exp - deltas[..., None])).astype(jnp.bfloat16)
    grad_queries = jnp.einsum(
        "shqk,skhd->sqhd", grad_scores, key_part, preferred_element_type=jnp.float32
    )
    grad_keys = jnp.einsum(
        "shqk,sqhd->skhd", grad_scores, queries, preferred_element_type=jnp.float32
    )
    grad_values = jnp.einsum(
        "shqk,sqhd->skhd",
        exp_scores.astype(jnp.bfloat16),
        scaled,
        preferred_element_type=jnp.float32,
    )
    return (grad_queries, grad_keys, grad_values)


def on_device_general(
    tokens,
    first_gain,
    first_shift,
    w_qkv,
    w_out,
    second_gain,
    second_shift,
    w_in,
    w_down,
    segment_ids,
    cls_positions,
    out_grad,
):
    seqs_here, block_len, width = tokens.shape
    head_count = H
    head_size = width // head_count
    blocks = lax.axis_size("blk")
    head_shape = (seqs_here, block_len, head_count, head_size)
    flat_shape = (seqs_here, block_len, width)
    tokens_wide = tokens.astype(jnp.float32)
    normed_low = layer_norm(tokens_wide, first_gain, first_shift).astype(jnp.bfloat16)
    projected = jnp.dot(normed_low, w_qkv, preferred_element_type=jnp.float32)
    queries = (projected[..., :width] * 0.125).astype(jnp.bfloat16).reshape(head_shape)
    key_part = projected[..., width : 2 * width].astype(jnp.bfloat16).reshape(head_shape)
    value_part = projected[..., 2 * width :].astype(jnp.bfloat16).reshape(head_shape)
    totals = jnp.zeros(head_shape, jnp.float32)
    weights = jnp.zeros((seqs_here, head_count, block_len), jnp.float32)
    totals, weights = forward_block(
        queries, key_part, value_part, segment_ids, segment_ids, totals, weights
    )

    def forward_step(position, loop_state):
        moving, totals_in, weights_in = loop_state
        moving = shifted((moving[0], moving[1], moving[2]), "blk", 1)
        totals_out, weights_out = forward_block(
            queries, moving[0], moving[1], segment_ids, moving[2], totals_in, weights_in
        )
        return (moving, totals_out, weights_out)

    moved_state, totals, weights = lax.fori_loop(
        0, blocks - 1, forward_step, ((key_part, value_part, segment_ids), totals, weights)
    )
    weights_rows = jnp.swapaxes(weights, 1, 2)[..., None]
    attended = totals / weights_rows
    attended_low = attended.reshape(flat_shape).astype(jnp.bfloat16)
    residual = tokens_wide + jnp.dot(attended_low, w_out, preferred_element_type=jnp.float32)
    normed_two_low = layer_norm(residual, second_gain, second_shift).astype(jnp.bfloat16)
    hidden_pre = jnp.dot(normed_two_low, w_in, preferred_element_type=jnp.float32)
    hidden_low = exact_gelu(hidden_pre).astype(jnp.bfloat16)
    layer = residual + jnp.dot(hidden_low, w_down, preferred_element_type=jnp.float32)
    offset = lax.axis_index("blk") * block_len
    places = (
        lax.broadcasted_iota(jnp.int32, (seqs_here, cls_positions.shape[1], block_len), 2) + offset
    )
    chosen = jnp.sum((places == cls_positions[:, :, None]).astype(jnp.float32), axis=1)
    cell_sums = jnp.sum(chosen[..., None] * layer, axis=(0, 1))
    cell_squares = jnp.sum(chosen[..., None] * layer * layer, axis=(0, 1))
    count = cls_positions.shape[0] * cls_positions.shape[1] * lax.axis_size("dp")
    share = width // (lax.axis_size("dp") * blocks)
    moment_sums = lax.psum((cell_sums, cell_squares), ("dp", "blk"))
    rank = lax.axis_index("dp") * blocks + lax.axis_index("blk")
    sum_share = lax.dynamic_slice_in_dim(moment_sums[0], rank * share, share)
    square_share = lax.dynamic_slice_in_dim(moment_sums[1], rank * share, share)
    grad_layer = out_grad.astype(jnp.float32)
    grad_down = jnp.einsum("sbf,sbd->fd", hidden_low, out_grad, preferred_element_type=jnp.float32)
    grad_hidden = jnp.einsum("sbd,fd->sbf", out_grad, w_down, preferred_element_type=jnp.float32)
    grad_pre = jax.vjp(exact_gelu, hidden_pre)[1](grad_hidden)[0].astype(jnp.bfloat16)
    grad_in = jnp.einsum(
        "sbd,sbf->df", normed_two_low, grad_pre, preferred_element_type=jnp.float32
    )
    grad_normed_two = jnp.einsum("sbf,df->sbd", grad_pre, w_in, preferred_element_type=jnp.float32)
    unused_two, pull_two = jax.vjp(layer_norm, residual, second_gain, second_shift)
    residual_part, second_gain_grad, second_shift_grad = pull_two(grad_normed_two)
    grad_residual = grad_layer + residual_part
    grad_proj = grad_residual.astype(jnp.bfloat16)
    grad_out = jnp.einsum(
        "sbd,sbe->de", attended_low, grad_proj, preferred_element_type=jnp.float32
    )
    grad_attended = jnp.einsum(
        "sbe,de->sbd", grad_proj, w_out, preferred_element_type=jnp.float32
    ).reshape(head_shape)
    scaled = (grad_attended / weights_rows).astype(jnp.bfloat16)
    deltas = jnp.swapaxes(jnp.sum(grad_attended * attended, axis=-1), 1, 2) / weights

    def key_step(position, loop_state):
        moving, key_sums, query_sum = loop_state
        grad_queries, grad_keys, grad_values = backward_block(
            queries, scaled, deltas, segment_ids, moving[0], moving[1], moving[2]
        )
        query_next = query_sum + grad_queries
        keys_next = key_sums[0] + grad_keys
        values_next = key_sums[1] + grad_values
        moving = shifted((moving[0], moving[1], moving[2]), "blk", 1)
        key_sums = (
            shifted(keys_next.astype(jnp.bfloat16), "blk", 1).astype(keys_next.dtype),
            shifted(values_next.astype(jnp.bfloat16), "blk", 1).astype(values_next.dtype),
        )
        return (moving, key_sums, query_next)

    zero_heads = jnp.zeros(head_shape, jnp.float32)
    moved_back, key_sums, query_total = lax.fori_loop(
        0,
        blocks,
        key_step,
        ((key_part, value_part, segment_ids), (zero_heads, zero_heads), zero_heads),
    )
    keys_total, values_total = (key_sums[0], key_sums[1])
    grad_qkv_low = jnp.concatenate(
        [
            (query_total * 0.125).reshape(flat_shape),
            keys_total.reshape(flat_shape),
            values_total.reshape(flat_shape),
        ],
        axis=-1,
    ).astype(jnp.bfloat16)
    grad_qkv = jnp.einsum(
        "sbd,sbe->de", normed_low, grad_qkv_low, preferred_element_type=jnp.float32
    )
    grad_normed_one = jnp.einsum(
        "sbe,de->sbd", grad_qkv_low, w_qkv, preferred_element_type=jnp.float32
    )
    unused_one, pull_one = jax.vjp(layer_norm, tokens_wide, first_gain, first_shift)
    tokens_part, first_gain_grad, first_shift_grad = pull_one(grad_normed_one)
    tokens_grad = (grad_residual + tokens_part).astype(jnp.bfloat16)
    summed = (
        lax.psum_scatter(grad_qkv, ("dp", "blk"), scatter_dimension=0, tiled=True),
        lax.psum_scatter(grad_out, ("dp", "blk"), scatter_dimension=0, tiled=True),
        lax.psum_scatter(grad_in, ("dp", "blk"), scatter_dimension=0, tiled=True),
        lax.psum_scatter(grad_down, ("dp", "blk"), scatter_dimension=0, tiled=True),
        lax.psum_scatter(first_gain_grad, ("dp", "blk"), scatter_dimension=0, tiled=True),
        lax.psum_scatter(first_shift_grad, ("dp", "blk"), scatter_dimension=0, tiled=True),
        lax.psum_scatter(second_gain_grad, ("dp", "blk"), scatter_dimension=0, tiled=True),
        lax.psum_scatter(second_shift_grad, ("dp", "blk"), scatter_dimension=0, tiled=True),
    )
    cls_mean = sum_share / count
    cls_variance = square_share / count - cls_mean * cls_mean
    return (
        layer.astype(jnp.bfloat16),
        tokens_grad,
        summed[0],
        summed[1],
        summed[2],
        summed[3],
        summed[4],
        summed[5],
        summed[6],
        summed[7],
        cls_mean,
        cls_variance,
    )


MESH = pl.DeviceIdType.MESH
F32 = jnp.float32
BF16 = jnp.bfloat16
NN = (((1,), (0,)), ((), ()))
NT = (((1,), (1,)), ((), ()))
TN = (((0,), (0,)), ((), ()))


def mm(left, right, dims=NN):
    return lax.dot_general(left, right, dims, preferred_element_type=F32)


def remote(src, dst, send, recv, target):
    return pltpu.make_async_remote_copy(
        src_ref=src, dst_ref=dst, send_sem=send, recv_sem=recv, device_id=target, device_id_type=MESH
    )


def greet(targets):
    barrier = pltpu.get_barrier_semaphore()
    for target in targets:
        pl.semaphore_signal(barrier, inc=1, device_id=target, device_id_type=MESH)
    pl.semaphore_wait(barrier, len(targets))


def place():
    dp, blk = lax.axis_index("dp"), lax.axis_index("blk")
    return dp, blk, dp // 2, lax.rem(dp, 2), blk // 2, lax.rem(blk, 2)


def piece(index, size):
    return pl.ds(pl.multiple_of(index * size, size), size)


def flip(mine, other):
    return mine + other - 2 * mine * other


class RowGather:
    def __init__(self, rows, size, y, c, sibling, ypeer, send, recv):
        near, far = rows.at[y, piece(c, size)], rows.at[1 - y, piece(c, size)]
        self.core = remote(near, near, send.at[0], recv.at[0], sibling)
        self.over = remote(near, near, send.at[1], recv.at[1], ypeer)
        self.last = remote(far, far, send.at[2], recv.at[2], sibling)

    def start(self):
        self.over.start()
        self.core.start()

    def forward(self):
        self.over.wait_recv()
        self.last.start()

    def arrive(self):
        self.core.wait_recv()
        self.last.wait_recv()

    def drain(self):
        for copy in (self.core, self.over, self.last):
            copy.wait_send()


class DpGather:
    def __init__(self, slots, z, x, blk, send, recv):
        self.slots, self.z, self.x, self.send, self.recv = slots, z, x, send, recv
        self.targets = ((2 * (z + 1) + x, blk), (2 * (z - 1) + x, blk), (2 * z + 1 - x, blk))

    def hop(self, kind, zz):
        slot = self.slots.at[self.x, zz]
        return remote(slot, slot, self.send.at[kind, zz], self.recv.at[self.x, zz], self.targets[kind])

    def up(self, zz):
        @pl.when(self.z < 3)
        def _():
            self.hop(0, zz).start()

        self.hop(2, zz).start()

    def down(self, zz):
        @pl.when(self.z > 0)
        def _():
            self.hop(1, zz).start()

    def start(self):
        self.up(self.z)
        self.down(self.z)

    def forward(self, step):
        below, above = self.z - step, self.z + step

        @pl.when(below >= 0)
        def _():
            self.hop(0, below).wait_recv()
            self.up(below)

        @pl.when(above <= 3)
        def _():
            self.hop(1, above).wait_recv()
            self.down(above)
            self.hop(2, above).start()

    def arrive(self, half):
        for k in range(2):
            slot = self.slots.at[1 - self.x, 2 * half + k]
            done = self.recv.at[1 - self.x, 2 * half + k]
            remote(slot, slot, self.send.at[2, k], done, self.targets[2]).wait_recv()

    def drain(self):
        for zz in range(4):
            self.hop(2, zz).wait_send()

            @pl.when((self.z < 3) & (zz <= self.z))
            def _():
                self.hop(0, zz).wait_send()

            @pl.when((self.z > 0) & (zz >= self.z))
            def _():
                self.hop(1, zz).wait_send()


def centered(values):
    center = values - jnp.mean(values, axis=-1, keepdims=True)
    spread = jnp.mean(center * center, axis=-1, keepdims=True)
    scale = lax.rsqrt(spread + EPSILON)
    return center * scale, scale


def norm_back(grad, unit, scale):
    return scale * (
        grad - jnp.mean(grad, axis=-1, keepdims=True) - unit * jnp.mean(grad * unit, axis=-1, keepdims=True)
    )


def half_of(pair, head):
    lanes = lax.broadcasted_iota(jnp.int32, pair.shape, 1) // 64
    return jnp.where(lanes == head, pair, jnp.zeros_like(pair))


def cells_at(cls_ref, places):
    found = jnp.zeros(places.shape, jnp.int32)
    for n in range(cls_ref.shape[1]):
        found = found + (places >= cls_ref[0, n]).astype(jnp.int32)
    return found


def same_cell(cls_ref, start, count, row_len):
    mine = lax.broadcasted_iota(jnp.int32, (count, 1), 0) + start
    other = lax.broadcasted_iota(jnp.int32, (1, row_len), 1)
    return cells_at(cls_ref, mine) == cells_at(cls_ref, other)


def gelu_parts(pre):
    cdf = 0.5 * (1.0 + lax.erf(pre * 0.7071067811865476))
    return cdf, cdf + pre * (0.3989422804014327 * jnp.exp(-0.5 * pre * pre))


def as_row(ref):
    return ref[...].reshape(1, ref.shape[0])


def layer_kernel(
    cls_ref, tok_hbm, grad_hbm, gain1_ref, shift1_ref, gain2_ref, shift2_ref, wqkv_ref, wout_ref, win_ref, wdown_ref,
    layer_out, tgrad_out, gqkv_out, gout_out, in_out, down_out, sums_ref,
    gg, rows_all, qkv_ref, att_ref, turned_ref, aturned_ref, attlow, abox, arow,
    layer_ref, tgrad_ref, gqkv_ref, gout_ref, in_ref, down_ref,
    st_in, st_dn, wi, wd, wo, gx, gp, ht, part_in, part_dn, sib_in, sib_dn, ysend_in, ysend_dn, yrecv_in, yrecv_dn,
    slab, slab_in, residual, unit, gnorm, grow, gatt, low, keys, values, part, xin, zout, zin, zlast, zfirst, hfirst, xfirst, full, fin, landing,
    sums, sbuf, sbox, tbox,
    isem, lsem, rsend, rrecv, ogsend, ogrecv, bsend, brecv, arsend, arrecv, outsem,
    wsem, ssem, osem, gsend, grecv, dsend, drecv, sibs, sibr, ysend, yrecv, qsend, qrecv,
    xsend, xrecv, zsend, zrecv, fsend, frecv, asend, arecv, usend, urecv, tsend, trecv,
):
    dp, blk, z, x, y, c = place()
    tokens, width = tok_hbm.shape
    row_len, both = 4 * tokens, 2 * tokens
    first, pairs = 5 * y + 3 * c, 3 - c
    cut, owned, rows = wi.shape[1], down_ref.shape[0], in_ref.shape[0]
    share = width // 8
    block = st_in.shape[2]
    steps = win_ref.shape[1] // block
    depth = st_in.shape[0]
    sibling, ypeer, diag = (dp, 2 * y + 1 - c), (dp, 2 * (1 - y) + c), (dp, 2 * (1 - y) + 1 - c)
    xpeer = (2 * z + 1 - x, blk)
    others = ((1, sibling), (2, ypeer), (3, diag))
    received = ((1, sibling, 2 + c), (2, ypeer, pairs), (3, diag, 2 + c))

    tok_in = pltpu.make_async_copy(tok_hbm, rows_all.at[y, piece(c, tokens), :], isem.at[0])
    grad_in = pltpu.make_async_copy(grad_hbm, gg.at[x, z], isem.at[1])
    tok_in.start()
    grad_in.start()

    def load(j, t):
        source = wqkv_ref.at[:, pl.ds(pl.multiple_of(t * width + (first + j) * 128, 128), 128)]
        return pltpu.make_async_copy(source, st_in.at[j, :, pl.ds(t * 128, 128)], lsem.at[j, t])

    @pl.loop(0, pairs)
    def _(j):
        for t in range(3):
            load(j, t).start()

    def stream_in(i):
        slot = lax.rem(i, depth)
        return pltpu.make_async_copy(win_ref.at[:, piece(i, block)], st_in.at[slot], ssem.at[0, slot])

    def stream_dn(i):
        slot = lax.rem(i, depth)
        return pltpu.make_async_copy(wdown_ref.at[piece(i, block), :], st_dn.at[slot], ssem.at[1, slot])

    tails = ((0, block), (1, block), (2, width - 2 * block))

    def load_out(i, size):
        return pltpu.make_async_copy(
            wout_ref.at[pl.ds(i * block, size), :], st_dn.at[i, pl.ds(0, size), :], ssem.at[1, i]
        )

    def load_rows(j):
        return pltpu.make_async_copy(wout_ref.at[piece(first + j, 128), :], wo.at[j], osem.at[j])

    greet([sibling, ypeer, diag] + [(lax.rem(dp + k, 8), blk) for k in range(1, 8)])
    row_tok = RowGather(rows_all, tokens, y, c, sibling, ypeer, rsend, rrecv)
    grads = DpGather(gg, z, x, blk, ogsend, ogrecv)
    tok_in.wait()
    row_tok.start()
    grad_in.wait()
    grads.start()
    for i, size in tails:
        load_out(i, size).start()

    @pl.loop(0, pairs)
    def _(j):
        load_rows(j).start()
        for t in range(3):
            load(j, t).wait()

    normed_rows = wd

    @pl.loop(0, 2)
    def _(step):
        @pl.when(step == 0)
        def _():
            row_tok.core.wait_recv()

        @pl.when(step == 1)
        def _():
            row_tok.forward()
            row_tok.last.wait_recv()
            grads.forward(1)

        chip = flip(y, step)
        at = piece(chip, both)
        normed_rows[at, :] = (centered(rows_all[chip].astype(F32))[0] * as_row(gain1_ref) + as_row(shift1_ref)).astype(BF16)

        @pl.loop(0, pairs)
        def _(j):
            made = mm(normed_rows[at, :], st_in[j, :, 0:384])
            qkv_ref[j, at, 0:128] = (made[:, 0:128] * 0.125).astype(BF16)
            qkv_ref[j, at, 128:384] = made[:, 128:384].astype(BF16)

    for i in range(depth - 1):
        stream_in(i).start()

    def to_own(j, r, target):
        return remote(attlow.at[j, piece(target[1], tokens), :], abox.at[r, j], bsend.at[r, j], brecv.at[r, j], target)

    @pl.loop(0, pairs)
    def _(j):
        @pl.loop(0, 2)
        def _(part):
            at = piece(part, both)
            same = same_cell(cls_ref, part * both, both, row_len)
            pair = jnp.zeros((both, 128), F32)
            for head in range(2):
                scores = mm(half_of(qkv_ref[j, at, 0:128], head), qkv_ref[j, :, 128:256], NT)
                weigh = jnp.where(same, jnp.exp(scores), 0.0)
                total = jnp.sum(weigh, axis=-1, keepdims=True)
                pair = pair + half_of(mm(weigh.astype(BF16), qkv_ref[j, :, 256:384]) / total, head)
            att_ref[j, at, :] = pair
            attlow[j, at, :] = pair.astype(BF16)

        for r, target in others:
            to_own(j, r, target).start()
        abox[0, j] = attlow[j, piece(blk, tokens), :]

        @pl.when(j == 1)
        def _():
            grads.forward(2)

    for b in range(4):
        at = slice(b * tokens, (b + 1) * tokens)
        turned_ref[:, at] = normed_rows[at, :].T

    for r, target, count in received:

        @pl.loop(0, count)
        def _(j):
            to_own(j, r, target).wait_recv()

    own_at = (y, piece(c, tokens))
    for p in range(10):
        yy, cc = p // 5, (p % 5) // 3
        slot = 2 * flip(y, yy) + flip(c, cc)
        arow[y, piece(c, tokens), 128 * p : 128 * p + 128] = abox[slot, p % 5 - 3 * cc]
    row_att = RowGather(arow, tokens, y, c, sibling, ypeer, arsend, arrecv)

    made = rows_all[y, piece(c, tokens), :].astype(F32)
    for i, size in tails:
        load_out(i, size).wait()
        made = made + mm(arow[y, piece(c, tokens), i * block : i * block + size], st_dn[i, :size, :])
    for i in range(depth - 1):
        stream_dn(i).start()
    residual[...] = made
    made, scale2 = centered(made)
    unit[...] = made
    gx[x, z] = (made * as_row(gain2_ref) + as_row(shift2_ref)).astype(BF16)
    normed = DpGather(gx, z, x, blk, dsend, drecv)
    normed.start()
    row_att.start()
    gnorm[...] = jnp.zeros_like(gnorm)

    @pl.loop(0, steps)
    def _(i):
        slot = lax.rem(i, depth)

        @pl.when(i + depth - 1 < steps)
        def _():
            stream_in(i + depth - 1).start()
            stream_dn(i + depth - 1).start()

        stream_in(i).wait()
        stream_dn(i).wait()
        pre = mm(gx[x, z], st_in[slot])
        cdf, slope = gelu_parts(pre)
        grad = (mm(gg[x, z], st_dn[slot], NT) * slope).astype(BF16)
        residual[...] += mm((pre * cdf).astype(BF16), st_dn[slot])
        gnorm[...] += mm(grad, st_in[slot], NT)

        @pl.when(i == 0)
        def _():
            grads.forward(3)

        @pl.when(i == 4)
        def _():
            row_att.forward()
            normed.forward(1)

        @pl.when(i == 8)
        def _():
            normed.forward(2)

    load_in = pltpu.make_async_copy(win_ref.at[:, piece(dp, cut)], wi, wsem.at[0])
    load_dn = pltpu.make_async_copy(wdown_ref.at[piece(dp, cut), :], wd, wsem.at[1])
    load_in.start()
    load_dn.start()
    layer = residual[...]
    layer_ref[...] = layer.astype(BF16)
    outs = [pltpu.make_async_copy(layer_ref, layer_out, outsem.at[0])]
    outs[0].start()
    sums[...] = jnp.zeros_like(sums)
    spots = lax.broadcasted_iota(jnp.int32, (tokens, 1), 0) + blk * tokens
    chosen = jnp.zeros((tokens, 1), F32)
    for n in range(cls_ref.shape[1]):
        chosen = chosen + (spots == cls_ref[0, n]).astype(F32)
    sums[4:5, :] = jnp.sum(chosen * layer, axis=0, keepdims=True)
    sums[5:6, :] = jnp.sum(chosen * layer * layer, axis=0, keepdims=True)
    grad = gnorm[...]
    sums[2:3, :] = jnp.sum(grad * unit[...], axis=0, keepdims=True)
    sums[3:4, :] = jnp.sum(grad, axis=0, keepdims=True)
    made = gg[x, z].astype(F32) + norm_back(grad * as_row(gain2_ref), unit[...], scale2)
    residual[...] = made
    grow[y, piece(c, tokens), :] = made.astype(BF16)
    row = RowGather(grow, tokens, y, c, sibling, ypeer, gsend, grecv)
    row.start()
    load_in.wait()
    load_dn.wait()

    near = z // 2

    def make(xx, half):
        at = piece(2 * xx + half, both)
        pre = mm(gx[xx, piece(half, 2)].reshape(both, width), wi[...])
        cdf, slope = gelu_parts(pre)
        ht[:, at] = (pre * cdf).astype(BF16).T
        gp[at, :] = (mm(gg[xx, piece(half, 2)].reshape(both, width), wd[...], NT) * slope).astype(BF16)

    def makes(first_step, last_step):
        @pl.loop(first_step, last_step)
        def _(step):
            make(flip(x, lax.rem(step, 2)), flip(near, step // 2))

    makes(0, 1)
    row_att.arrive()
    for b in range(4):
        aturned_ref[:, b * tokens : (b + 1) * tokens] = arow[b // 2, (b % 2) * tokens : (b % 2 + 1) * tokens, :].T
    row.forward()
    normed.forward(3)
    row.arrive()

    @pl.loop(0, pairs)
    def _(j):
        load_rows(j).wait()
        gatt[j] = mm(grow[...].reshape(row_len, width), wo[j], NT)

    even, pair_z, half_z = lax.rem(z, 2), z + 1 - 2 * lax.rem(z, 2), lax.rem(z + 2, 4)

    def to_x(s):
        return remote(part.at[s, 1 - x], xin.at[s - 1], xsend.at[s], xrecv.at[s], xpeer)

    def to_pair(s):
        return remote(zout.at[s - 1, 1 - even], zin.at[s - 1], zsend.at[s, 0], zrecv.at[s, 0], (2 * pair_z + x, blk))

    def to_half(s):
        return remote(zlast.at[s - 1, 0], zlast.at[s - 1, 1], zsend.at[s, 1], zrecv.at[s, 1], (2 * half_z + x, blk))

    other_half, my_half = 1 - z // 2, z // 2
    first_pair = remote(part.at[0, :, 1 - even], zfirst, zsend.at[0, 0], zrecv.at[0, 0], (2 * pair_z + x, blk))
    first_half = remote(hfirst.at[0], hfirst.at[1], zsend.at[0, 1], zrecv.at[0, 1], (2 * half_z + x, blk))
    first_x = remote(xfirst.at[0], xfirst.at[1], xsend.at[0], xrecv.at[0], xpeer)

    def to_blk(s, r, target):
        return remote(full.at[s, target[1]], fin.at[r, s], fsend.at[r, s], frecv.at[r, s], target)

    def to_low(j, r, target):
        return remote(low.at[j, piece(target[1], tokens), :], landing.at[r, j], asend.at[r, j], arecv.at[r, j], target)

    def add_x(s):
        to_x(s).wait()
        for k in range(4):
            zout[s - 1, k // 2, k % 2] = (part[s, x, k // 2, k % 2].astype(F32) + xin[s - 1, k // 2, k % 2].astype(F32)).astype(BF16)
        to_pair(s).start()

    def add_pair(s):
        to_pair(s).wait()
        away = 1 - z // 2
        zlast[s - 1, 0] = (zout[s - 1, even, away].astype(F32) + zin[s - 1, away].astype(F32)).astype(BF16)
        to_half(s).start()

    def add_half(s):
        to_half(s).wait()
        mine = z // 2
        total = zout[s - 1, even, mine].astype(F32) + zin[s - 1, mine].astype(F32) + zlast[s - 1, 1].astype(F32)
        to_owners(s, total)

    def to_owners(s, total):
        for b in range(4):
            full[s, b] = total[b * rows : (b + 1) * rows]
        for r, target in others:
            to_blk(s, r, target).start()
        fin[0, s] = full[s, blk]

    def first_a():
        first_pair.wait()
        for xx in range(2):
            hfirst[0, xx] = (part[0, xx, even, other_half].astype(F32) + zfirst[xx, other_half].astype(F32)).astype(BF16)
        first_half.start()

    def first_sum(xx):
        return part[0, xx, even, my_half].astype(F32) + zfirst[xx, my_half].astype(F32) + hfirst[1, xx].astype(F32)

    def first_b():
        first_half.wait()
        xfirst[0] = first_sum(1 - x).astype(BF16)
        first_x.start()

    def first_c():
        first_x.wait()
        to_owners(0, first_sum(x) + xfirst[1].astype(F32))

    def weight_part(s, left, right):
        @pl.loop(0, 4)
        def _(zz):
            made = mm(left[piece(zz, 2 * share), :], right)
            part[s, 0, lax.rem(zz, 2), zz // 2] = made[:share].astype(BF16)
            part[s, 1, lax.rem(zz, 2), zz // 2] = made[share:].astype(BF16)

    @pl.when(c == 0)
    def _():
        weight_part(0, aturned_ref, grow[:, :, pl.ds(pl.multiple_of(first * 128, 128), 384)].reshape(row_len, 384))

    @pl.when(c == 1)
    def _():
        right = grow[:, :, pl.ds(pl.multiple_of(first * 128, 128), 256)].reshape(row_len, 256)
        weight_part(0, aturned_ref, jnp.concatenate([right, jnp.zeros((row_len, 128), BF16)], axis=1))

    first_pair.start()
    to_sibling = []
    for kind, source, box in ((0, part_in, sib_in), (1, part_dn, sib_dn)):
        for yy in range(2):
            away = source.at[2 * yy + (1 - c)]
            to_sibling.append(remote(away, box.at[yy], sibs.at[kind, yy], sibr.at[kind, yy], sibling))
    to_y = (
        remote(ysend_in, yrecv_in, ysend.at[0], yrecv.at[0], ypeer),
        remote(ysend_dn, yrecv_dn, ysend.at[1], yrecv.at[1], ypeer),
    )

    over = 2 * (1 - y) + c

    @pl.loop(0, pairs)
    def _(j):
        keys[...] = jnp.zeros_like(keys)
        values[...] = jnp.zeros_like(values)

        @pl.loop(0, 2)
        def _(half):
            at = piece(half, both)
            same = same_cell(cls_ref, half * both, both, row_len)
            queries_grad = jnp.zeros((both, 128), F32)
            for head in range(2):
                query = half_of(qkv_ref[j, at, 0:128], head)
                key = half_of(qkv_ref[j, :, 128:256], head)
                grad = half_of(gatt[j, at, :], head)
                weigh = jnp.where(same, jnp.exp(mm(query, key, NT)), 0.0)
                total = jnp.sum(weigh, axis=-1, keepdims=True)
                scaled = (grad / total).astype(BF16)
                delta = jnp.sum(grad * att_ref[j, at, :], axis=-1, keepdims=True) / total
                spread = mm(scaled, qkv_ref[j, :, 256:384], NT)
                score = (weigh * (spread - delta)).astype(BF16)
                queries_grad = queries_grad + mm(score, key)
                keys[...] += mm(score, query, TN)
                values[...] += mm(weigh.astype(BF16), scaled, TN)
            low[j, at, 0:128] = (queries_grad * 0.125).astype(BF16)

        low[j, :, 128:256] = keys[...].astype(BF16)
        low[j, :, 256:384] = values[...].astype(BF16)
        for r, target in others:
            to_low(j, r, target).start()
        weight_part(j + 1, turned_ref, low[j])
        to_x(j + 1).start()

        @pl.when(j == 2)
        def _():
            add_pair(1)
            first_c()

        @pl.when(j == 1)
        def _():
            for half in range(2):
                normed.arrive(half)
                grads.arrive(half)
            makes(1, 4)
            first_a()

            @pl.loop(0, 2)
            def _(half):
                left = gx[:, :, :, piece(half, width // 2)].reshape(8 * tokens, width // 2)
                made = mm(left, gp[...], TN)
                for n in range(4):
                    for q in range(4):
                        at = n * share + q * rows
                        part_in[q, 4 * half + n] = made[at : at + rows].astype(BF16)

            to_sibling[0].start()
            to_sibling[1].start()
            every = gg[...].reshape(8 * tokens, width)

            @pl.loop(0, 4)
            def _(q):
                part_dn[q] = mm(ht[piece(q, owned), :], every).astype(BF16)

            to_sibling[2].start()
            to_sibling[3].start()
            to_sibling[0].wait()
            to_sibling[1].wait()
            ysend_in[...] = (part_in[over].astype(F32) + sib_in[1 - y].astype(F32)).astype(BF16)
            to_y[0].start()
            to_sibling[2].wait()
            to_sibling[3].wait()
            ysend_dn[...] = (part_dn[over].astype(F32) + sib_dn[1 - y].astype(F32)).astype(BF16)
            first_b()
            add_x(1)

    @pl.when(c == 1)
    def _():
        add_pair(1)
        first_c()

    mine = 2 * y + c
    to_q = []
    for k in range(1, 8):
        target = lax.rem(dp + k, 8)
        to_q.append(remote(slab.at[target], slab_in.at[dp], qsend.at[k], qrecv.at[k], (target, blk)))

    def start_q():
        to_y[0].wait()
        to_y[1].start()
        total = part_in[mine].astype(F32) + sib_in[y].astype(F32) + yrecv_in[...].astype(F32)
        slab[...] = total.astype(BF16)
        for copy in to_q:
            copy.start()
        slab_in[dp] = slab[dp]

    start_q()

    @pl.loop(0, pairs)
    def _(j):
        landing[0, j] = low[j, piece(blk, tokens), :]
        for r, target in others:
            to_low(j, r, target).wait_send()

    for r, target, count in received:

        @pl.loop(0, count)
        def _(j):
            to_low(j, r, target).wait_recv()

    def stream_qkv(p, t):
        slot = lax.rem(p, depth)
        source = wqkv_ref.at[:, pl.ds(pl.multiple_of(t * width + p * 128, 128), 128)]
        return pltpu.make_async_copy(source, st_in.at[slot, :, pl.ds(t * 128, 128)], wsem.at[2 + 3 * slot + t])

    for p in range(depth - 1):
        for t in range(3):
            stream_qkv(p, t).start()
    gnorm[...] = jnp.zeros_like(gnorm)
    add_x(2)

    @pl.loop(0, 10)
    def _(p):
        @pl.when(p + depth - 1 < 10)
        def _():
            for t in range(3):
                stream_qkv(p + depth - 1, t).start()

        for t in range(3):
            stream_qkv(p, t).wait()
        yy, pp = p // 5, lax.rem(p, 5)
        cc = pp // 3
        slot = 2 * flip(y, yy) + flip(c, cc)
        gnorm[...] += mm(landing[slot, pp - 3 * cc], st_in[lax.rem(p, depth), :, 0:384], NT)

    grad = gnorm[...]
    made, scale1 = centered(rows_all[y, piece(c, tokens), :].astype(F32))
    sums[0:1, :] = jnp.sum(grad * made, axis=0, keepdims=True)
    sums[1:2, :] = jnp.sum(grad, axis=0, keepdims=True)
    sbuf[...] = jnp.zeros_like(sbuf)
    for k in range(8):
        sbuf[k, :, 0:share] = sums[:, k * share : (k + 1) * share]
    to_u = []
    for k in range(1, 8):
        target = lax.rem(dp + k, 8)
        to_u.append(remote(sbuf.at[target], sbox.at[dp], usend.at[k], urecv.at[k], (target, blk)))
        to_u[-1].start()
    sbox[dp] = sbuf[dp]
    tgrad_ref[...] = (residual[...] + norm_back(grad * as_row(gain1_ref), made, scale1)).astype(BF16)
    outs.append(pltpu.make_async_copy(tgrad_ref, tgrad_out, outsem.at[1]))
    outs[-1].start()

    def end_down():
        to_y[1].wait()
        down_ref[...] = part_dn[mine].astype(F32) + sib_dn[y].astype(F32) + yrecv_dn[...].astype(F32)
        outs.append(pltpu.make_async_copy(down_ref, down_out, outsem.at[2]))
        outs[-1].start()

    def end_q():
        for copy in to_q:
            copy.wait()
        for s in range(8):
            in_ref[:, s * cut : (s + 1) * cut] = slab_in[s].astype(F32)
        outs.append(pltpu.make_async_copy(in_ref, in_out, outsem.at[3]))
        outs[-1].start()

    to_t = [remote(tbox.at[0], tbox.at[r], tsend.at[r], trecv.at[r], target) for r, target in others]

    def start_t():
        for copy in to_u:
            copy.wait()
        tbox[0] = jnp.sum(sbox[...], axis=0)
        for copy in to_t:
            copy.start()

    def end_t():
        for copy in to_t:
            copy.wait()
        total = (tbox[0] + tbox[1]) + (tbox[2] + tbox[3])
        for b in range(4):

            @pl.when(blk == b)
            def _():
                sums_ref[...] = total[:, b * rows : (b + 1) * rows]

    add_pair(2)

    @pl.when(c == 0)
    def _():
        add_x(3)

    add_half(1)
    start_t()

    @pl.when(c == 0)
    def _():
        add_pair(3)

    add_half(2)
    end_down()
    end_t()
    end_q()

    @pl.when(c == 0)
    def _():
        add_half(3)

    @pl.loop(0, pairs + 1)
    def _(s):
        for r, target in others:
            to_blk(s, r, target).wait_send()

    for r, target, count in received:

        @pl.loop(0, count + 1)
        def _(s):
            to_blk(s, r, target).wait_recv()

    for yy in range(2):
        for cc in range(2):
            slot = 2 * flip(y, yy) + flip(c, cc)
            p = 5 * yy + 3 * cc
            wide = 128 * (3 - cc)
            gout_ref[:, 128 * p : 128 * p + wide] = fin[slot, 0, :, :wide]
            for j in range(3 - cc):
                for t in range(3):
                    at = t * width + 128 * (p + j)
                    gqkv_ref[:, at : at + 128] = fin[slot, j + 1, :, 128 * t : 128 * t + 128]
    outs.append(pltpu.make_async_copy(gqkv_ref, gqkv_out, outsem.at[4]))
    outs[-1].start()
    outs.append(pltpu.make_async_copy(gout_ref, gout_out, outsem.at[5]))
    outs[-1].start()

    @pl.loop(0, pairs)
    def _(j):
        for r, target in others:
            to_own(j, r, target).wait_send()

    for gather in (row_tok, row_att, row, grads, normed):
        gather.drain()
    for copy in outs:
        copy.wait()


def finish_kernel(cells, sums_ref, *refs):
    count = 6
    arrays, (mean_ref, variance_ref, *grads), outs = refs[:count], refs[count : count + 6], refs[count + 6 : 2 * count + 6]
    held, isem, osem = refs[2 * count + 6 : -2], refs[-2], refs[-1]
    loads = [pltpu.make_async_copy(arrays[i], held[i], isem.at[i]) for i in range(count)]
    stores = [pltpu.make_async_copy(held[i], outs[i], osem.at[i]) for i in range(count)]
    for load in loads:
        load.start()
    for load, store in zip(loads, stores):
        load.wait()
        store.start()
    mean = sums_ref[4:5, :] / cells
    mean_ref[...] = mean
    variance_ref[...] = sums_ref[5:6, :] / cells - mean * mean
    for i in range(4):
        grads[i][...] = sums_ref[i : i + 1, :]
    for store in stores:
        store.wait()


def finish(cells, sums, *arrays):
    anywhere, v = pl.BlockSpec(memory_space=pl.ANY), pl.BlockSpec(memory_space=pltpu.VMEM)
    count = len(arrays)
    small = jax.ShapeDtypeStruct((1, sums.shape[1]), F32)
    return pl.pallas_call(
        functools.partial(finish_kernel, cells),
        out_shape=(small,) * 6 + tuple(jax.ShapeDtypeStruct(a.shape, a.dtype) for a in arrays),
        in_specs=[v] + [anywhere] * count,
        out_specs=(v,) * 6 + (anywhere,) * count,
        scratch_shapes=[pltpu.VMEM(a.shape, a.dtype) for a in arrays]
        + [pltpu.SemaphoreType.DMA((count,)), pltpu.SemaphoreType.DMA((count,))],
    )(sums, *arrays)


def whole_layer(cls_positions, tokens, grad, gain1, shift1, gain2, shift2, w_qkv, w_out, w_in, w_down):
    count, width = tokens.shape
    inner = w_in.shape[1]
    row_len, share = 4 * count, width // 8
    cut, owned, rows = inner // 8, inner // 32, width // 32
    block, depth = 512, 3
    v = pltpu.VMEM
    dma = pltpu.SemaphoreType.DMA
    anywhere = pl.BlockSpec(memory_space=pl.ANY)
    return pl.pallas_call(
        layer_kernel,
        out_shape=(
            jax.ShapeDtypeStruct((count, width), BF16),
            jax.ShapeDtypeStruct((count, width), BF16),
            jax.ShapeDtypeStruct((rows, 3 * width), F32),
            jax.ShapeDtypeStruct((rows, width), F32),
            jax.ShapeDtypeStruct((rows, inner), F32),
            jax.ShapeDtypeStruct((owned, width), F32),
            jax.ShapeDtypeStruct((8, rows), F32),
        ),
        in_specs=[pl.BlockSpec(memory_space=pltpu.SMEM)]
        + [anywhere] * 2
        + [pl.BlockSpec(memory_space=v)] * 4
        + [anywhere] * 4,
        out_specs=(anywhere,) * 6 + (pl.BlockSpec(memory_space=v),),
        scratch_shapes=[
            v((2, 4, count, width), BF16), v((2, 2 * count, width), BF16),
            v((3, row_len, 384), BF16), v((3, row_len, 128), F32), v((width, row_len), BF16), v((width, row_len), BF16),
            v((3, row_len, 128), BF16), v((4, 3, count, 128), BF16), v((2, 2 * count, width), BF16),
            v((count, width), BF16), v((count, width), BF16), v((rows, 3 * width), F32), v((rows, width), F32),
            v((rows, inner), F32), v((owned, width), F32),
            v((depth, width, block), BF16), v((depth, block, width), BF16),
            v((width, cut), BF16), v((cut, width), BF16), v((3, 128, width), BF16),
            v((2, 4, count, width), BF16), v((8 * count, cut), BF16), v((cut, 8 * count), BF16),
            v((4, 8, rows, cut), BF16), v((4, owned, width), BF16),
            v((2, 8, rows, cut), BF16), v((2, owned, width), BF16),
            v((8, rows, cut), BF16), v((owned, width), BF16), v((8, rows, cut), BF16), v((owned, width), BF16),
            v((8, rows, cut), BF16), v((8, rows, cut), BF16),
            v((count, width), F32), v((count, width), F32), v((count, width), F32),
            v((2, 2 * count, width), BF16), v((3, row_len, 128), F32), v((3, row_len, 384), BF16),
            v((row_len, 128), F32), v((row_len, 128), F32),
            v((4, 2, 2, 2, share, 384), BF16), v((3, 2, 2, share, 384), BF16), v((3, 2, 2, share, 384), BF16),
            v((3, 2, share, 384), BF16), v((3, 2, share, 384), BF16),
            v((2, 2, share, 384), BF16), v((2, 2, share, 384), BF16), v((2, share, 384), BF16),
            v((4, 4, share // 4, 384), F32), v((4, 4, share // 4, 384), F32),
            v((4, 3, count, 384), BF16),
            v((8, width), F32), v((8, 8, 256), F32), v((8, 8, 256), F32), v((4, 8, 256), F32),
            dma((2,)), dma((3, 3)), dma((3,)), dma((3,)), dma((3, 4)), dma((2, 4)), dma((4, 3)), dma((4, 3)),
            dma((3,)), dma((3,)), dma((6,)),
            dma((2 + 3 * depth,)), dma((2, depth)), dma((3,)), dma((3,)), dma((3,)), dma((3, 4)), dma((2, 4)),
            dma((2, 2)), dma((2, 2)), dma((2,)), dma((2,)), dma((8,)), dma((8,)),
            dma((4,)), dma((4,)), dma((4, 3)), dma((4, 3)), dma((4, 4)), dma((4, 4)), dma((4, 3)), dma((4, 3)),
            dma((8,)), dma((8,)), dma((4,)), dma((4,)),
        ],
        compiler_params=pltpu.CompilerParams(collective_id=1, has_side_effects=True, vmem_limit_bytes=64 * 2**20),
        cost_estimate=pl.CostEstimate(flops=40 * 2**30, bytes_accessed=50 * 2**20, transcendentals=0),
    )(cls_positions, tokens, grad, gain1, shift1, gain2, shift2, w_qkv, w_out, w_in, w_down)


def on_device(
    tokens,
    first_gain,
    first_shift,
    w_qkv,
    w_out,
    second_gain,
    second_shift,
    w_in,
    w_down,
    segment_ids,
    cls_positions,
    out_grad,
):
    tokens, out_grad = tokens[0], out_grad[0]
    layer, tokens_grad, grad_qkv, grad_out, grad_in, grad_down, sums = whole_layer(
        cls_positions, tokens, out_grad, first_gain, first_shift, second_gain, second_shift, w_qkv, w_out, w_in, w_down
    )
    mean, variance, gain1_grad, shift1_grad, gain2_grad, shift2_grad, *large = finish(
        cls_positions.size * lax.axis_size("dp"), sums, layer, tokens_grad, grad_qkv, grad_out, grad_in, grad_down
    )
    return (
        large[0][None],
        large[1][None],
        *large[2:],
        gain1_grad[0],
        shift1_grad[0],
        gain2_grad[0],
        shift2_grad[0],
        mean[0],
        variance[0],
    )


def solution(mesh):
    placed = (
        P("dp", "blk", None),
        P(),
        P(),
        P(),
        P(),
        P(),
        P(),
        P(),
        P(),
        P("dp", "blk"),
        P("dp", None),
        P("dp", "blk", None),
    )
    small = mesh.shape["dp"] == 8 and mesh.shape["blk"] == 4
    return jax.shard_map(
        on_device if small else on_device_general,
        mesh=mesh,
        in_specs=placed,
        out_specs=(
            P("dp", "blk", None),
            P("dp", "blk", None),
            P(("dp", "blk"), None),
            P(("dp", "blk"), None),
            P(("dp", "blk"), None),
            P(("dp", "blk"), None),
            P(("dp", "blk")),
            P(("dp", "blk")),
            P(("dp", "blk")),
            P(("dp", "blk")),
            P(("dp", "blk")),
            P(("dp", "blk")),
        ),
        check_vma=False,
    )
```

```python
import functools

import jax
import jax.numpy as jnp
from jax import lax
from jax.experimental import pallas as pl
from jax.experimental.pallas import tpu as pltpu
from jax.sharding import PartitionSpec as P

H = 20


EPSILON = 1e-05


def shifted(block, axis, distance):
    devices = range(lax.axis_size(axis))
    route = [((i - distance) % len(devices), i) for i in devices]
    return lax.ppermute(block, axis, route)


def layer_norm(values, gain, shift):
    center = values - jnp.mean(values, axis=-1, keepdims=True)
    spread = jnp.mean(center * center, axis=-1, keepdims=True)
    return center * lax.rsqrt(spread + EPSILON) * gain + shift


def exact_gelu(values):
    return jax.nn.gelu(values, approximate=False)


def same_cells(query_cells, key_cells):
    return query_cells[:, :, None] == key_cells[:, None, :]


def forward_block(queries, key_part, value_part, query_cells, key_cells, totals, weights):
    scores = jnp.einsum("sqhd,skhd->shqk", queries, key_part, preferred_element_type=jnp.float32)
    exp_scores = jnp.where(same_cells(query_cells, key_cells)[:, None], jnp.exp(scores), 0.0)
    weights = weights + jnp.sum(exp_scores, axis=-1)
    totals = totals + jnp.einsum(
        "shqk,skhd->sqhd",
        exp_scores.astype(jnp.bfloat16),
        value_part,
        preferred_element_type=jnp.float32,
    )
    return (totals, weights)


def backward_block(queries, scaled, deltas, query_cells, key_part, value_part, key_cells):
    scores = jnp.einsum("sqhd,skhd->shqk", queries, key_part, preferred_element_type=jnp.float32)
    exp_scores = jnp.where(same_cells(query_cells, key_cells)[:, None], jnp.exp(scores), 0.0)
    grad_exp = jnp.einsum("sqhd,skhd->shqk", scaled, value_part, preferred_element_type=jnp.float32)
    grad_scores = (exp_scores * (grad_exp - deltas[..., None])).astype(jnp.bfloat16)
    grad_queries = jnp.einsum(
        "shqk,skhd->sqhd", grad_scores, key_part, preferred_element_type=jnp.float32
    )
    grad_keys = jnp.einsum(
        "shqk,sqhd->skhd", grad_scores, queries, preferred_element_type=jnp.float32
    )
    grad_values = jnp.einsum(
        "shqk,sqhd->skhd",
        exp_scores.astype(jnp.bfloat16),
        scaled,
        preferred_element_type=jnp.float32,
    )
    return (grad_queries, grad_keys, grad_values)


def on_device_general(
    tokens,
    first_gain,
    first_shift,
    w_qkv,
    w_out,
    second_gain,
    second_shift,
    w_in,
    w_down,
    segment_ids,
    cls_positions,
    out_grad,
):
    seqs_here, block_len, width = tokens.shape
    head_count = H
    head_size = width // head_count
    blocks = lax.axis_size("blk")
    head_shape = (seqs_here, block_len, head_count, head_size)
    flat_shape = (seqs_here, block_len, width)
    tokens_wide = tokens.astype(jnp.float32)
    normed_low = layer_norm(tokens_wide, first_gain, first_shift).astype(jnp.bfloat16)
    projected = jnp.dot(normed_low, w_qkv, preferred_element_type=jnp.float32)
    queries = (projected[..., :width] * 0.125).astype(jnp.bfloat16).reshape(head_shape)
    key_part = projected[..., width : 2 * width].astype(jnp.bfloat16).reshape(head_shape)
    value_part = projected[..., 2 * width :].astype(jnp.bfloat16).reshape(head_shape)
    totals = jnp.zeros(head_shape, jnp.float32)
    weights = jnp.zeros((seqs_here, head_count, block_len), jnp.float32)
    totals, weights = forward_block(
        queries, key_part, value_part, segment_ids, segment_ids, totals, weights
    )

    def forward_step(position, loop_state):
        moving, totals_in, weights_in = loop_state
        moving = shifted((moving[0], moving[1], moving[2]), "blk", 1)
        totals_out, weights_out = forward_block(
            queries, moving[0], moving[1], segment_ids, moving[2], totals_in, weights_in
        )
        return (moving, totals_out, weights_out)

    moved_state, totals, weights = lax.fori_loop(
        0, blocks - 1, forward_step, ((key_part, value_part, segment_ids), totals, weights)
    )
    weights_rows = jnp.swapaxes(weights, 1, 2)[..., None]
    attended = totals / weights_rows
    attended_low = attended.reshape(flat_shape).astype(jnp.bfloat16)
    residual = tokens_wide + jnp.dot(attended_low, w_out, preferred_element_type=jnp.float32)
    normed_two_low = layer_norm(residual, second_gain, second_shift).astype(jnp.bfloat16)
    hidden_pre = jnp.dot(normed_two_low, w_in, preferred_element_type=jnp.float32)
    hidden_low = exact_gelu(hidden_pre).astype(jnp.bfloat16)
    layer = residual + jnp.dot(hidden_low, w_down, preferred_element_type=jnp.float32)
    offset = lax.axis_index("blk") * block_len
    places = (
        lax.broadcasted_iota(jnp.int32, (seqs_here, cls_positions.shape[1], block_len), 2) + offset
    )
    chosen = jnp.sum((places == cls_positions[:, :, None]).astype(jnp.float32), axis=1)
    cell_sums = jnp.sum(chosen[..., None] * layer, axis=(0, 1))
    cell_squares = jnp.sum(chosen[..., None] * layer * layer, axis=(0, 1))
    count = cls_positions.shape[0] * cls_positions.shape[1] * lax.axis_size("dp")
    share = width // (lax.axis_size("dp") * blocks)
    moment_sums = lax.psum((cell_sums, cell_squares), ("dp", "blk"))
    rank = lax.axis_index("dp") * blocks + lax.axis_index("blk")
    sum_share = lax.dynamic_slice_in_dim(moment_sums[0], rank * share, share)
    square_share = lax.dynamic_slice_in_dim(moment_sums[1], rank * share, share)
    grad_layer = out_grad.astype(jnp.float32)
    grad_down = jnp.einsum("sbf,sbd->fd", hidden_low, out_grad, preferred_element_type=jnp.float32)
    grad_hidden = jnp.einsum("sbd,fd->sbf", out_grad, w_down, preferred_element_type=jnp.float32)
    grad_pre = jax.vjp(exact_gelu, hidden_pre)[1](grad_hidden)[0].astype(jnp.bfloat16)
    grad_in = jnp.einsum(
        "sbd,sbf->df", normed_two_low, grad_pre, preferred_element_type=jnp.float32
    )
    grad_normed_two = jnp.einsum("sbf,df->sbd", grad_pre, w_in, preferred_element_type=jnp.float32)
    unused_two, pull_two = jax.vjp(layer_norm, residual, second_gain, second_shift)
    residual_part, second_gain_grad, second_shift_grad = pull_two(grad_normed_two)
    grad_residual = grad_layer + residual_part
    grad_proj = grad_residual.astype(jnp.bfloat16)
    grad_out = jnp.einsum(
        "sbd,sbe->de", attended_low, grad_proj, preferred_element_type=jnp.float32
    )
    grad_attended = jnp.einsum(
        "sbe,de->sbd", grad_proj, w_out, preferred_element_type=jnp.float32
    ).reshape(head_shape)
    scaled = (grad_attended / weights_rows).astype(jnp.bfloat16)
    deltas = jnp.swapaxes(jnp.sum(grad_attended * attended, axis=-1), 1, 2) / weights

    def key_step(position, loop_state):
        moving, key_sums, query_sum = loop_state
        grad_queries, grad_keys, grad_values = backward_block(
            queries, scaled, deltas, segment_ids, moving[0], moving[1], moving[2]
        )
        query_next = query_sum + grad_queries
        keys_next = key_sums[0] + grad_keys
        values_next = key_sums[1] + grad_values
        moving = shifted((moving[0], moving[1], moving[2]), "blk", 1)
        key_sums = (
            shifted(keys_next.astype(jnp.bfloat16), "blk", 1).astype(keys_next.dtype),
            shifted(values_next.astype(jnp.bfloat16), "blk", 1).astype(values_next.dtype),
        )
        return (moving, key_sums, query_next)

    zero_heads = jnp.zeros(head_shape, jnp.float32)
    moved_back, key_sums, query_total = lax.fori_loop(
        0,
        blocks,
        key_step,
        ((key_part, value_part, segment_ids), (zero_heads, zero_heads), zero_heads),
    )
    keys_total, values_total = (key_sums[0], key_sums[1])
    grad_qkv_low = jnp.concatenate(
        [
            (query_total * 0.125).reshape(flat_shape),
            keys_total.reshape(flat_shape),
            values_total.reshape(flat_shape),
        ],
        axis=-1,
    ).astype(jnp.bfloat16)
    grad_qkv = jnp.einsum(
        "sbd,sbe->de", normed_low, grad_qkv_low, preferred_element_type=jnp.float32
    )
    grad_normed_one = jnp.einsum(
        "sbe,de->sbd", grad_qkv_low, w_qkv, preferred_element_type=jnp.float32
    )
    unused_one, pull_one = jax.vjp(layer_norm, tokens_wide, first_gain, first_shift)
    tokens_part, first_gain_grad, first_shift_grad = pull_one(grad_normed_one)
    tokens_grad = (grad_residual + tokens_part).astype(jnp.bfloat16)
    summed = (
        lax.psum_scatter(grad_qkv, ("dp", "blk"), scatter_dimension=0, tiled=True),
        lax.psum_scatter(grad_out, ("dp", "blk"), scatter_dimension=0, tiled=True),
        lax.psum_scatter(grad_in, ("dp", "blk"), scatter_dimension=0, tiled=True),
        lax.psum_scatter(grad_down, ("dp", "blk"), scatter_dimension=0, tiled=True),
        lax.psum_scatter(first_gain_grad, ("dp", "blk"), scatter_dimension=0, tiled=True),
        lax.psum_scatter(first_shift_grad, ("dp", "blk"), scatter_dimension=0, tiled=True),
        lax.psum_scatter(second_gain_grad, ("dp", "blk"), scatter_dimension=0, tiled=True),
        lax.psum_scatter(second_shift_grad, ("dp", "blk"), scatter_dimension=0, tiled=True),
    )
    cls_mean = sum_share / count
    cls_variance = square_share / count - cls_mean * cls_mean
    return (
        layer.astype(jnp.bfloat16),
        tokens_grad,
        summed[0],
        summed[1],
        summed[2],
        summed[3],
        summed[4],
        summed[5],
        summed[6],
        summed[7],
        cls_mean,
        cls_variance,
    )


MESH = pl.DeviceIdType.MESH
F32 = jnp.float32
BF16 = jnp.bfloat16
NN = (((1,), (0,)), ((), ()))
NT = (((1,), (1,)), ((), ()))
TN = (((0,), (0,)), ((), ()))


def mm(left, right, dims=NN):
    return lax.dot_general(left, right, dims, preferred_element_type=F32)


def remote(src, dst, send, recv, target):
    return pltpu.make_async_remote_copy(
        src_ref=src, dst_ref=dst, send_sem=send, recv_sem=recv, device_id=target, device_id_type=MESH
    )


def greet(targets):
    barrier = pltpu.get_barrier_semaphore()
    for target in targets:
        pl.semaphore_signal(barrier, inc=1, device_id=target, device_id_type=MESH)
    pl.semaphore_wait(barrier, len(targets))


def place():
    dp, blk = lax.axis_index("dp"), lax.axis_index("blk")
    return dp, blk, dp // 2, lax.rem(dp, 2), blk // 2, lax.rem(blk, 2)


def piece(index, size):
    return pl.ds(pl.multiple_of(index * size, size), size)


def flip(mine, other):
    return mine + other - 2 * mine * other


class RowGather:
    def __init__(self, rows, size, y, c, sibling, ypeer, send, recv):
        near, far = rows.at[y, piece(c, size)], rows.at[1 - y, piece(c, size)]
        self.core = remote(near, near, send.at[0], recv.at[0], sibling)
        self.over = remote(near, near, send.at[1], recv.at[1], ypeer)
        self.last = remote(far, far, send.at[2], recv.at[2], sibling)

    def start(self):
        self.over.start()
        self.core.start()

    def forward(self):
        self.over.wait_recv()
        self.last.start()

    def arrive(self):
        self.core.wait_recv()
        self.last.wait_recv()

    def drain(self):
        for copy in (self.core, self.over, self.last):
            copy.wait_send()


class DpGather:
    def __init__(self, slots, z, x, blk, send, recv):
        self.slots, self.z, self.x, self.send, self.recv = slots, z, x, send, recv
        self.targets = ((2 * (z + 1) + x, blk), (2 * (z - 1) + x, blk), (2 * z + 1 - x, blk))

    def hop(self, kind, zz):
        slot = self.slots.at[self.x, zz]
        return remote(slot, slot, self.send.at[kind, zz], self.recv.at[self.x, zz], self.targets[kind])

    def up(self, zz):
        @pl.when(self.z < 3)
        def _():
            self.hop(0, zz).start()

        self.hop(2, zz).start()

    def down(self, zz):
        @pl.when(self.z > 0)
        def _():
            self.hop(1, zz).start()

    def start(self):
        self.up(self.z)
        self.down(self.z)

    def forward(self, step):
        below, above = self.z - step, self.z + step

        @pl.when(below >= 0)
        def _():
            self.hop(0, below).wait_recv()
            self.up(below)

        @pl.when(above <= 3)
        def _():
            self.hop(1, above).wait_recv()
            self.down(above)
            self.hop(2, above).start()

    def arrive(self, half):
        for k in range(2):
            slot = self.slots.at[1 - self.x, 2 * half + k]
            done = self.recv.at[1 - self.x, 2 * half + k]
            remote(slot, slot, self.send.at[2, k], done, self.targets[2]).wait_recv()

    def drain(self):
        for zz in range(4):
            self.hop(2, zz).wait_send()

            @pl.when((self.z < 3) & (zz <= self.z))
            def _():
                self.hop(0, zz).wait_send()

            @pl.when((self.z > 0) & (zz >= self.z))
            def _():
                self.hop(1, zz).wait_send()


def centered(values):
    center = values - jnp.mean(values, axis=-1, keepdims=True)
    spread = jnp.mean(center * center, axis=-1, keepdims=True)
    scale = lax.rsqrt(spread + EPSILON)
    return center * scale, scale


def norm_back(grad, unit, scale):
    return scale * (
        grad - jnp.mean(grad, axis=-1, keepdims=True) - unit * jnp.mean(grad * unit, axis=-1, keepdims=True)
    )


def half_of(pair, head):
    lanes = lax.broadcasted_iota(jnp.int32, pair.shape, 1) // 64
    return jnp.where(lanes == head, pair, jnp.zeros_like(pair))


def cells_at(cls_ref, places):
    found = jnp.zeros(places.shape, jnp.int32)
    for n in range(cls_ref.shape[1]):
        found = found + (places >= cls_ref[0, n]).astype(jnp.int32)
    return found


def same_cell(cls_ref, start, count, row_len):
    mine = lax.broadcasted_iota(jnp.int32, (count, 1), 0) + start
    other = lax.broadcasted_iota(jnp.int32, (1, row_len), 1)
    return cells_at(cls_ref, mine) == cells_at(cls_ref, other)


def gelu_parts(pre):
    cdf = 0.5 * (1.0 + lax.erf(pre * 0.7071067811865476))
    return cdf, cdf + pre * (0.3989422804014327 * jnp.exp(-0.5 * pre * pre))


def as_row(ref):
    return ref[...].reshape(1, ref.shape[0])


def layer_kernel(
    cls_ref, tok_hbm, grad_hbm, gain1_ref, shift1_ref, gain2_ref, shift2_ref, wqkv_ref, wout_ref, win_ref, wdown_ref,
    layer_out, tgrad_out, gqkv_out, gout_out, in_out, down_out, sums_ref,
    gg, rows_all, qkv_ref, att_ref, turned_ref, aturned_ref, attlow, abox, arow,
    layer_ref, tgrad_ref, gqkv_ref, gout_ref, in_ref, down_ref,
    st_in, st_dn, wi, wd, wo, gx, gp, ht, part_in, part_dn, sib_in, sib_dn, ysend_in, ysend_dn, yrecv_in, yrecv_dn,
    slab, slab_in, residual, unit, gnorm, grow, gatt, low, keys, values, part, xin, zout, zin, zlast, zfirst, hfirst, xfirst, full, fin, landing,
    sums, sbuf, sbox, tbox,
    isem, lsem, rsend, rrecv, ogsend, ogrecv, bsend, brecv, arsend, arrecv, outsem,
    wsem, ssem, osem, gsend, grecv, dsend, drecv, sibs, sibr, ysend, yrecv, qsend, qrecv,
    xsend, xrecv, zsend, zrecv, fsend, frecv, asend, arecv, usend, urecv, tsend, trecv,
):
    dp, blk, z, x, y, c = place()
    tokens, width = tok_hbm.shape
    row_len, both = 4 * tokens, 2 * tokens
    first, pairs = 5 * y + 3 * c, 3 - c
    cut, owned, rows = wi.shape[1], down_ref.shape[0], in_ref.shape[0]
    share = width // 8
    block = st_in.shape[2]
    steps = win_ref.shape[1] // block
    depth = st_in.shape[0]
    sibling, ypeer, diag = (dp, 2 * y + 1 - c), (dp, 2 * (1 - y) + c), (dp, 2 * (1 - y) + 1 - c)
    xpeer = (2 * z + 1 - x, blk)
    others = ((1, sibling), (2, ypeer), (3, diag))
    received = ((1, sibling, 2 + c), (2, ypeer, pairs), (3, diag, 2 + c))

    tok_in = pltpu.make_async_copy(tok_hbm, rows_all.at[y, piece(c, tokens), :], isem.at[0])
    grad_in = pltpu.make_async_copy(grad_hbm, gg.at[x, z], isem.at[1])
    tok_in.start()
    grad_in.start()

    def load(j, t):
        source = wqkv_ref.at[:, pl.ds(pl.multiple_of(t * width + (first + j) * 128, 128), 128)]
        return pltpu.make_async_copy(source, st_in.at[j, :, pl.ds(t * 128, 128)], lsem.at[j, t])

    @pl.loop(0, pairs)
    def _(j):
        for t in range(3):
            load(j, t).start()

    def stream_in(i):
        slot = lax.rem(i, depth)
        return pltpu.make_async_copy(win_ref.at[:, piece(i, block)], st_in.at[slot], ssem.at[0, slot])

    def stream_dn(i):
        slot = lax.rem(i, depth)
        return pltpu.make_async_copy(wdown_ref.at[piece(i, block), :], st_dn.at[slot], ssem.at[1, slot])

    tails = ((0, block), (1, block), (2, width - 2 * block))

    def load_out(i, size):
        return pltpu.make_async_copy(
            wout_ref.at[pl.ds(i * block, size), :], st_dn.at[i, pl.ds(0, size), :], ssem.at[1, i]
        )

    def load_rows(j):
        return pltpu.make_async_copy(wout_ref.at[piece(first + j, 128), :], wo.at[j], osem.at[j])

    greet([sibling, ypeer, diag] + [(lax.rem(dp + k, 8), blk) for k in range(1, 8)])
    row_tok = RowGather(rows_all, tokens, y, c, sibling, ypeer, rsend, rrecv)
    grads = DpGather(gg, z, x, blk, ogsend, ogrecv)
    tok_in.wait()
    row_tok.start()
    grad_in.wait()
    grads.start()
    for i, size in tails:
        load_out(i, size).start()

    @pl.loop(0, pairs)
    def _(j):
        load_rows(j).start()
        for t in range(3):
            load(j, t).wait()

    normed_rows = wd

    @pl.loop(0, 2)
    def _(step):
        @pl.when(step == 0)
        def _():
            row_tok.core.wait_recv()

        @pl.when(step == 1)
        def _():
            row_tok.forward()
            row_tok.last.wait_recv()
            grads.forward(1)

        chip = flip(y, step)
        at = piece(chip, both)
        normed_rows[at, :] = (centered(rows_all[chip].astype(F32))[0] * as_row(gain1_ref) + as_row(shift1_ref)).astype(BF16)

        @pl.loop(0, pairs)
        def _(j):
            made = mm(normed_rows[at, :], st_in[j, :, 0:384])
            qkv_ref[j, at, 0:128] = (made[:, 0:128] * 0.125).astype(BF16)
            qkv_ref[j, at, 128:384] = made[:, 128:384].astype(BF16)

    for i in range(depth - 1):
        stream_in(i).start()

    def to_own(j, r, target):
        return remote(attlow.at[j, piece(target[1], tokens), :], abox.at[r, j], bsend.at[r, j], brecv.at[r, j], target)

    @pl.loop(0, pairs)
    def _(j):
        @pl.loop(0, 2)
        def _(part):
            at = piece(part, both)
            same = same_cell(cls_ref, part * both, both, row_len)
            pair = jnp.zeros((both, 128), F32)
            for head in range(2):
                scores = mm(half_of(qkv_ref[j, at, 0:128], head), qkv_ref[j, :, 128:256], NT)
                weigh = jnp.where(same, jnp.exp(scores), 0.0)
                total = jnp.sum(weigh, axis=-1, keepdims=True)
                pair = pair + half_of(mm(weigh.astype(BF16), qkv_ref[j, :, 256:384]) / total, head)
            att_ref[j, at, :] = pair
            attlow[j, at, :] = pair.astype(BF16)

        for r, target in others:
            to_own(j, r, target).start()
        abox[0, j] = attlow[j, piece(blk, tokens), :]

        @pl.when(j == 1)
        def _():
            grads.forward(2)

    for b in range(4):
        at = slice(b * tokens, (b + 1) * tokens)
        turned_ref[:, at] = normed_rows[at, :].T

    for r, target, count in received:

        @pl.loop(0, count)
        def _(j):
            to_own(j, r, target).wait_recv()

    own_at = (y, piece(c, tokens))
    for p in range(10):
        yy, cc = p // 5, (p % 5) // 3
        slot = 2 * flip(y, yy) + flip(c, cc)
        arow[y, piece(c, tokens), 128 * p : 128 * p + 128] = abox[slot, p % 5 - 3 * cc]
    row_att = RowGather(arow, tokens, y, c, sibling, ypeer, arsend, arrecv)

    made = rows_all[y, piece(c, tokens), :].astype(F32)
    for i, size in tails:
        load_out(i, size).wait()
        made = made + mm(arow[y, piece(c, tokens), i * block : i * block + size], st_dn[i, :size, :])
    for i in range(depth - 1):
        stream_dn(i).start()
    residual[...] = made
    made, scale2 = centered(made)
    unit[...] = made
    gx[x, z] = (made * as_row(gain2_ref) + as_row(shift2_ref)).astype(BF16)
    normed = DpGather(gx, z, x, blk, dsend, drecv)
    normed.start()
    row_att.start()
    gnorm[...] = jnp.zeros_like(gnorm)

    @pl.loop(0, steps)
    def _(i):
        slot = lax.rem(i, depth)

        @pl.when(i + depth - 1 < steps)
        def _():
            stream_in(i + depth - 1).start()
            stream_dn(i + depth - 1).start()

        stream_in(i).wait()
        stream_dn(i).wait()
        pre = mm(gx[x, z], st_in[slot])
        cdf, slope = gelu_parts(pre)
        grad = (mm(gg[x, z], st_dn[slot], NT) * slope).astype(BF16)
        residual[...] += mm((pre * cdf).astype(BF16), st_dn[slot])
        gnorm[...] += mm(grad, st_in[slot], NT)

        @pl.when(i == 2)
        def _():
            grads.forward(3)

        @pl.when(i == 6)
        def _():
            row_att.forward()
            normed.forward(1)

    load_in = pltpu.make_async_copy(win_ref.at[:, piece(dp, cut)], wi, wsem.at[0])
    load_dn = pltpu.make_async_copy(wdown_ref.at[piece(dp, cut), :], wd, wsem.at[1])
    load_in.start()
    load_dn.start()
    layer = residual[...]
    layer_ref[...] = layer.astype(BF16)
    outs = [pltpu.make_async_copy(layer_ref, layer_out, outsem.at[0])]
    outs[0].start()
    sums[...] = jnp.zeros_like(sums)
    spots = lax.broadcasted_iota(jnp.int32, (tokens, 1), 0) + blk * tokens
    chosen = jnp.zeros((tokens, 1), F32)
    for n in range(cls_ref.shape[1]):
        chosen = chosen + (spots == cls_ref[0, n]).astype(F32)
    sums[4:5, :] = jnp.sum(chosen * layer, axis=0, keepdims=True)
    sums[5:6, :] = jnp.sum(chosen * layer * layer, axis=0, keepdims=True)
    grad = gnorm[...]
    sums[2:3, :] = jnp.sum(grad * unit[...], axis=0, keepdims=True)
    sums[3:4, :] = jnp.sum(grad, axis=0, keepdims=True)
    made = gg[x, z].astype(F32) + norm_back(grad * as_row(gain2_ref), unit[...], scale2)
    residual[...] = made
    grow[y, piece(c, tokens), :] = made.astype(BF16)
    row = RowGather(grow, tokens, y, c, sibling, ypeer, gsend, grecv)
    row.start()
    normed.forward(2)
    load_in.wait()
    load_dn.wait()

    def stream_qkv(p, t):
        slot = lax.rem(p, depth)
        source = wqkv_ref.at[:, pl.ds(pl.multiple_of(t * width + p * 128, 128), 128)]
        return pltpu.make_async_copy(source, st_in.at[slot, :, pl.ds(t * 128, 128)], wsem.at[2 + 3 * slot + t])

    for p in range(depth):
        for t in range(3):
            stream_qkv(p, t).start()
    near = z // 2

    def make(xx, half):
        at = piece(2 * xx + half, both)
        pre = mm(gx[xx, piece(half, 2)].reshape(both, width), wi[...])
        cdf, slope = gelu_parts(pre)
        ht[:, at] = (pre * cdf).astype(BF16).T
        gp[at, :] = (mm(gg[xx, piece(half, 2)].reshape(both, width), wd[...], NT) * slope).astype(BF16)

    def makes(first_step, last_step):
        @pl.loop(first_step, last_step)
        def _(step):
            make(flip(x, lax.rem(step, 2)), flip(near, step // 2))

    makes(0, 1)
    row_att.arrive()
    for b in range(4):
        aturned_ref[:, b * tokens : (b + 1) * tokens] = arow[b // 2, (b % 2) * tokens : (b % 2 + 1) * tokens, :].T
    row.forward()
    row.arrive()

    @pl.loop(0, pairs)
    def _(j):
        load_rows(j).wait()
        gatt[j] = mm(grow[...].reshape(row_len, width), wo[j], NT)

    even, pair_z, half_z = lax.rem(z, 2), z + 1 - 2 * lax.rem(z, 2), lax.rem(z + 2, 4)

    def to_x(s):
        return remote(part.at[s, 1 - x], xin.at[s - 1], xsend.at[s], xrecv.at[s], xpeer)

    def to_pair(s):
        return remote(zout.at[s - 1, 1 - even], zin.at[s - 1], zsend.at[s, 0], zrecv.at[s, 0], (2 * pair_z + x, blk))

    def to_half(s):
        return remote(zlast.at[s - 1, 0], zlast.at[s - 1, 1], zsend.at[s, 1], zrecv.at[s, 1], (2 * half_z + x, blk))

    other_half, my_half = 1 - z // 2, z // 2
    first_pair = remote(part.at[0, :, 1 - even], zfirst, zsend.at[0, 0], zrecv.at[0, 0], (2 * pair_z + x, blk))
    first_half = remote(hfirst.at[0], hfirst.at[1], zsend.at[0, 1], zrecv.at[0, 1], (2 * half_z + x, blk))
    first_x = remote(xfirst.at[0], xfirst.at[1], xsend.at[0], xrecv.at[0], xpeer)

    def to_blk(s, r, target):
        return remote(full.at[s, target[1]], fin.at[r, s], fsend.at[r, s], frecv.at[r, s], target)

    def to_low(j, r, target):
        return remote(low.at[j, piece(target[1], tokens), :], landing.at[r, j], asend.at[r, j], arecv.at[r, j], target)

    def add_x(s):
        to_x(s).wait()
        for k in range(4):
            zout[s - 1, k // 2, k % 2] = (part[s, x, k // 2, k % 2].astype(F32) + xin[s - 1, k // 2, k % 2].astype(F32)).astype(BF16)
        to_pair(s).start()

    def add_pair(s):
        to_pair(s).wait()
        away = 1 - z // 2
        zlast[s - 1, 0] = (zout[s - 1, even, away].astype(F32) + zin[s - 1, away].astype(F32)).astype(BF16)
        to_half(s).start()

    def add_half(s):
        to_half(s).wait()
        mine = z // 2
        total = zout[s - 1, even, mine].astype(F32) + zin[s - 1, mine].astype(F32) + zlast[s - 1, 1].astype(F32)
        to_owners(s, total)

    def to_owners(s, total):
        for b in range(4):
            full[s, b] = total[b * rows : (b + 1) * rows]
        for r, target in others:
            to_blk(s, r, target).start()
        fin[0, s] = full[s, blk]

    def first_a():
        first_pair.wait()
        for xx in range(2):
            hfirst[0, xx] = (part[0, xx, even, other_half].astype(F32) + zfirst[xx, other_half].astype(F32)).astype(BF16)
        first_half.start()

    def first_sum(xx):
        return part[0, xx, even, my_half].astype(F32) + zfirst[xx, my_half].astype(F32) + hfirst[1, xx].astype(F32)

    def first_b():
        first_half.wait()
        xfirst[0] = first_sum(1 - x).astype(BF16)
        first_x.start()

    def first_c():
        first_x.wait()
        to_owners(0, first_sum(x) + xfirst[1].astype(F32))

    def weight_part(s, left, right):
        @pl.loop(0, 4)
        def _(zz):
            made = mm(left[piece(zz, 2 * share), :], right)
            part[s, 0, lax.rem(zz, 2), zz // 2] = made[:share].astype(BF16)
            part[s, 1, lax.rem(zz, 2), zz // 2] = made[share:].astype(BF16)

    @pl.when(c == 0)
    def _():
        weight_part(0, aturned_ref, grow[:, :, pl.ds(pl.multiple_of(first * 128, 128), 384)].reshape(row_len, 384))

    @pl.when(c == 1)
    def _():
        right = grow[:, :, pl.ds(pl.multiple_of(first * 128, 128), 256)].reshape(row_len, 256)
        weight_part(0, aturned_ref, jnp.concatenate([right, jnp.zeros((row_len, 128), BF16)], axis=1))

    first_pair.start()
    normed.forward(3)
    to_sibling = []
    for kind, source, box in ((0, part_in, sib_in), (1, part_dn, sib_dn)):
        for yy in range(2):
            away = source.at[2 * yy + (1 - c)]
            to_sibling.append(remote(away, box.at[yy], sibs.at[kind, yy], sibr.at[kind, yy], sibling))
    to_y = (
        remote(ysend_in, yrecv_in, ysend.at[0], yrecv.at[0], ypeer),
        remote(ysend_dn, yrecv_dn, ysend.at[1], yrecv.at[1], ypeer),
    )

    over = 2 * (1 - y) + c

    @pl.loop(0, pairs)
    def _(j):
        keys[...] = jnp.zeros_like(keys)
        values[...] = jnp.zeros_like(values)

        @pl.loop(0, 2)
        def _(half):
            at = piece(half, both)
            same = same_cell(cls_ref, half * both, both, row_len)
            queries_grad = jnp.zeros((both, 128), F32)
            for head in range(2):
                query = half_of(qkv_ref[j, at, 0:128], head)
                key = half_of(qkv_ref[j, :, 128:256], head)
                grad = half_of(gatt[j, at, :], head)
                weigh = jnp.where(same, jnp.exp(mm(query, key, NT)), 0.0)
                total = jnp.sum(weigh, axis=-1, keepdims=True)
                scaled = (grad / total).astype(BF16)
                delta = jnp.sum(grad * att_ref[j, at, :], axis=-1, keepdims=True) / total
                spread = mm(scaled, qkv_ref[j, :, 256:384], NT)
                score = (weigh * (spread - delta)).astype(BF16)
                queries_grad = queries_grad + mm(score, key)
                keys[...] += mm(score, query, TN)
                values[...] += mm(weigh.astype(BF16), scaled, TN)
            low[j, at, 0:128] = (queries_grad * 0.125).astype(BF16)

        low[j, :, 128:256] = keys[...].astype(BF16)
        low[j, :, 256:384] = values[...].astype(BF16)
        for r, target in others:
            to_low(j, r, target).start()
        weight_part(j + 1, turned_ref, low[j])
        to_x(j + 1).start()

        @pl.when(j == pairs - 1)
        def _():
            for half in range(2):
                normed.arrive(half)
                grads.arrive(half)
            makes(1, 4)
            first_a()

            @pl.loop(0, 2)
            def _(half):
                left = gx[:, :, :, piece(half, width // 2)].reshape(8 * tokens, width // 2)
                made = mm(left, gp[...], TN)
                for n in range(4):
                    for q in range(4):
                        at = n * share + q * rows
                        part_in[q, 4 * half + n] = made[at : at + rows].astype(BF16)

            to_sibling[0].start()
            to_sibling[1].start()
            every = gg[...].reshape(8 * tokens, width)

            @pl.loop(0, 4)
            def _(q):
                part_dn[q] = mm(ht[piece(q, owned), :], every).astype(BF16)

            to_sibling[2].start()
            to_sibling[3].start()
            to_sibling[0].wait()
            to_sibling[1].wait()
            ysend_in[...] = (part_in[over].astype(F32) + sib_in[1 - y].astype(F32)).astype(BF16)
            to_y[0].start()
            to_sibling[2].wait()
            to_sibling[3].wait()
            ysend_dn[...] = (part_dn[over].astype(F32) + sib_dn[1 - y].astype(F32)).astype(BF16)
            first_b()
            add_x(1)

    add_x(2)
    add_pair(1)

    mine = 2 * y + c
    to_q = []
    for k in range(1, 8):
        target = lax.rem(dp + k, 8)
        to_q.append(remote(slab.at[target], slab_in.at[dp], qsend.at[k], qrecv.at[k], (target, blk)))

    def start_q():
        to_y[0].wait()
        to_y[1].start()
        total = part_in[mine].astype(F32) + sib_in[y].astype(F32) + yrecv_in[...].astype(F32)
        slab[...] = total.astype(BF16)
        for copy in to_q:
            copy.start()
        slab_in[dp] = slab[dp]

    start_q()
    @pl.when(c == 0)
    def _():
        add_x(3)

    first_c()

    @pl.loop(0, pairs)
    def _(j):
        landing[0, j] = low[j, piece(blk, tokens), :]
        for r, target in others:
            to_low(j, r, target).wait_send()

    for r, target, count in received:

        @pl.loop(0, count)
        def _(j):
            to_low(j, r, target).wait_recv()

    gnorm[...] = jnp.zeros_like(gnorm)
    @pl.loop(0, 10)
    def _(p):
        @pl.when((p > 0) & (p + depth - 1 < 10))
        def _():
            for t in range(3):
                stream_qkv(p + depth - 1, t).start()

        for t in range(3):
            stream_qkv(p, t).wait()
        yy, pp = p // 5, lax.rem(p, 5)
        cc = pp // 3
        slot = 2 * flip(y, yy) + flip(c, cc)
        gnorm[...] += mm(landing[slot, pp - 3 * cc], st_in[lax.rem(p, depth), :, 0:384], NT)

    grad = gnorm[...]
    made, scale1 = centered(rows_all[y, piece(c, tokens), :].astype(F32))
    sums[0:1, :] = jnp.sum(grad * made, axis=0, keepdims=True)
    sums[1:2, :] = jnp.sum(grad, axis=0, keepdims=True)
    sbuf[...] = jnp.zeros_like(sbuf)
    for k in range(8):
        sbuf[k, :, 0:share] = sums[:, k * share : (k + 1) * share]
    to_u = []
    for k in range(1, 8):
        target = lax.rem(dp + k, 8)
        to_u.append(remote(sbuf.at[target], sbox.at[dp], usend.at[k], urecv.at[k], (target, blk)))
        to_u[-1].start()
    sbox[dp] = sbuf[dp]
    tgrad_ref[...] = (residual[...] + norm_back(grad * as_row(gain1_ref), made, scale1)).astype(BF16)
    outs.append(pltpu.make_async_copy(tgrad_ref, tgrad_out, outsem.at[1]))
    outs[-1].start()

    def end_down():
        to_y[1].wait()
        down_ref[...] = part_dn[mine].astype(F32) + sib_dn[y].astype(F32) + yrecv_dn[...].astype(F32)
        outs.append(pltpu.make_async_copy(down_ref, down_out, outsem.at[2]))
        outs[-1].start()

    def end_q():
        for copy in to_q:
            copy.wait()
        for s in range(8):
            in_ref[:, s * cut : (s + 1) * cut] = slab_in[s].astype(F32)
        outs.append(pltpu.make_async_copy(in_ref, in_out, outsem.at[3]))
        outs[-1].start()

    to_t = [remote(tbox.at[0], tbox.at[r], tsend.at[r], trecv.at[r], target) for r, target in others]

    def start_t():
        for copy in to_u:
            copy.wait()
        tbox[0] = jnp.sum(sbox[...], axis=0)
        for copy in to_t:
            copy.start()

    def end_t():
        for copy in to_t:
            copy.wait()
        total = (tbox[0] + tbox[1]) + (tbox[2] + tbox[3])
        for b in range(4):

            @pl.when(blk == b)
            def _():
                sums_ref[...] = total[:, b * rows : (b + 1) * rows]

    add_pair(2)
    add_half(1)

    @pl.when(c == 0)
    def _():
        add_pair(3)

    start_t()
    add_half(2)

    @pl.when(c == 0)
    def _():
        add_half(3)

    end_down()
    end_t()
    end_q()

    @pl.loop(0, pairs + 1)
    def _(s):
        for r, target in others:
            to_blk(s, r, target).wait_send()

    for r, target, count in received:

        @pl.loop(0, count + 1)
        def _(s):
            to_blk(s, r, target).wait_recv()

    for yy in range(2):
        for cc in range(2):
            slot = 2 * flip(y, yy) + flip(c, cc)
            p = 5 * yy + 3 * cc
            wide = 128 * (3 - cc)
            gout_ref[:, 128 * p : 128 * p + wide] = fin[slot, 0, :, :wide]
            for j in range(3 - cc):
                for t in range(3):
                    at = t * width + 128 * (p + j)
                    gqkv_ref[:, at : at + 128] = fin[slot, j + 1, :, 128 * t : 128 * t + 128]
    outs.append(pltpu.make_async_copy(gqkv_ref, gqkv_out, outsem.at[4]))
    outs[-1].start()
    outs.append(pltpu.make_async_copy(gout_ref, gout_out, outsem.at[5]))
    outs[-1].start()

    @pl.loop(0, pairs)
    def _(j):
        for r, target in others:
            to_own(j, r, target).wait_send()

    for gather in (row_tok, row_att, row, grads, normed):
        gather.drain()
    for copy in outs:
        copy.wait()


def finish_kernel(cells, sums_ref, *refs):
    count = 6
    arrays, (mean_ref, variance_ref, *grads), outs = refs[:count], refs[count : count + 6], refs[count + 6 : 2 * count + 6]
    held, isem, osem = refs[2 * count + 6 : -2], refs[-2], refs[-1]
    loads = [pltpu.make_async_copy(arrays[i], held[i], isem.at[i]) for i in range(count)]
    stores = [pltpu.make_async_copy(held[i], outs[i], osem.at[i]) for i in range(count)]
    for load in loads:
        load.start()
    for load, store in zip(loads, stores):
        load.wait()
        store.start()
    mean = sums_ref[4:5, :] / cells
    mean_ref[...] = mean
    variance_ref[...] = sums_ref[5:6, :] / cells - mean * mean
    for i in range(4):
        grads[i][...] = sums_ref[i : i + 1, :]
    for store in stores:
        store.wait()


def finish(cells, sums, *arrays):
    anywhere, v = pl.BlockSpec(memory_space=pl.ANY), pl.BlockSpec(memory_space=pltpu.VMEM)
    count = len(arrays)
    small = jax.ShapeDtypeStruct((1, sums.shape[1]), F32)
    return pl.pallas_call(
        functools.partial(finish_kernel, cells),
        out_shape=(small,) * 6 + tuple(jax.ShapeDtypeStruct(a.shape, a.dtype) for a in arrays),
        in_specs=[v] + [anywhere] * count,
        out_specs=(v,) * 6 + (anywhere,) * count,
        scratch_shapes=[pltpu.VMEM(a.shape, a.dtype) for a in arrays]
        + [pltpu.SemaphoreType.DMA((count,)), pltpu.SemaphoreType.DMA((count,))],
    )(sums, *arrays)


def whole_layer(cls_positions, tokens, grad, gain1, shift1, gain2, shift2, w_qkv, w_out, w_in, w_down):
    count, width = tokens.shape
    inner = w_in.shape[1]
    row_len, share = 4 * count, width // 8
    cut, owned, rows = inner // 8, inner // 32, width // 32
    block, depth = 512, 3
    v = pltpu.VMEM
    dma = pltpu.SemaphoreType.DMA
    anywhere = pl.BlockSpec(memory_space=pl.ANY)
    return pl.pallas_call(
        layer_kernel,
        out_shape=(
            jax.ShapeDtypeStruct((count, width), BF16),
            jax.ShapeDtypeStruct((count, width), BF16),
            jax.ShapeDtypeStruct((rows, 3 * width), F32),
            jax.ShapeDtypeStruct((rows, width), F32),
            jax.ShapeDtypeStruct((rows, inner), F32),
            jax.ShapeDtypeStruct((owned, width), F32),
            jax.ShapeDtypeStruct((8, rows), F32),
        ),
        in_specs=[pl.BlockSpec(memory_space=pltpu.SMEM)]
        + [anywhere] * 2
        + [pl.BlockSpec(memory_space=v)] * 4
        + [anywhere] * 4,
        out_specs=(anywhere,) * 6 + (pl.BlockSpec(memory_space=v),),
        scratch_shapes=[
            v((2, 4, count, width), BF16), v((2, 2 * count, width), BF16),
            v((3, row_len, 384), BF16), v((3, row_len, 128), F32), v((width, row_len), BF16), v((width, row_len), BF16),
            v((3, row_len, 128), BF16), v((4, 3, count, 128), BF16), v((2, 2 * count, width), BF16),
            v((count, width), BF16), v((count, width), BF16), v((rows, 3 * width), F32), v((rows, width), F32),
            v((rows, inner), F32), v((owned, width), F32),
            v((depth, width, block), BF16), v((depth, block, width), BF16),
            v((width, cut), BF16), v((cut, width), BF16), v((3, 128, width), BF16),
            v((2, 4, count, width), BF16), v((8 * count, cut), BF16), v((cut, 8 * count), BF16),
            v((4, 8, rows, cut), BF16), v((4, owned, width), BF16),
            v((2, 8, rows, cut), BF16), v((2, owned, width), BF16),
            v((8, rows, cut), BF16), v((owned, width), BF16), v((8, rows, cut), BF16), v((owned, width), BF16),
            v((8, rows, cut), BF16), v((8, rows, cut), BF16),
            v((count, width), F32), v((count, width), F32), v((count, width), F32),
            v((2, 2 * count, width), BF16), v((3, row_len, 128), F32), v((3, row_len, 384), BF16),
            v((row_len, 128), F32), v((row_len, 128), F32),
            v((4, 2, 2, 2, share, 384), BF16), v((3, 2, 2, share, 384), BF16), v((3, 2, 2, share, 384), BF16),
            v((3, 2, share, 384), BF16), v((3, 2, share, 384), BF16),
            v((2, 2, share, 384), BF16), v((2, 2, share, 384), BF16), v((2, share, 384), BF16),
            v((4, 4, share // 4, 384), F32), v((4, 4, share // 4, 384), F32),
            v((4, 3, count, 384), BF16),
            v((8, width), F32), v((8, 8, 256), F32), v((8, 8, 256), F32), v((4, 8, 256), F32),
            dma((2,)), dma((3, 3)), dma((3,)), dma((3,)), dma((3, 4)), dma((2, 4)), dma((4, 3)), dma((4, 3)),
            dma((3,)), dma((3,)), dma((6,)),
            dma((2 + 3 * depth,)), dma((2, depth)), dma((3,)), dma((3,)), dma((3,)), dma((3, 4)), dma((2, 4)),
            dma((2, 2)), dma((2, 2)), dma((2,)), dma((2,)), dma((8,)), dma((8,)),
            dma((4,)), dma((4,)), dma((4, 3)), dma((4, 3)), dma((4, 4)), dma((4, 4)), dma((4, 3)), dma((4, 3)),
            dma((8,)), dma((8,)), dma((4,)), dma((4,)),
        ],
        compiler_params=pltpu.CompilerParams(collective_id=1, has_side_effects=True, vmem_limit_bytes=64 * 2**20),
        cost_estimate=pl.CostEstimate(flops=40 * 2**30, bytes_accessed=50 * 2**20, transcendentals=0),
    )(cls_positions, tokens, grad, gain1, shift1, gain2, shift2, w_qkv, w_out, w_in, w_down)


def on_device(
    tokens,
    first_gain,
    first_shift,
    w_qkv,
    w_out,
    second_gain,
    second_shift,
    w_in,
    w_down,
    segment_ids,
    cls_positions,
    out_grad,
):
    tokens, out_grad = tokens[0], out_grad[0]
    layer, tokens_grad, grad_qkv, grad_out, grad_in, grad_down, sums = whole_layer(
        cls_positions, tokens, out_grad, first_gain, first_shift, second_gain, second_shift, w_qkv, w_out, w_in, w_down
    )
    mean, variance, gain1_grad, shift1_grad, gain2_grad, shift2_grad, *large = finish(
        cls_positions.size * lax.axis_size("dp"), sums, layer, tokens_grad, grad_qkv, grad_out, grad_in, grad_down
    )
    return (
        large[0][None],
        large[1][None],
        *large[2:],
        gain1_grad[0],
        shift1_grad[0],
        gain2_grad[0],
        shift2_grad[0],
        mean[0],
        variance[0],
    )


def solution(mesh):
    placed = (
        P("dp", "blk", None),
        P(),
        P(),
        P(),
        P(),
        P(),
        P(),
        P(),
        P(),
        P("dp", "blk"),
        P("dp", None),
        P("dp", "blk", None),
    )
    small = mesh.shape["dp"] == 8 and mesh.shape["blk"] == 4
    return jax.shard_map(
        on_device if small else on_device_general,
        mesh=mesh,
        in_specs=placed,
        out_specs=(
            P("dp", "blk", None),
            P("dp", "blk", None),
            P(("dp", "blk"), None),
            P(("dp", "blk"), None),
            P(("dp", "blk"), None),
            P(("dp", "blk"), None),
            P(("dp", "blk")),
            P(("dp", "blk")),
            P(("dp", "blk")),
            P(("dp", "blk")),
            P(("dp", "blk")),
            P(("dp", "blk")),
        ),
        check_vma=False,
    )
```

```python
import functools

import jax
import jax.numpy as jnp
from jax import lax
from jax.experimental import pallas as pl
from jax.experimental.pallas import tpu as pltpu
from jax.sharding import PartitionSpec as P

H = 20


EPSILON = 1e-05


def shifted(block, axis, distance):
    devices = range(lax.axis_size(axis))
    route = [((i - distance) % len(devices), i) for i in devices]
    return lax.ppermute(block, axis, route)


def layer_norm(values, gain, shift):
    center = values - jnp.mean(values, axis=-1, keepdims=True)
    spread = jnp.mean(center * center, axis=-1, keepdims=True)
    return center * lax.rsqrt(spread + EPSILON) * gain + shift


def exact_gelu(values):
    return jax.nn.gelu(values, approximate=False)


def same_cells(query_cells, key_cells):
    return query_cells[:, :, None] == key_cells[:, None, :]


def forward_block(queries, key_part, value_part, query_cells, key_cells, totals, weights):
    scores = jnp.einsum("sqhd,skhd->shqk", queries, key_part, preferred_element_type=jnp.float32)
    exp_scores = jnp.where(same_cells(query_cells, key_cells)[:, None], jnp.exp(scores), 0.0)
    weights = weights + jnp.sum(exp_scores, axis=-1)
    totals = totals + jnp.einsum(
        "shqk,skhd->sqhd",
        exp_scores.astype(jnp.bfloat16),
        value_part,
        preferred_element_type=jnp.float32,
    )
    return (totals, weights)


def backward_block(queries, scaled, deltas, query_cells, key_part, value_part, key_cells):
    scores = jnp.einsum("sqhd,skhd->shqk", queries, key_part, preferred_element_type=jnp.float32)
    exp_scores = jnp.where(same_cells(query_cells, key_cells)[:, None], jnp.exp(scores), 0.0)
    grad_exp = jnp.einsum("sqhd,skhd->shqk", scaled, value_part, preferred_element_type=jnp.float32)
    grad_scores = (exp_scores * (grad_exp - deltas[..., None])).astype(jnp.bfloat16)
    grad_queries = jnp.einsum(
        "shqk,skhd->sqhd", grad_scores, key_part, preferred_element_type=jnp.float32
    )
    grad_keys = jnp.einsum(
        "shqk,sqhd->skhd", grad_scores, queries, preferred_element_type=jnp.float32
    )
    grad_values = jnp.einsum(
        "shqk,sqhd->skhd",
        exp_scores.astype(jnp.bfloat16),
        scaled,
        preferred_element_type=jnp.float32,
    )
    return (grad_queries, grad_keys, grad_values)


def on_device_general(
    tokens,
    first_gain,
    first_shift,
    w_qkv,
    w_out,
    second_gain,
    second_shift,
    w_in,
    w_down,
    segment_ids,
    cls_positions,
    out_grad,
):
    seqs_here, block_len, width = tokens.shape
    head_count = H
    head_size = width // head_count
    blocks = lax.axis_size("blk")
    head_shape = (seqs_here, block_len, head_count, head_size)
    flat_shape = (seqs_here, block_len, width)
    tokens_wide = tokens.astype(jnp.float32)
    normed_low = layer_norm(tokens_wide, first_gain, first_shift).astype(jnp.bfloat16)
    projected = jnp.dot(normed_low, w_qkv, preferred_element_type=jnp.float32)
    queries = (projected[..., :width] * 0.125).astype(jnp.bfloat16).reshape(head_shape)
    key_part = projected[..., width : 2 * width].astype(jnp.bfloat16).reshape(head_shape)
    value_part = projected[..., 2 * width :].astype(jnp.bfloat16).reshape(head_shape)
    totals = jnp.zeros(head_shape, jnp.float32)
    weights = jnp.zeros((seqs_here, head_count, block_len), jnp.float32)
    totals, weights = forward_block(
        queries, key_part, value_part, segment_ids, segment_ids, totals, weights
    )

    def forward_step(position, loop_state):
        moving, totals_in, weights_in = loop_state
        moving = shifted((moving[0], moving[1], moving[2]), "blk", 1)
        totals_out, weights_out = forward_block(
            queries, moving[0], moving[1], segment_ids, moving[2], totals_in, weights_in
        )
        return (moving, totals_out, weights_out)

    moved_state, totals, weights = lax.fori_loop(
        0, blocks - 1, forward_step, ((key_part, value_part, segment_ids), totals, weights)
    )
    weights_rows = jnp.swapaxes(weights, 1, 2)[..., None]
    attended = totals / weights_rows
    attended_low = attended.reshape(flat_shape).astype(jnp.bfloat16)
    residual = tokens_wide + jnp.dot(attended_low, w_out, preferred_element_type=jnp.float32)
    normed_two_low = layer_norm(residual, second_gain, second_shift).astype(jnp.bfloat16)
    hidden_pre = jnp.dot(normed_two_low, w_in, preferred_element_type=jnp.float32)
    hidden_low = exact_gelu(hidden_pre).astype(jnp.bfloat16)
    layer = residual + jnp.dot(hidden_low, w_down, preferred_element_type=jnp.float32)
    offset = lax.axis_index("blk") * block_len
    places = (
        lax.broadcasted_iota(jnp.int32, (seqs_here, cls_positions.shape[1], block_len), 2) + offset
    )
    chosen = jnp.sum((places == cls_positions[:, :, None]).astype(jnp.float32), axis=1)
    cell_sums = jnp.sum(chosen[..., None] * layer, axis=(0, 1))
    cell_squares = jnp.sum(chosen[..., None] * layer * layer, axis=(0, 1))
    count = cls_positions.shape[0] * cls_positions.shape[1] * lax.axis_size("dp")
    share = width // (lax.axis_size("dp") * blocks)
    moment_sums = lax.psum((cell_sums, cell_squares), ("dp", "blk"))
    rank = lax.axis_index("dp") * blocks + lax.axis_index("blk")
    sum_share = lax.dynamic_slice_in_dim(moment_sums[0], rank * share, share)
    square_share = lax.dynamic_slice_in_dim(moment_sums[1], rank * share, share)
    grad_layer = out_grad.astype(jnp.float32)
    grad_down = jnp.einsum("sbf,sbd->fd", hidden_low, out_grad, preferred_element_type=jnp.float32)
    grad_hidden = jnp.einsum("sbd,fd->sbf", out_grad, w_down, preferred_element_type=jnp.float32)
    grad_pre = jax.vjp(exact_gelu, hidden_pre)[1](grad_hidden)[0].astype(jnp.bfloat16)
    grad_in = jnp.einsum(
        "sbd,sbf->df", normed_two_low, grad_pre, preferred_element_type=jnp.float32
    )
    grad_normed_two = jnp.einsum("sbf,df->sbd", grad_pre, w_in, preferred_element_type=jnp.float32)
    unused_two, pull_two = jax.vjp(layer_norm, residual, second_gain, second_shift)
    residual_part, second_gain_grad, second_shift_grad = pull_two(grad_normed_two)
    grad_residual = grad_layer + residual_part
    grad_proj = grad_residual.astype(jnp.bfloat16)
    grad_out = jnp.einsum(
        "sbd,sbe->de", attended_low, grad_proj, preferred_element_type=jnp.float32
    )
    grad_attended = jnp.einsum(
        "sbe,de->sbd", grad_proj, w_out, preferred_element_type=jnp.float32
    ).reshape(head_shape)
    scaled = (grad_attended / weights_rows).astype(jnp.bfloat16)
    deltas = jnp.swapaxes(jnp.sum(grad_attended * attended, axis=-1), 1, 2) / weights

    def key_step(position, loop_state):
        moving, key_sums, query_sum = loop_state
        grad_queries, grad_keys, grad_values = backward_block(
            queries, scaled, deltas, segment_ids, moving[0], moving[1], moving[2]
        )
        query_next = query_sum + grad_queries
        keys_next = key_sums[0] + grad_keys
        values_next = key_sums[1] + grad_values
        moving = shifted((moving[0], moving[1], moving[2]), "blk", 1)
        key_sums = (
            shifted(keys_next.astype(jnp.bfloat16), "blk", 1).astype(keys_next.dtype),
            shifted(values_next.astype(jnp.bfloat16), "blk", 1).astype(values_next.dtype),
        )
        return (moving, key_sums, query_next)

    zero_heads = jnp.zeros(head_shape, jnp.float32)
    moved_back, key_sums, query_total = lax.fori_loop(
        0,
        blocks,
        key_step,
        ((key_part, value_part, segment_ids), (zero_heads, zero_heads), zero_heads),
    )
    keys_total, values_total = (key_sums[0], key_sums[1])
    grad_qkv_low = jnp.concatenate(
        [
            (query_total * 0.125).reshape(flat_shape),
            keys_total.reshape(flat_shape),
            values_total.reshape(flat_shape),
        ],
        axis=-1,
    ).astype(jnp.bfloat16)
    grad_qkv = jnp.einsum(
        "sbd,sbe->de", normed_low, grad_qkv_low, preferred_element_type=jnp.float32
    )
    grad_normed_one = jnp.einsum(
        "sbe,de->sbd", grad_qkv_low, w_qkv, preferred_element_type=jnp.float32
    )
    unused_one, pull_one = jax.vjp(layer_norm, tokens_wide, first_gain, first_shift)
    tokens_part, first_gain_grad, first_shift_grad = pull_one(grad_normed_one)
    tokens_grad = (grad_residual + tokens_part).astype(jnp.bfloat16)
    summed = (
        lax.psum_scatter(grad_qkv, ("dp", "blk"), scatter_dimension=0, tiled=True),
        lax.psum_scatter(grad_out, ("dp", "blk"), scatter_dimension=0, tiled=True),
        lax.psum_scatter(grad_in, ("dp", "blk"), scatter_dimension=0, tiled=True),
        lax.psum_scatter(grad_down, ("dp", "blk"), scatter_dimension=0, tiled=True),
        lax.psum_scatter(first_gain_grad, ("dp", "blk"), scatter_dimension=0, tiled=True),
        lax.psum_scatter(first_shift_grad, ("dp", "blk"), scatter_dimension=0, tiled=True),
        lax.psum_scatter(second_gain_grad, ("dp", "blk"), scatter_dimension=0, tiled=True),
        lax.psum_scatter(second_shift_grad, ("dp", "blk"), scatter_dimension=0, tiled=True),
    )
    cls_mean = sum_share / count
    cls_variance = square_share / count - cls_mean * cls_mean
    return (
        layer.astype(jnp.bfloat16),
        tokens_grad,
        summed[0],
        summed[1],
        summed[2],
        summed[3],
        summed[4],
        summed[5],
        summed[6],
        summed[7],
        cls_mean,
        cls_variance,
    )


MESH = pl.DeviceIdType.MESH
F32 = jnp.float32
BF16 = jnp.bfloat16
NN = (((1,), (0,)), ((), ()))
NT = (((1,), (1,)), ((), ()))
TN = (((0,), (0,)), ((), ()))


def mm(left, right, dims=NN):
    return lax.dot_general(left, right, dims, preferred_element_type=F32)


def remote(src, dst, send, recv, target):
    return pltpu.make_async_remote_copy(
        src_ref=src, dst_ref=dst, send_sem=send, recv_sem=recv, device_id=target, device_id_type=MESH
    )


def greet(targets):
    barrier = pltpu.get_barrier_semaphore()
    for target in targets:
        pl.semaphore_signal(barrier, inc=1, device_id=target, device_id_type=MESH)
    pl.semaphore_wait(barrier, len(targets))


def place():
    dp, blk = lax.axis_index("dp"), lax.axis_index("blk")
    return dp, blk, dp // 2, lax.rem(dp, 2), blk // 2, lax.rem(blk, 2)


def piece(index, size):
    return pl.ds(pl.multiple_of(index * size, size), size)


def flip(mine, other):
    return mine + other - 2 * mine * other


class RowGather:
    def __init__(self, rows, size, y, c, sibling, ypeer, send, recv, source=None):
        near, far = rows.at[y, piece(c, size)], rows.at[1 - y, piece(c, size)]
        source = near if source is None else source
        self.core = remote(source, near, send.at[0], recv.at[0], sibling)
        self.over = remote(source, near, send.at[1], recv.at[1], ypeer)
        self.last = remote(far, far, send.at[2], recv.at[2], sibling)

    def start(self):
        self.over.start()
        self.core.start()

    def forward(self):
        self.over.wait_recv()
        self.last.start()

    def arrive(self):
        self.core.wait_recv()
        self.last.wait_recv()

    def drain(self):
        for copy in (self.core, self.over, self.last):
            copy.wait_send()


class DpGather:
    def __init__(self, slots, z, x, blk, send, recv):
        self.slots, self.z, self.x, self.send, self.recv = slots, z, x, send, recv
        above, below = lax.rem(z + 1, 4), lax.rem(z + 3, 4)
        self.targets = ((2 * above + x, blk), (2 * below + x, blk), (2 * z + 1 - x, blk))

    def hop(self, kind, zz):
        slot = self.slots.at[self.x, zz]
        return remote(slot, slot, self.send.at[kind, zz], self.recv.at[self.x, zz], self.targets[kind])

    def up(self, zz):
        @pl.when(self.z < 3)
        def _():
            self.hop(0, zz).start()

        self.hop(2, zz).start()

    def down(self, zz):
        @pl.when(self.z > 0)
        def _():
            self.hop(1, zz).start()

    def start(self):
        self.up(self.z)
        self.down(self.z)

    def forward(self, step):
        below, above = self.z - step, self.z + step

        @pl.when(below >= 0)
        def _():
            self.hop(0, below).wait_recv()
            self.up(below)

        @pl.when(above <= 3)
        def _():
            self.hop(1, above).wait_recv()
            self.down(above)
            self.hop(2, above).start()

    def arrive(self, half):
        for k in range(2):
            slot = self.slots.at[1 - self.x, 2 * half + k]
            done = self.recv.at[1 - self.x, 2 * half + k]
            remote(slot, slot, self.send.at[2, k], done, self.targets[2]).wait_recv()

    def drain(self):
        for zz in range(4):
            self.hop(2, zz).wait_send()

            @pl.when((self.z < 3) & (zz <= self.z))
            def _():
                self.hop(0, zz).wait_send()

            @pl.when((self.z > 0) & (zz >= self.z))
            def _():
                self.hop(1, zz).wait_send()


def centered(values):
    center = values - jnp.mean(values, axis=-1, keepdims=True)
    spread = jnp.mean(center * center, axis=-1, keepdims=True)
    scale = lax.rsqrt(spread + EPSILON)
    return center * scale, scale


def norm_back(grad, unit, scale):
    return scale * (
        grad - jnp.mean(grad, axis=-1, keepdims=True) - unit * jnp.mean(grad * unit, axis=-1, keepdims=True)
    )


def half_of(pair, head):
    lanes = lax.broadcasted_iota(jnp.int32, pair.shape, 1) // 64
    return jnp.where(lanes == head, pair, jnp.zeros_like(pair))


def cells_at(cls_ref, places):
    found = jnp.zeros(places.shape, jnp.int32)
    for n in range(cls_ref.shape[1]):
        found = found + (places >= cls_ref[0, n]).astype(jnp.int32)
    return found


def same_cell(cls_ref, start, count, row_len):
    mine = lax.broadcasted_iota(jnp.int32, (count, 1), 0) + start
    other = lax.broadcasted_iota(jnp.int32, (1, row_len), 1)
    return cells_at(cls_ref, mine) == cells_at(cls_ref, other)


def gelu_parts(pre):
    cdf = 0.5 * (1.0 + lax.erf(pre * 0.7071067811865476))
    return cdf, cdf + pre * (0.3989422804014327 * jnp.exp(-0.5 * pre * pre))


def as_row(ref):
    return ref[...].reshape(1, ref.shape[0])


def layer_kernel(
    cls_ref, tok_hbm, grad_hbm, gain1_ref, shift1_ref, gain2_ref, shift2_ref, wqkv_ref, wout_ref, win_ref, wdown_ref,
    layer_out, tgrad_out, gqkv_out, gout_out, in_out, down_out, sums_ref,
    gg, rows_all, qkv_ref, att_ref, turned_ref, aturned_ref, attlow, abox, arow,
    layer_ref, tgrad_ref, gqkv_ref, gout_ref, in_ref, down_ref,
    st_in, st_dn, wi, wd, wo, gx, gp, ht, part_in, part_dn, sib_in, sib_dn, ysend_in, ysend_dn, yrecv_in, yrecv_dn,
    slab, slab_in, residual, unit, gnorm, grow, gatt, low, keys, values, part, xin, zout, zin, zlast, zfirst, hfirst, xfirst, full, fin, landing,
    sums, sbuf, sbox, tbox,
    isem, lsem, rsend, rrecv, ogsend, ogrecv, bsend, brecv, arsend, arrecv, outsem,
    wsem, ssem, osem, gsend, grecv, dsend, drecv, sibs, sibr, ysend, yrecv, qsend, qrecv,
    xsend, xrecv, zsend, zrecv, fsend, frecv, asend, arecv, usend, urecv, tsend, trecv,
):
    dp, blk, z, x, y, c = place()
    tokens, width = tok_hbm.shape
    row_len, both = 4 * tokens, 2 * tokens
    first, pairs = 5 * y + 3 * c, 3 - c
    cut, owned, rows = wi.shape[1], down_ref.shape[0], in_ref.shape[0]
    share = width // 8
    block = st_in.shape[2]
    steps = win_ref.shape[1] // block
    depth = st_in.shape[0]
    sibling, ypeer, diag = (dp, 2 * y + 1 - c), (dp, 2 * (1 - y) + c), (dp, 2 * (1 - y) + 1 - c)
    xpeer = (2 * z + 1 - x, blk)
    others = ((1, sibling), (2, ypeer), (3, diag))
    received = ((1, sibling, 2 + c), (2, ypeer, pairs), (3, diag, 2 + c))

    tok_in = pltpu.make_async_copy(tok_hbm, rows_all.at[y, piece(c, tokens), :], isem.at[0])
    grad_in = pltpu.make_async_copy(grad_hbm, gg.at[x, z], isem.at[1])
    tok_in.start()
    grad_in.start()

    def load(j, t):
        source = wqkv_ref.at[:, pl.ds(pl.multiple_of(t * width + (first + j) * 128, 128), 128)]
        return pltpu.make_async_copy(source, st_in.at[j, :, pl.ds(t * 128, 128)], lsem.at[j, t])

    @pl.loop(0, pairs)
    def _(j):
        for t in range(3):
            load(j, t).start()

    def stream_in(i):
        slot = lax.rem(i, depth)
        return pltpu.make_async_copy(win_ref.at[:, piece(i, block)], st_in.at[slot], ssem.at[0, slot])

    def stream_dn(i):
        slot = lax.rem(i, depth)
        return pltpu.make_async_copy(wdown_ref.at[piece(i, block), :], st_dn.at[slot], ssem.at[1, slot])

    tails = ((0, block), (1, block), (2, width - 2 * block))

    def load_out(i, size):
        return pltpu.make_async_copy(
            wout_ref.at[pl.ds(i * block, size), :], st_dn.at[i, pl.ds(0, size), :], ssem.at[1, i]
        )

    def load_rows(j):
        return pltpu.make_async_copy(wout_ref.at[piece(first + j, 128), :], wo.at[j], osem.at[j])

    greet([sibling, ypeer, diag] + [(lax.rem(dp + k, 8), blk) for k in range(1, 8)])
    row_tok = RowGather(rows_all, tokens, y, c, sibling, ypeer, rsend, rrecv, tok_hbm)
    grads = DpGather(gg, z, x, blk, ogsend, ogrecv)
    row_tok.start()
    tok_in.wait()
    grad_in.wait()
    grads.start()
    for i, size in tails:
        load_out(i, size).start()

    @pl.loop(0, pairs)
    def _(j):
        load_rows(j).start()
        for t in range(3):
            load(j, t).wait()

    normed_rows = wd

    @pl.loop(0, 2)
    def _(step):
        @pl.when(step == 0)
        def _():
            row_tok.core.wait_recv()

        @pl.when(step == 1)
        def _():
            row_tok.forward()
            row_tok.last.wait_recv()
            grads.forward(1)

        chip = flip(y, step)
        at = piece(chip, both)
        normed_rows[at, :] = (centered(rows_all[chip].astype(F32))[0] * as_row(gain1_ref) + as_row(shift1_ref)).astype(BF16)

        @pl.loop(0, pairs)
        def _(j):
            made = mm(normed_rows[at, :], st_in[j, :, 0:384])
            qkv_ref[j, at, 0:128] = (made[:, 0:128] * 0.125).astype(BF16)
            qkv_ref[j, at, 128:384] = made[:, 128:384].astype(BF16)

    for i in range(depth - 1):
        stream_in(i).start()

    def to_own(j, r, target):
        return remote(attlow.at[j, piece(target[1], tokens), :], abox.at[r, j], bsend.at[r, j], brecv.at[r, j], target)

    @pl.loop(0, pairs)
    def _(j):
        @pl.loop(0, 2)
        def _(part):
            at = piece(part, both)
            same = same_cell(cls_ref, part * both, both, row_len)
            pair = jnp.zeros((both, 128), F32)
            for head in range(2):
                scores = mm(half_of(qkv_ref[j, at, 0:128], head), qkv_ref[j, :, 128:256], NT)
                weigh = jnp.where(same, jnp.exp(scores), 0.0)
                total = jnp.sum(weigh, axis=-1, keepdims=True)
                pair = pair + half_of(mm(weigh.astype(BF16), qkv_ref[j, :, 256:384]) / total, head)
            att_ref[j, at, :] = pair
            attlow[j, at, :] = pair.astype(BF16)

        for r, target in others:
            to_own(j, r, target).start()
        abox[0, j] = attlow[j, piece(blk, tokens), :]

        @pl.when(j == 1)
        def _():
            grads.forward(2)

    for b in range(4):
        at = slice(b * tokens, (b + 1) * tokens)
        turned_ref[:, at] = normed_rows[at, :].T

    for r, target, count in received:

        @pl.loop(0, count)
        def _(j):
            to_own(j, r, target).wait_recv()

    own_at = (y, piece(c, tokens))
    for p in range(10):
        yy, cc = p // 5, (p % 5) // 3
        slot = 2 * flip(y, yy) + flip(c, cc)
        arow[y, piece(c, tokens), 128 * p : 128 * p + 128] = abox[slot, p % 5 - 3 * cc]
    row_att = RowGather(arow, tokens, y, c, sibling, ypeer, arsend, arrecv)

    made = rows_all[y, piece(c, tokens), :].astype(F32)
    for i, size in tails:
        load_out(i, size).wait()
        made = made + mm(arow[y, piece(c, tokens), i * block : i * block + size], st_dn[i, :size, :])
    for i in range(depth - 1):
        stream_dn(i).start()
    residual[...] = made
    made, scale2 = centered(made)
    unit[...] = made
    gx[x, z] = (made * as_row(gain2_ref) + as_row(shift2_ref)).astype(BF16)
    normed = DpGather(gx, z, x, blk, dsend, drecv)
    normed.start()
    row_att.start()
    gnorm[...] = jnp.zeros_like(gnorm)

    @pl.loop(0, steps)
    def _(i):
        slot = lax.rem(i, depth)

        @pl.when(i + depth - 1 < steps)
        def _():
            stream_in(i + depth - 1).start()
            stream_dn(i + depth - 1).start()

        stream_in(i).wait()
        stream_dn(i).wait()
        pre = mm(gx[x, z], st_in[slot])
        cdf, slope = gelu_parts(pre)
        grad = (mm(gg[x, z], st_dn[slot], NT) * slope).astype(BF16)
        residual[...] += mm((pre * cdf).astype(BF16), st_dn[slot])
        gnorm[...] += mm(grad, st_in[slot], NT)

        @pl.when(i == 2)
        def _():
            grads.forward(3)

        @pl.when(i == 6)
        def _():
            row_att.forward()
            normed.forward(1)

    load_in = pltpu.make_async_copy(win_ref.at[:, piece(dp, cut)], wi, wsem.at[0])
    load_dn = pltpu.make_async_copy(wdown_ref.at[piece(dp, cut), :], wd, wsem.at[1])
    load_in.start()
    load_dn.start()
    layer = residual[...]
    layer_ref[...] = layer.astype(BF16)
    outs = [pltpu.make_async_copy(layer_ref, layer_out, outsem.at[0])]
    outs[0].start()
    sums[...] = jnp.zeros_like(sums)
    spots = lax.broadcasted_iota(jnp.int32, (tokens, 1), 0) + blk * tokens
    chosen = jnp.zeros((tokens, 1), F32)
    for n in range(cls_ref.shape[1]):
        chosen = chosen + (spots == cls_ref[0, n]).astype(F32)
    sums[4:5, :] = jnp.sum(chosen * layer, axis=0, keepdims=True)
    sums[5:6, :] = jnp.sum(chosen * layer * layer, axis=0, keepdims=True)
    grad = gnorm[...]
    sums[2:3, :] = jnp.sum(grad * unit[...], axis=0, keepdims=True)
    sums[3:4, :] = jnp.sum(grad, axis=0, keepdims=True)
    made = gg[x, z].astype(F32) + norm_back(grad * as_row(gain2_ref), unit[...], scale2)
    residual[...] = made
    grow[y, piece(c, tokens), :] = made.astype(BF16)
    row = RowGather(grow, tokens, y, c, sibling, ypeer, gsend, grecv)
    row.start()
    normed.forward(2)
    load_in.wait()
    load_dn.wait()

    def stream_qkv(p, t):
        slot = lax.rem(p, depth)
        source = wqkv_ref.at[:, pl.ds(pl.multiple_of(t * width + p * 128, 128), 128)]
        return pltpu.make_async_copy(source, st_in.at[slot, :, pl.ds(t * 128, 128)], wsem.at[2 + 3 * slot + t])

    for p in range(depth):
        for t in range(3):
            stream_qkv(p, t).start()
    near = z // 2

    def make(xx, half):
        at = piece(2 * xx + half, both)
        pre = mm(gx[xx, piece(half, 2)].reshape(both, width), wi[...])
        cdf, slope = gelu_parts(pre)
        ht[:, at] = (pre * cdf).astype(BF16).T
        gp[at, :] = (mm(gg[xx, piece(half, 2)].reshape(both, width), wd[...], NT) * slope).astype(BF16)

    def makes(first_step, last_step):
        @pl.loop(first_step, last_step)
        def _(step):
            make(flip(x, lax.rem(step, 2)), flip(near, step // 2))

    makes(0, 1)
    row_att.arrive()
    for b in range(4):
        aturned_ref[:, b * tokens : (b + 1) * tokens] = arow[b // 2, (b % 2) * tokens : (b % 2 + 1) * tokens, :].T
    row.forward()
    row.arrive()

    @pl.loop(0, pairs)
    def _(j):
        load_rows(j).wait()
        gatt[j] = mm(grow[...].reshape(row_len, width), wo[j], NT)

    even, pair_z, half_z = lax.rem(z, 2), z + 1 - 2 * lax.rem(z, 2), lax.rem(z + 2, 4)

    def to_x(s):
        return remote(part.at[s, 1 - x], xin.at[s - 1], xsend.at[s], xrecv.at[s], xpeer)

    def to_pair(s):
        return remote(zout.at[s - 1, 1 - even], zin.at[s - 1], zsend.at[s, 0], zrecv.at[s, 0], (2 * pair_z + x, blk))

    def to_half(s):
        return remote(zlast.at[s - 1, 0], zlast.at[s - 1, 1], zsend.at[s, 1], zrecv.at[s, 1], (2 * half_z + x, blk))

    other_half, my_half = 1 - z // 2, z // 2
    first_pair = remote(part.at[0, :, 1 - even], zfirst, zsend.at[0, 0], zrecv.at[0, 0], (2 * pair_z + x, blk))
    first_half = remote(hfirst.at[0], hfirst.at[1], zsend.at[0, 1], zrecv.at[0, 1], (2 * half_z + x, blk))
    first_x = remote(xfirst.at[0], xfirst.at[1], xsend.at[0], xrecv.at[0], xpeer)

    def to_blk(s, r, target):
        return remote(full.at[s, target[1]], fin.at[r, s], fsend.at[r, s], frecv.at[r, s], target)

    def to_low(j, r, target):
        return remote(low.at[j, piece(target[1], tokens), :], landing.at[r, j], asend.at[r, j], arecv.at[r, j], target)

    def add_x(s):
        to_x(s).wait()
        for k in range(4):
            zout[s - 1, k // 2, k % 2] = (part[s, x, k // 2, k % 2].astype(F32) + xin[s - 1, k // 2, k % 2].astype(F32)).astype(BF16)
        to_pair(s).start()

    def add_pair(s):
        to_pair(s).wait()
        away = 1 - z // 2
        zlast[s - 1, 0] = (zout[s - 1, even, away].astype(F32) + zin[s - 1, away].astype(F32)).astype(BF16)
        to_half(s).start()

    def add_half(s):
        to_half(s).wait()
        mine = z // 2
        total = zout[s - 1, even, mine].astype(F32) + zin[s - 1, mine].astype(F32) + zlast[s - 1, 1].astype(F32)
        to_owners(s, total)

    def to_owners(s, total):
        for b in range(4):
            full[s, b] = total[b * rows : (b + 1) * rows].astype(BF16)
        for r, target in others:
            to_blk(s, r, target).start()
        fin[0, s] = full[s, blk]

    def first_a():
        first_pair.wait()
        for xx in range(2):
            hfirst[0, xx] = (part[0, xx, even, other_half].astype(F32) + zfirst[xx, other_half].astype(F32)).astype(BF16)
        first_half.start()

    def first_sum(xx):
        return part[0, xx, even, my_half].astype(F32) + zfirst[xx, my_half].astype(F32) + hfirst[1, xx].astype(F32)

    def first_b():
        first_half.wait()
        xfirst[0] = first_sum(1 - x).astype(BF16)
        first_x.start()

    def first_c():
        first_x.wait()
        to_owners(0, first_sum(x) + xfirst[1].astype(F32))

    def weight_part(s, left, right):
        @pl.loop(0, 4)
        def _(zz):
            made = mm(left[piece(zz, 2 * share), :], right)
            part[s, 0, lax.rem(zz, 2), zz // 2] = made[:share].astype(BF16)
            part[s, 1, lax.rem(zz, 2), zz // 2] = made[share:].astype(BF16)

    @pl.when(c == 0)
    def _():
        weight_part(0, aturned_ref, grow[:, :, pl.ds(pl.multiple_of(first * 128, 128), 384)].reshape(row_len, 384))

    @pl.when(c == 1)
    def _():
        right = grow[:, :, pl.ds(pl.multiple_of(first * 128, 128), 256)].reshape(row_len, 256)
        weight_part(0, aturned_ref, jnp.concatenate([right, jnp.zeros((row_len, 128), BF16)], axis=1))

    first_pair.start()
    normed.forward(3)
    to_sibling = []
    for kind, source, box in ((0, part_in, sib_in), (1, part_dn, sib_dn)):
        for yy in range(2):
            away = source.at[2 * yy + (1 - c)]
            to_sibling.append(remote(away, box.at[yy], sibs.at[kind, yy], sibr.at[kind, yy], sibling))
    to_y = (
        remote(ysend_in, yrecv_in, ysend.at[0], yrecv.at[0], ypeer),
        remote(ysend_dn, yrecv_dn, ysend.at[1], yrecv.at[1], ypeer),
    )

    over = 2 * (1 - y) + c

    @pl.loop(0, pairs)
    def _(j):
        keys[...] = jnp.zeros_like(keys)
        values[...] = jnp.zeros_like(values)

        @pl.loop(0, 2)
        def _(half):
            at = piece(half, both)
            same = same_cell(cls_ref, half * both, both, row_len)
            queries_grad = jnp.zeros((both, 128), F32)
            for head in range(2):
                query = half_of(qkv_ref[j, at, 0:128], head)
                key = half_of(qkv_ref[j, :, 128:256], head)
                grad = half_of(gatt[j, at, :], head)
                weigh = jnp.where(same, jnp.exp(mm(query, key, NT)), 0.0)
                total = jnp.sum(weigh, axis=-1, keepdims=True)
                scaled = (grad / total).astype(BF16)
                delta = jnp.sum(grad * att_ref[j, at, :], axis=-1, keepdims=True) / total
                spread = mm(scaled, qkv_ref[j, :, 256:384], NT)
                score = (weigh * (spread - delta)).astype(BF16)
                queries_grad = queries_grad + mm(score, key)
                keys[...] += mm(score, query, TN)
                values[...] += mm(weigh.astype(BF16), scaled, TN)
            low[j, at, 0:128] = (queries_grad * 0.125).astype(BF16)

        low[j, :, 128:256] = keys[...].astype(BF16)
        low[j, :, 256:384] = values[...].astype(BF16)
        for r, target in others:
            to_low(j, r, target).start()
        weight_part(j + 1, turned_ref, low[j])

        @pl.when(j == 0)
        def _():
            to_x(1).start()

        @pl.when(j == pairs - 1)
        def _():
            for half in range(2):
                normed.arrive(half)
                grads.arrive(half)
            to_x(2).start()

            @pl.when(c == 0)
            def _():
                to_x(3).start()

            makes(1, 4)
            first_a()

            @pl.loop(0, 2)
            def _(half):
                left = gx[:, :, :, piece(half, width // 2)].reshape(8 * tokens, width // 2)
                made = mm(left, gp[...], TN)
                for n in range(4):
                    for q in range(4):
                        at = n * share + q * rows
                        part_in[q, 4 * half + n] = made[at : at + rows].astype(BF16)

            to_sibling[0].start()
            to_sibling[1].start()
            every = gg[...].reshape(8 * tokens, width)

            @pl.loop(0, 4)
            def _(q):
                part_dn[q] = mm(ht[piece(q, owned), :], every).astype(BF16)

            to_sibling[2].start()
            to_sibling[3].start()
            to_sibling[0].wait()
            to_sibling[1].wait()
            ysend_in[...] = (part_in[over].astype(F32) + sib_in[1 - y].astype(F32)).astype(BF16)
            to_y[0].start()
            to_sibling[2].wait()
            to_sibling[3].wait()
            ysend_dn[...] = (part_dn[over].astype(F32) + sib_dn[1 - y].astype(F32)).astype(BF16)
            first_b()
            add_x(1)

    add_x(2)
    add_pair(1)

    mine = 2 * y + c
    to_q = []
    for k in range(1, 8):
        target = lax.rem(dp + k, 8)
        to_q.append(remote(slab.at[target], slab_in.at[dp], qsend.at[k], qrecv.at[k], (target, blk)))

    def start_q():
        to_y[0].wait()
        to_y[1].start()
        total = part_in[mine].astype(F32) + sib_in[y].astype(F32) + yrecv_in[...].astype(F32)
        slab[...] = total.astype(BF16)
        for copy in to_q:
            copy.start()
        slab_in[dp] = slab[dp]

    start_q()
    @pl.when(c == 0)
    def _():
        add_x(3)

    first_c()

    @pl.loop(0, pairs)
    def _(j):
        landing[0, j] = low[j, piece(blk, tokens), :]
        for r, target in others:
            to_low(j, r, target).wait_send()

    for r, target, count in received:

        @pl.loop(0, count)
        def _(j):
            to_low(j, r, target).wait_recv()

    gnorm[...] = jnp.zeros_like(gnorm)
    @pl.loop(0, 10)
    def _(p):
        @pl.when((p > 0) & (p + depth - 1 < 10))
        def _():
            for t in range(3):
                stream_qkv(p + depth - 1, t).start()

        for t in range(3):
            stream_qkv(p, t).wait()
        yy, pp = p // 5, lax.rem(p, 5)
        cc = pp // 3
        slot = 2 * flip(y, yy) + flip(c, cc)
        gnorm[...] += mm(landing[slot, pp - 3 * cc], st_in[lax.rem(p, depth), :, 0:384], NT)

    grad = gnorm[...]
    made, scale1 = centered(rows_all[y, piece(c, tokens), :].astype(F32))
    sums[0:1, :] = jnp.sum(grad * made, axis=0, keepdims=True)
    sums[1:2, :] = jnp.sum(grad, axis=0, keepdims=True)
    sbuf[...] = jnp.zeros_like(sbuf)
    for k in range(8):
        sbuf[k, :, 0:share] = sums[:, k * share : (k + 1) * share]
    to_u = []
    for k in range(1, 8):
        target = lax.rem(dp + k, 8)
        to_u.append(remote(sbuf.at[target], sbox.at[dp], usend.at[k], urecv.at[k], (target, blk)))
        to_u[-1].start()
    sbox[dp] = sbuf[dp]
    tgrad_ref[...] = (residual[...] + norm_back(grad * as_row(gain1_ref), made, scale1)).astype(BF16)
    outs.append(pltpu.make_async_copy(tgrad_ref, tgrad_out, outsem.at[1]))
    outs[-1].start()

    def end_down():
        to_y[1].wait()
        down_ref[...] = part_dn[mine].astype(F32) + sib_dn[y].astype(F32) + yrecv_dn[...].astype(F32)
        outs.append(pltpu.make_async_copy(down_ref, down_out, outsem.at[2]))
        outs[-1].start()

    def end_q():
        for copy in to_q:
            copy.wait()
        for s in range(8):
            in_ref[:, s * cut : (s + 1) * cut] = slab_in[s].astype(F32)
        outs.append(pltpu.make_async_copy(in_ref, in_out, outsem.at[3]))
        outs[-1].start()

    to_t = [remote(tbox.at[0], tbox.at[r], tsend.at[r], trecv.at[r], target) for r, target in others]

    def start_t():
        for copy in to_u:
            copy.wait()
        tbox[0] = jnp.sum(sbox[...], axis=0)
        for copy in to_t:
            copy.start()

    def end_t():
        for copy in to_t:
            copy.wait()
        total = (tbox[0] + tbox[1]) + (tbox[2] + tbox[3])
        for b in range(4):

            @pl.when(blk == b)
            def _():
                sums_ref[...] = total[:, b * rows : (b + 1) * rows]

    add_pair(2)
    add_half(1)

    @pl.when(c == 0)
    def _():
        add_pair(3)

    start_t()
    add_half(2)

    @pl.when(c == 0)
    def _():
        add_half(3)

    end_down()
    end_t()
    end_q()

    @pl.loop(0, pairs + 1)
    def _(s):
        for r, target in others:
            to_blk(s, r, target).wait_send()

    for r, target, count in received:

        @pl.loop(0, count + 1)
        def _(s):
            to_blk(s, r, target).wait_recv()

    for yy in range(2):
        for cc in range(2):
            slot = 2 * flip(y, yy) + flip(c, cc)
            p = 5 * yy + 3 * cc
            wide = 128 * (3 - cc)
            gout_ref[:, 128 * p : 128 * p + wide] = fin[slot, 0, :, :wide].astype(F32)
            for j in range(3 - cc):
                for t in range(3):
                    at = t * width + 128 * (p + j)
                    gqkv_ref[:, at : at + 128] = fin[slot, j + 1, :, 128 * t : 128 * t + 128].astype(F32)
    outs.append(pltpu.make_async_copy(gqkv_ref, gqkv_out, outsem.at[4]))
    outs[-1].start()
    outs.append(pltpu.make_async_copy(gout_ref, gout_out, outsem.at[5]))
    outs[-1].start()

    @pl.loop(0, pairs)
    def _(j):
        for r, target in others:
            to_own(j, r, target).wait_send()

    for gather in (row_tok, row_att, row, grads, normed):
        gather.drain()
    for copy in outs:
        copy.wait()


def finish_kernel(cells, sums_ref, *refs):
    count = 6
    arrays, (mean_ref, variance_ref, *grads), outs = refs[:count], refs[count : count + 6], refs[count + 6 : 2 * count + 6]
    held, isem, osem = refs[2 * count + 6 : -2], refs[-2], refs[-1]
    loads = [pltpu.make_async_copy(arrays[i], held[i], isem.at[i]) for i in range(count)]
    stores = [pltpu.make_async_copy(held[i], outs[i], osem.at[i]) for i in range(count)]
    for load in loads:
        load.start()
    for load, store in zip(loads, stores):
        load.wait()
        store.start()
    mean = sums_ref[4:5, :] / cells
    mean_ref[...] = mean
    variance_ref[...] = sums_ref[5:6, :] / cells - mean * mean
    for i in range(4):
        grads[i][...] = sums_ref[i : i + 1, :]
    for store in stores:
        store.wait()


def finish(cells, sums, *arrays):
    anywhere, v = pl.BlockSpec(memory_space=pl.ANY), pl.BlockSpec(memory_space=pltpu.VMEM)
    count = len(arrays)
    small = jax.ShapeDtypeStruct((1, sums.shape[1]), F32)
    return pl.pallas_call(
        functools.partial(finish_kernel, cells),
        out_shape=(small,) * 6 + tuple(jax.ShapeDtypeStruct(a.shape, a.dtype) for a in arrays),
        in_specs=[v] + [anywhere] * count,
        out_specs=(v,) * 6 + (anywhere,) * count,
        scratch_shapes=[pltpu.VMEM(a.shape, a.dtype) for a in arrays]
        + [pltpu.SemaphoreType.DMA((count,)), pltpu.SemaphoreType.DMA((count,))],
    )(sums, *arrays)


def whole_layer(cls_positions, tokens, grad, gain1, shift1, gain2, shift2, w_qkv, w_out, w_in, w_down):
    count, width = tokens.shape
    inner = w_in.shape[1]
    row_len, share = 4 * count, width // 8
    cut, owned, rows = inner // 8, inner // 32, width // 32
    block, depth = 512, 3
    v = pltpu.VMEM
    dma = pltpu.SemaphoreType.DMA
    anywhere = pl.BlockSpec(memory_space=pl.ANY)
    return pl.pallas_call(
        layer_kernel,
        out_shape=(
            jax.ShapeDtypeStruct((count, width), BF16),
            jax.ShapeDtypeStruct((count, width), BF16),
            jax.ShapeDtypeStruct((rows, 3 * width), F32),
            jax.ShapeDtypeStruct((rows, width), F32),
            jax.ShapeDtypeStruct((rows, inner), F32),
            jax.ShapeDtypeStruct((owned, width), F32),
            jax.ShapeDtypeStruct((8, rows), F32),
        ),
        in_specs=[pl.BlockSpec(memory_space=pltpu.SMEM)]
        + [anywhere] * 2
        + [pl.BlockSpec(memory_space=v)] * 4
        + [anywhere] * 4,
        out_specs=(anywhere,) * 6 + (pl.BlockSpec(memory_space=v),),
        scratch_shapes=[
            v((2, 4, count, width), BF16), v((2, 2 * count, width), BF16),
            v((3, row_len, 384), BF16), v((3, row_len, 128), F32), v((width, row_len), BF16), v((width, row_len), BF16),
            v((3, row_len, 128), BF16), v((4, 3, count, 128), BF16), v((2, 2 * count, width), BF16),
            v((count, width), BF16), v((count, width), BF16), v((rows, 3 * width), F32), v((rows, width), F32),
            v((rows, inner), F32), v((owned, width), F32),
            v((depth, width, block), BF16), v((depth, block, width), BF16),
            v((width, cut), BF16), v((cut, width), BF16), v((3, 128, width), BF16),
            v((2, 4, count, width), BF16), v((8 * count, cut), BF16), v((cut, 8 * count), BF16),
            v((4, 8, rows, cut), BF16), v((4, owned, width), BF16),
            v((2, 8, rows, cut), BF16), v((2, owned, width), BF16),
            v((8, rows, cut), BF16), v((owned, width), BF16), v((8, rows, cut), BF16), v((owned, width), BF16),
            v((8, rows, cut), BF16), v((8, rows, cut), BF16),
            v((count, width), F32), v((count, width), F32), v((count, width), F32),
            v((2, 2 * count, width), BF16), v((3, row_len, 128), F32), v((3, row_len, 384), BF16),
            v((row_len, 128), F32), v((row_len, 128), F32),
            v((4, 2, 2, 2, share, 384), BF16), v((3, 2, 2, share, 384), BF16), v((3, 2, 2, share, 384), BF16),
            v((3, 2, share, 384), BF16), v((3, 2, share, 384), BF16),
            v((2, 2, share, 384), BF16), v((2, 2, share, 384), BF16), v((2, share, 384), BF16),
            v((4, 4, share // 4, 384), BF16), v((4, 4, share // 4, 384), BF16),
            v((4, 3, count, 384), BF16),
            v((8, width), F32), v((8, 8, 256), F32), v((8, 8, 256), F32), v((4, 8, 256), F32),
            dma((2,)), dma((3, 3)), dma((3,)), dma((3,)), dma((3, 4)), dma((2, 4)), dma((4, 3)), dma((4, 3)),
            dma((3,)), dma((3,)), dma((6,)),
            dma((2 + 3 * depth,)), dma((2, depth)), dma((3,)), dma((3,)), dma((3,)), dma((3, 4)), dma((2, 4)),
            dma((2, 2)), dma((2, 2)), dma((2,)), dma((2,)), dma((8,)), dma((8,)),
            dma((4,)), dma((4,)), dma((4, 3)), dma((4, 3)), dma((4, 4)), dma((4, 4)), dma((4, 3)), dma((4, 3)),
            dma((8,)), dma((8,)), dma((4,)), dma((4,)),
        ],
        compiler_params=pltpu.CompilerParams(collective_id=1, has_side_effects=True, vmem_limit_bytes=64 * 2**20),
        cost_estimate=pl.CostEstimate(flops=40 * 2**30, bytes_accessed=50 * 2**20, transcendentals=0),
    )(cls_positions, tokens, grad, gain1, shift1, gain2, shift2, w_qkv, w_out, w_in, w_down)


def on_device(
    tokens,
    first_gain,
    first_shift,
    w_qkv,
    w_out,
    second_gain,
    second_shift,
    w_in,
    w_down,
    segment_ids,
    cls_positions,
    out_grad,
):
    tokens, out_grad = tokens[0], out_grad[0]
    layer, tokens_grad, grad_qkv, grad_out, grad_in, grad_down, sums = whole_layer(
        cls_positions, tokens, out_grad, first_gain, first_shift, second_gain, second_shift, w_qkv, w_out, w_in, w_down
    )
    mean, variance, gain1_grad, shift1_grad, gain2_grad, shift2_grad, *large = finish(
        cls_positions.size * lax.axis_size("dp"), sums, layer, tokens_grad, grad_qkv, grad_out, grad_in, grad_down
    )
    return (
        large[0][None],
        large[1][None],
        *large[2:],
        gain1_grad[0],
        shift1_grad[0],
        gain2_grad[0],
        shift2_grad[0],
        mean[0],
        variance[0],
    )


def solution(mesh):
    placed = (
        P("dp", "blk", None),
        P(),
        P(),
        P(),
        P(),
        P(),
        P(),
        P(),
        P(),
        P("dp", "blk"),
        P("dp", None),
        P("dp", "blk", None),
    )
    small = mesh.shape["dp"] == 8 and mesh.shape["blk"] == 4
    return jax.shard_map(
        on_device if small else on_device_general,
        mesh=mesh,
        in_specs=placed,
        out_specs=(
            P("dp", "blk", None),
            P("dp", "blk", None),
            P(("dp", "blk"), None),
            P(("dp", "blk"), None),
            P(("dp", "blk"), None),
            P(("dp", "blk"), None),
            P(("dp", "blk")),
            P(("dp", "blk")),
            P(("dp", "blk")),
            P(("dp", "blk")),
            P(("dp", "blk")),
            P(("dp", "blk")),
        ),
        check_vma=False,
    )
```

```python
import functools

import jax
import jax.numpy as jnp
from jax import lax
from jax.experimental import pallas as pl
from jax.experimental.pallas import tpu as pltpu
from jax.sharding import PartitionSpec as P

H = 20


EPSILON = 1e-05


def shifted(block, axis, distance):
    devices = range(lax.axis_size(axis))
    route = [((i - distance) % len(devices), i) for i in devices]
    return lax.ppermute(block, axis, route)


def layer_norm(values, gain, shift):
    center = values - jnp.mean(values, axis=-1, keepdims=True)
    spread = jnp.mean(center * center, axis=-1, keepdims=True)
    return center * lax.rsqrt(spread + EPSILON) * gain + shift


def exact_gelu(values):
    return jax.nn.gelu(values, approximate=False)


def same_cells(query_cells, key_cells):
    return query_cells[:, :, None] == key_cells[:, None, :]


def forward_block(queries, key_part, value_part, query_cells, key_cells, totals, weights):
    scores = jnp.einsum("sqhd,skhd->shqk", queries, key_part, preferred_element_type=jnp.float32)
    exp_scores = jnp.where(same_cells(query_cells, key_cells)[:, None], jnp.exp(scores), 0.0)
    weights = weights + jnp.sum(exp_scores, axis=-1)
    totals = totals + jnp.einsum(
        "shqk,skhd->sqhd",
        exp_scores.astype(jnp.bfloat16),
        value_part,
        preferred_element_type=jnp.float32,
    )
    return (totals, weights)


def backward_block(queries, scaled, deltas, query_cells, key_part, value_part, key_cells):
    scores = jnp.einsum("sqhd,skhd->shqk", queries, key_part, preferred_element_type=jnp.float32)
    exp_scores = jnp.where(same_cells(query_cells, key_cells)[:, None], jnp.exp(scores), 0.0)
    grad_exp = jnp.einsum("sqhd,skhd->shqk", scaled, value_part, preferred_element_type=jnp.float32)
    grad_scores = (exp_scores * (grad_exp - deltas[..., None])).astype(jnp.bfloat16)
    grad_queries = jnp.einsum(
        "shqk,skhd->sqhd", grad_scores, key_part, preferred_element_type=jnp.float32
    )
    grad_keys = jnp.einsum(
        "shqk,sqhd->skhd", grad_scores, queries, preferred_element_type=jnp.float32
    )
    grad_values = jnp.einsum(
        "shqk,sqhd->skhd",
        exp_scores.astype(jnp.bfloat16),
        scaled,
        preferred_element_type=jnp.float32,
    )
    return (grad_queries, grad_keys, grad_values)


def on_device_general(
    tokens,
    first_gain,
    first_shift,
    w_qkv,
    w_out,
    second_gain,
    second_shift,
    w_in,
    w_down,
    segment_ids,
    cls_positions,
    out_grad,
):
    seqs_here, block_len, width = tokens.shape
    head_count = H
    head_size = width // head_count
    blocks = lax.axis_size("blk")
    head_shape = (seqs_here, block_len, head_count, head_size)
    flat_shape = (seqs_here, block_len, width)
    tokens_wide = tokens.astype(jnp.float32)
    normed_low = layer_norm(tokens_wide, first_gain, first_shift).astype(jnp.bfloat16)
    projected = jnp.dot(normed_low, w_qkv, preferred_element_type=jnp.float32)
    queries = (projected[..., :width] * 0.125).astype(jnp.bfloat16).reshape(head_shape)
    key_part = projected[..., width : 2 * width].astype(jnp.bfloat16).reshape(head_shape)
    value_part = projected[..., 2 * width :].astype(jnp.bfloat16).reshape(head_shape)
    totals = jnp.zeros(head_shape, jnp.float32)
    weights = jnp.zeros((seqs_here, head_count, block_len), jnp.float32)
    totals, weights = forward_block(
        queries, key_part, value_part, segment_ids, segment_ids, totals, weights
    )

    def forward_step(position, loop_state):
        moving, totals_in, weights_in = loop_state
        moving = shifted((moving[0], moving[1], moving[2]), "blk", 1)
        totals_out, weights_out = forward_block(
            queries, moving[0], moving[1], segment_ids, moving[2], totals_in, weights_in
        )
        return (moving, totals_out, weights_out)

    moved_state, totals, weights = lax.fori_loop(
        0, blocks - 1, forward_step, ((key_part, value_part, segment_ids), totals, weights)
    )
    weights_rows = jnp.swapaxes(weights, 1, 2)[..., None]
    attended = totals / weights_rows
    attended_low = attended.reshape(flat_shape).astype(jnp.bfloat16)
    residual = tokens_wide + jnp.dot(attended_low, w_out, preferred_element_type=jnp.float32)
    normed_two_low = layer_norm(residual, second_gain, second_shift).astype(jnp.bfloat16)
    hidden_pre = jnp.dot(normed_two_low, w_in, preferred_element_type=jnp.float32)
    hidden_low = exact_gelu(hidden_pre).astype(jnp.bfloat16)
    layer = residual + jnp.dot(hidden_low, w_down, preferred_element_type=jnp.float32)
    offset = lax.axis_index("blk") * block_len
    places = (
        lax.broadcasted_iota(jnp.int32, (seqs_here, cls_positions.shape[1], block_len), 2) + offset
    )
    chosen = jnp.sum((places == cls_positions[:, :, None]).astype(jnp.float32), axis=1)
    cell_sums = jnp.sum(chosen[..., None] * layer, axis=(0, 1))
    cell_squares = jnp.sum(chosen[..., None] * layer * layer, axis=(0, 1))
    count = cls_positions.shape[0] * cls_positions.shape[1] * lax.axis_size("dp")
    share = width // (lax.axis_size("dp") * blocks)
    moment_sums = lax.psum((cell_sums, cell_squares), ("dp", "blk"))
    rank = lax.axis_index("dp") * blocks + lax.axis_index("blk")
    sum_share = lax.dynamic_slice_in_dim(moment_sums[0], rank * share, share)
    square_share = lax.dynamic_slice_in_dim(moment_sums[1], rank * share, share)
    grad_layer = out_grad.astype(jnp.float32)
    grad_down = jnp.einsum("sbf,sbd->fd", hidden_low, out_grad, preferred_element_type=jnp.float32)
    grad_hidden = jnp.einsum("sbd,fd->sbf", out_grad, w_down, preferred_element_type=jnp.float32)
    grad_pre = jax.vjp(exact_gelu, hidden_pre)[1](grad_hidden)[0].astype(jnp.bfloat16)
    grad_in = jnp.einsum(
        "sbd,sbf->df", normed_two_low, grad_pre, preferred_element_type=jnp.float32
    )
    grad_normed_two = jnp.einsum("sbf,df->sbd", grad_pre, w_in, preferred_element_type=jnp.float32)
    unused_two, pull_two = jax.vjp(layer_norm, residual, second_gain, second_shift)
    residual_part, second_gain_grad, second_shift_grad = pull_two(grad_normed_two)
    grad_residual = grad_layer + residual_part
    grad_proj = grad_residual.astype(jnp.bfloat16)
    grad_out = jnp.einsum(
        "sbd,sbe->de", attended_low, grad_proj, preferred_element_type=jnp.float32
    )
    grad_attended = jnp.einsum(
        "sbe,de->sbd", grad_proj, w_out, preferred_element_type=jnp.float32
    ).reshape(head_shape)
    scaled = (grad_attended / weights_rows).astype(jnp.bfloat16)
    deltas = jnp.swapaxes(jnp.sum(grad_attended * attended, axis=-1), 1, 2) / weights

    def key_step(position, loop_state):
        moving, key_sums, query_sum = loop_state
        grad_queries, grad_keys, grad_values = backward_block(
            queries, scaled, deltas, segment_ids, moving[0], moving[1], moving[2]
        )
        query_next = query_sum + grad_queries
        keys_next = key_sums[0] + grad_keys
        values_next = key_sums[1] + grad_values
        moving = shifted((moving[0], moving[1], moving[2]), "blk", 1)
        key_sums = (
            shifted(keys_next.astype(jnp.bfloat16), "blk", 1).astype(keys_next.dtype),
            shifted(values_next.astype(jnp.bfloat16), "blk", 1).astype(values_next.dtype),
        )
        return (moving, key_sums, query_next)

    zero_heads = jnp.zeros(head_shape, jnp.float32)
    moved_back, key_sums, query_total = lax.fori_loop(
        0,
        blocks,
        key_step,
        ((key_part, value_part, segment_ids), (zero_heads, zero_heads), zero_heads),
    )
    keys_total, values_total = (key_sums[0], key_sums[1])
    grad_qkv_low = jnp.concatenate(
        [
            (query_total * 0.125).reshape(flat_shape),
            keys_total.reshape(flat_shape),
            values_total.reshape(flat_shape),
        ],
        axis=-1,
    ).astype(jnp.bfloat16)
    grad_qkv = jnp.einsum(
        "sbd,sbe->de", normed_low, grad_qkv_low, preferred_element_type=jnp.float32
    )
    grad_normed_one = jnp.einsum(
        "sbe,de->sbd", grad_qkv_low, w_qkv, preferred_element_type=jnp.float32
    )
    unused_one, pull_one = jax.vjp(layer_norm, tokens_wide, first_gain, first_shift)
    tokens_part, first_gain_grad, first_shift_grad = pull_one(grad_normed_one)
    tokens_grad = (grad_residual + tokens_part).astype(jnp.bfloat16)
    summed = (
        lax.psum_scatter(grad_qkv, ("dp", "blk"), scatter_dimension=0, tiled=True),
        lax.psum_scatter(grad_out, ("dp", "blk"), scatter_dimension=0, tiled=True),
        lax.psum_scatter(grad_in, ("dp", "blk"), scatter_dimension=0, tiled=True),
        lax.psum_scatter(grad_down, ("dp", "blk"), scatter_dimension=0, tiled=True),
        lax.psum_scatter(first_gain_grad, ("dp", "blk"), scatter_dimension=0, tiled=True),
        lax.psum_scatter(first_shift_grad, ("dp", "blk"), scatter_dimension=0, tiled=True),
        lax.psum_scatter(second_gain_grad, ("dp", "blk"), scatter_dimension=0, tiled=True),
        lax.psum_scatter(second_shift_grad, ("dp", "blk"), scatter_dimension=0, tiled=True),
    )
    cls_mean = sum_share / count
    cls_variance = square_share / count - cls_mean * cls_mean
    return (
        layer.astype(jnp.bfloat16),
        tokens_grad,
        summed[0],
        summed[1],
        summed[2],
        summed[3],
        summed[4],
        summed[5],
        summed[6],
        summed[7],
        cls_mean,
        cls_variance,
    )


MESH = pl.DeviceIdType.MESH
F32 = jnp.float32
BF16 = jnp.bfloat16
NN = (((1,), (0,)), ((), ()))
NT = (((1,), (1,)), ((), ()))
TN = (((0,), (0,)), ((), ()))


def mm(left, right, dims=NN):
    return lax.dot_general(left, right, dims, preferred_element_type=F32)


def remote(src, dst, send, recv, target):
    return pltpu.make_async_remote_copy(
        src_ref=src, dst_ref=dst, send_sem=send, recv_sem=recv, device_id=target, device_id_type=MESH
    )


def greet(targets):
    barrier = pltpu.get_barrier_semaphore()
    for target in targets:
        pl.semaphore_signal(barrier, inc=1, device_id=target, device_id_type=MESH)
    pl.semaphore_wait(barrier, len(targets))


def place():
    dp, blk = lax.axis_index("dp"), lax.axis_index("blk")
    return dp, blk, dp // 2, lax.rem(dp, 2), blk // 2, lax.rem(blk, 2)


def piece(index, size):
    return pl.ds(pl.multiple_of(index * size, size), size)


def flip(mine, other):
    return mine + other - 2 * mine * other


class RowGather:
    def __init__(self, rows, size, y, c, sibling, ypeer, send, recv, source=None):
        near, far = rows.at[y, piece(c, size)], rows.at[1 - y, piece(c, size)]
        source = near if source is None else source
        self.core = remote(source, near, send.at[0], recv.at[0], sibling)
        self.over = remote(source, near, send.at[1], recv.at[1], ypeer)
        self.last = remote(far, far, send.at[2], recv.at[2], sibling)

    def start(self):
        self.over.start()
        self.core.start()

    def forward(self):
        self.over.wait_recv()
        self.last.start()

    def arrive(self):
        self.core.wait_recv()
        self.last.wait_recv()

    def drain(self):
        for copy in (self.core, self.over, self.last):
            copy.wait_send()


class DpGather:
    def __init__(self, slots, z, x, blk, send, recv):
        self.slots, self.z, self.x, self.send, self.recv = slots, z, x, send, recv
        above, below = lax.rem(z + 1, 4), lax.rem(z + 3, 4)
        self.targets = ((2 * above + x, blk), (2 * below + x, blk), (2 * z + 1 - x, blk))

    def hop(self, kind, zz):
        slot = self.slots.at[self.x, zz]
        return remote(slot, slot, self.send.at[kind, zz], self.recv.at[self.x, zz], self.targets[kind])

    def up(self, zz):
        @pl.when(self.z < 3)
        def _():
            self.hop(0, zz).start()

        self.hop(2, zz).start()

    def down(self, zz):
        @pl.when(self.z > 0)
        def _():
            self.hop(1, zz).start()

    def start(self):
        self.up(self.z)
        self.down(self.z)

    def forward(self, step):
        below, above = self.z - step, self.z + step

        @pl.when(below >= 0)
        def _():
            self.hop(0, below).wait_recv()
            self.up(below)

        @pl.when(above <= 3)
        def _():
            self.hop(1, above).wait_recv()
            self.down(above)
            self.hop(2, above).start()

    def arrive(self, half):
        for k in range(2):
            slot = self.slots.at[1 - self.x, 2 * half + k]
            done = self.recv.at[1 - self.x, 2 * half + k]
            remote(slot, slot, self.send.at[2, k], done, self.targets[2]).wait_recv()

    def drain(self):
        for zz in range(4):
            self.hop(2, zz).wait_send()

            @pl.when((self.z < 3) & (zz <= self.z))
            def _():
                self.hop(0, zz).wait_send()

            @pl.when((self.z > 0) & (zz >= self.z))
            def _():
                self.hop(1, zz).wait_send()


def centered(values):
    center = values - jnp.mean(values, axis=-1, keepdims=True)
    spread = jnp.mean(center * center, axis=-1, keepdims=True)
    scale = lax.rsqrt(spread + EPSILON)
    return center * scale, scale


def norm_back(grad, unit, scale):
    return scale * (
        grad - jnp.mean(grad, axis=-1, keepdims=True) - unit * jnp.mean(grad * unit, axis=-1, keepdims=True)
    )


def half_of(pair, head):
    lanes = lax.broadcasted_iota(jnp.int32, pair.shape, 1) // 64
    return jnp.where(lanes == head, pair, jnp.zeros_like(pair))


def cells_at(cls_ref, places):
    found = jnp.zeros(places.shape, jnp.int32)
    for n in range(cls_ref.shape[1]):
        found = found + (places >= cls_ref[0, n]).astype(jnp.int32)
    return found


def same_cell(cls_ref, start, count, row_len):
    mine = lax.broadcasted_iota(jnp.int32, (count, 1), 0) + start
    other = lax.broadcasted_iota(jnp.int32, (1, row_len), 1)
    return cells_at(cls_ref, mine) == cells_at(cls_ref, other)


def gelu_parts(pre):
    cdf = 0.5 * (1.0 + lax.erf(pre * 0.7071067811865476))
    return cdf, cdf + pre * (0.3989422804014327 * jnp.exp(-0.5 * pre * pre))


def as_row(ref):
    return ref[...].reshape(1, ref.shape[0])


def layer_kernel(
    cls_ref, tok_hbm, grad_hbm, gain1_ref, shift1_ref, gain2_ref, shift2_ref, wqkv_ref, wout_ref, win_ref, wdown_ref,
    layer_out, tgrad_out, gqkv_out, gout_out, in_out, down_out, sums_ref,
    gg, rows_all, qkv_ref, att_ref, turned_ref, aturned_ref, attlow, abox, arow,
    layer_ref, tgrad_ref, gqkv_ref, gout_ref, in_ref, down_ref,
    st_in, st_dn, wi, wd, wo, gx, gp, ht, part_in, part_dn, sib_in, sib_dn, ysend_in, ysend_dn, yrecv_in, yrecv_dn,
    slab, slab_in, residual, unit, gnorm, grow, gatt, low, keys, values, part, xin, zout, zin, zlast, zfirst, hfirst, xfirst, full, fin, landing,
    sums, sbuf, sbox, tbox,
    isem, lsem, rsend, rrecv, ogsend, ogrecv, bsend, brecv, arsend, arrecv, outsem,
    wsem, ssem, osem, gsend, grecv, dsend, drecv, sibs, sibr, ysend, yrecv, qsend, qrecv,
    xsend, xrecv, zsend, zrecv, fsend, frecv, asend, arecv, usend, urecv, tsend, trecv,
):
    dp, blk, z, x, y, c = place()
    tokens, width = tok_hbm.shape
    row_len, both = 4 * tokens, 2 * tokens
    first, pairs = 5 * y + 3 * c, 3 - c
    cut, owned, rows = wi.shape[1], down_ref.shape[0], in_ref.shape[0]
    share = width // 8
    block = st_in.shape[2]
    steps = win_ref.shape[1] // block
    depth = st_in.shape[0]
    sibling, ypeer, diag = (dp, 2 * y + 1 - c), (dp, 2 * (1 - y) + c), (dp, 2 * (1 - y) + 1 - c)
    xpeer = (2 * z + 1 - x, blk)
    others = ((1, sibling), (2, ypeer), (3, diag))
    received = ((1, sibling, 2 + c), (2, ypeer, pairs), (3, diag, 2 + c))

    tok_in = pltpu.make_async_copy(tok_hbm, rows_all.at[y, piece(c, tokens), :], isem.at[0])
    grad_in = pltpu.make_async_copy(grad_hbm, gg.at[x, z], isem.at[1])
    tok_in.start()
    grad_in.start()

    def load(j, t):
        source = wqkv_ref.at[:, pl.ds(pl.multiple_of(t * width + (first + j) * 128, 128), 128)]
        return pltpu.make_async_copy(source, st_in.at[j, :, pl.ds(t * 128, 128)], lsem.at[j, t])

    @pl.loop(0, pairs)
    def _(j):
        for t in range(3):
            load(j, t).start()

    def stream_in(i):
        slot = lax.rem(i, depth)
        return pltpu.make_async_copy(win_ref.at[:, piece(i, block)], st_in.at[slot], ssem.at[0, slot])

    def stream_dn(i):
        slot = lax.rem(i, depth)
        return pltpu.make_async_copy(wdown_ref.at[piece(i, block), :], st_dn.at[slot], ssem.at[1, slot])

    tails = ((0, block), (1, block), (2, width - 2 * block))

    def load_out(i, size):
        return pltpu.make_async_copy(
            wout_ref.at[pl.ds(i * block, size), :], st_dn.at[i, pl.ds(0, size), :], ssem.at[1, i]
        )

    def load_rows(j):
        return pltpu.make_async_copy(wout_ref.at[piece(first + j, 128), :], wo.at[j], osem.at[j])

    greet([sibling, ypeer, diag] + [(lax.rem(dp + k, 8), blk) for k in range(1, 8)])
    row_tok = RowGather(rows_all, tokens, y, c, sibling, ypeer, rsend, rrecv, tok_hbm)
    grads = DpGather(gg, z, x, blk, ogsend, ogrecv)
    row_tok.start()
    tok_in.wait()
    grad_in.wait()
    grads.start()
    for i, size in tails:
        load_out(i, size).start()

    @pl.loop(0, pairs)
    def _(j):
        load_rows(j).start()
        for t in range(3):
            load(j, t).wait()

    normed_rows = wd

    @pl.loop(0, 2)
    def _(step):
        @pl.when(step == 0)
        def _():
            row_tok.core.wait_recv()

        @pl.when(step == 1)
        def _():
            row_tok.forward()
            row_tok.last.wait_recv()
            grads.forward(1)

        chip = flip(y, step)
        at = piece(chip, both)
        normed_rows[at, :] = (centered(rows_all[chip].astype(F32))[0] * as_row(gain1_ref) + as_row(shift1_ref)).astype(BF16)

        @pl.loop(0, pairs)
        def _(j):
            made = mm(normed_rows[at, :], st_in[j, :, 0:384])
            qkv_ref[j, at, 0:128] = (made[:, 0:128] * 0.125).astype(BF16)
            qkv_ref[j, at, 128:384] = made[:, 128:384].astype(BF16)

    for i in range(depth - 1):
        stream_in(i).start()

    def to_own(j, r, target):
        return remote(attlow.at[j, piece(target[1], tokens), :], abox.at[r, j], bsend.at[r, j], brecv.at[r, j], target)

    @pl.loop(0, pairs)
    def _(j):
        @pl.loop(0, 2)
        def _(part):
            at = piece(part, both)
            same = same_cell(cls_ref, part * both, both, row_len)
            pair = jnp.zeros((both, 128), F32)
            for head in range(2):
                scores = mm(half_of(qkv_ref[j, at, 0:128], head), qkv_ref[j, :, 128:256], NT)
                weigh = jnp.where(same, jnp.exp(scores), 0.0)
                total = jnp.sum(weigh, axis=-1, keepdims=True)
                pair = pair + half_of(mm(weigh.astype(BF16), qkv_ref[j, :, 256:384]) / total, head)
            att_ref[j, at, :] = pair
            attlow[j, at, :] = pair.astype(BF16)

        for r, target in others:
            to_own(j, r, target).start()
        abox[0, j] = attlow[j, piece(blk, tokens), :]

        @pl.when(j == 1)
        def _():
            grads.forward(2)

    for b in range(4):
        at = slice(b * tokens, (b + 1) * tokens)
        turned_ref[:, at] = normed_rows[at, :].T

    for r, target, count in received:

        @pl.loop(0, count)
        def _(j):
            to_own(j, r, target).wait_recv()

    own_at = (y, piece(c, tokens))
    for p in range(10):
        yy, cc = p // 5, (p % 5) // 3
        slot = 2 * flip(y, yy) + flip(c, cc)
        arow[y, piece(c, tokens), 128 * p : 128 * p + 128] = abox[slot, p % 5 - 3 * cc]
    row_att = RowGather(arow, tokens, y, c, sibling, ypeer, arsend, arrecv)

    made = rows_all[y, piece(c, tokens), :].astype(F32)
    for i, size in tails:
        load_out(i, size).wait()
        made = made + mm(arow[y, piece(c, tokens), i * block : i * block + size], st_dn[i, :size, :])
    for i in range(depth - 1):
        stream_dn(i).start()
    residual[...] = made
    made, scale2 = centered(made)
    unit[...] = made
    gx[x, z] = (made * as_row(gain2_ref) + as_row(shift2_ref)).astype(BF16)
    normed = DpGather(gx, z, x, blk, dsend, drecv)
    normed.start()
    row_att.start()
    gnorm[...] = jnp.zeros_like(gnorm)

    @pl.loop(0, steps)
    def _(i):
        slot = lax.rem(i, depth)

        @pl.when(i + depth - 1 < steps)
        def _():
            stream_in(i + depth - 1).start()
            stream_dn(i + depth - 1).start()

        stream_in(i).wait()
        stream_dn(i).wait()
        pre = mm(gx[x, z], st_in[slot])
        cdf, slope = gelu_parts(pre)
        grad = (mm(gg[x, z], st_dn[slot], NT) * slope).astype(BF16)
        residual[...] += mm((pre * cdf).astype(BF16), st_dn[slot])
        gnorm[...] += mm(grad, st_in[slot], NT)

        @pl.when(i == 2)
        def _():
            grads.forward(3)

        @pl.when(i == 6)
        def _():
            row_att.forward()
            normed.forward(1)

    load_in = pltpu.make_async_copy(win_ref.at[:, piece(dp, cut)], wi, wsem.at[0])
    load_dn = pltpu.make_async_copy(wdown_ref.at[piece(dp, cut), :], wd, wsem.at[1])
    load_in.start()
    load_dn.start()
    layer = residual[...]
    layer_ref[...] = layer.astype(BF16)
    outs = [pltpu.make_async_copy(layer_ref, layer_out, outsem.at[0])]
    outs[0].start()
    sums[...] = jnp.zeros_like(sums)
    spots = lax.broadcasted_iota(jnp.int32, (tokens, 1), 0) + blk * tokens
    chosen = jnp.zeros((tokens, 1), F32)
    for n in range(cls_ref.shape[1]):
        chosen = chosen + (spots == cls_ref[0, n]).astype(F32)
    sums[4:5, :] = jnp.sum(chosen * layer, axis=0, keepdims=True)
    sums[5:6, :] = jnp.sum(chosen * layer * layer, axis=0, keepdims=True)
    grad = gnorm[...]
    sums[2:3, :] = jnp.sum(grad * unit[...], axis=0, keepdims=True)
    sums[3:4, :] = jnp.sum(grad, axis=0, keepdims=True)
    made = gg[x, z].astype(F32) + norm_back(grad * as_row(gain2_ref), unit[...], scale2)
    residual[...] = made
    grow[y, piece(c, tokens), :] = made.astype(BF16)
    row = RowGather(grow, tokens, y, c, sibling, ypeer, gsend, grecv)
    row.start()
    normed.forward(2)
    load_in.wait()
    load_dn.wait()

    def stream_qkv(p, t):
        slot = lax.rem(p, depth)
        source = wqkv_ref.at[:, pl.ds(pl.multiple_of(t * width + p * 128, 128), 128)]
        return pltpu.make_async_copy(source, st_in.at[slot, :, pl.ds(t * 128, 128)], wsem.at[2 + 3 * slot + t])

    for p in range(depth):
        for t in range(3):
            stream_qkv(p, t).start()
    near = z // 2

    def make(xx, half):
        at = piece(2 * xx + half, both)
        pre = mm(gx[xx, piece(half, 2)].reshape(both, width), wi[...])
        cdf, slope = gelu_parts(pre)
        ht[:, at] = (pre * cdf).astype(BF16).T
        gp[at, :] = (mm(gg[xx, piece(half, 2)].reshape(both, width), wd[...], NT) * slope).astype(BF16)

    def makes(first_step, last_step):
        @pl.loop(first_step, last_step)
        def _(step):
            make(flip(x, lax.rem(step, 2)), flip(near, step // 2))

    makes(0, 1)
    row_att.arrive()
    for b in range(4):
        aturned_ref[:, b * tokens : (b + 1) * tokens] = arow[b // 2, (b % 2) * tokens : (b % 2 + 1) * tokens, :].T
    row.forward()
    row.arrive()

    @pl.loop(0, pairs)
    def _(j):
        load_rows(j).wait()
        gatt[j] = mm(grow[...].reshape(row_len, width), wo[j], NT)

    even, pair_z, half_z = lax.rem(z, 2), z + 1 - 2 * lax.rem(z, 2), lax.rem(z + 2, 4)

    def to_x(s):
        return remote(part.at[s, 1 - x], xin.at[s - 1], xsend.at[s], xrecv.at[s], xpeer)

    def to_pair(s):
        return remote(zout.at[s - 1, 1 - even], zin.at[s - 1], zsend.at[s, 0], zrecv.at[s, 0], (2 * pair_z + x, blk))

    def to_half(s):
        return remote(zlast.at[s - 1, 0], zlast.at[s - 1, 1], zsend.at[s, 1], zrecv.at[s, 1], (2 * half_z + x, blk))

    other_half, my_half = 1 - z // 2, z // 2
    def first_moves(wide):
        lanes = pl.ds(0, wide)
        return (
            lambda: remote(
                part.at[0, :, 1 - even, :, :, lanes], zfirst.at[:, :, :, lanes], zsend.at[0, 0], zrecv.at[0, 0],
                (2 * pair_z + x, blk),
            ),
            lambda: remote(
                hfirst.at[0, :, :, lanes], hfirst.at[1, :, :, lanes], zsend.at[0, 1], zrecv.at[0, 1],
                (2 * half_z + x, blk),
            ),
            lambda: remote(xfirst.at[0, :, lanes], xfirst.at[1, :, lanes], xsend.at[0], xrecv.at[0], xpeer),
        )

    def first_move(stage, act):
        for core in range(2):

            @pl.when(c == core)
            def _():
                act(first_moves(128 * (3 - core))[stage]())

    def begin(copy):
        copy.start()

    def finish_copy(copy):
        copy.wait()

    def to_blk(s, r, target):
        return remote(full.at[s, target[1]], fin.at[r, s], fsend.at[r, s], frecv.at[r, s], target)

    def to_low(j, r, target):
        return remote(low.at[j, piece(target[1], tokens), :], landing.at[r, j], asend.at[r, j], arecv.at[r, j], target)

    def add_x(s):
        to_x(s).wait()
        for k in range(4):
            zout[s - 1, k // 2, k % 2] = (part[s, x, k // 2, k % 2].astype(F32) + xin[s - 1, k // 2, k % 2].astype(F32)).astype(BF16)
        to_pair(s).start()

    def add_pair(s):
        to_pair(s).wait()
        away = 1 - z // 2
        zlast[s - 1, 0] = (zout[s - 1, even, away].astype(F32) + zin[s - 1, away].astype(F32)).astype(BF16)
        to_half(s).start()

    def add_half(s):
        to_half(s).wait()
        mine = z // 2
        total = zout[s - 1, even, mine].astype(F32) + zin[s - 1, mine].astype(F32) + zlast[s - 1, 1].astype(F32)
        to_owners(s, total)

    def to_owners(s, total):
        for b in range(4):
            full[s, b] = total[b * rows : (b + 1) * rows].astype(BF16)
        for r, target in others:
            to_blk(s, r, target).start()
        fin[0, s] = full[s, blk]

    def first_a():
        first_move(0, finish_copy)
        for xx in range(2):
            hfirst[0, xx] = (part[0, xx, even, other_half].astype(F32) + zfirst[xx, other_half].astype(F32)).astype(BF16)
        first_move(1, begin)

    def first_sum(xx):
        return part[0, xx, even, my_half].astype(F32) + zfirst[xx, my_half].astype(F32) + hfirst[1, xx].astype(F32)

    def first_b():
        first_move(1, finish_copy)
        xfirst[0] = first_sum(1 - x).astype(BF16)
        first_move(2, begin)

    def first_c():
        first_move(2, finish_copy)
        to_owners(0, first_sum(x) + xfirst[1].astype(F32))

    def weight_part(s, left, right):
        @pl.loop(0, 4)
        def _(zz):
            made = mm(left[piece(zz, 2 * share), :], right)
            part[s, 0, lax.rem(zz, 2), zz // 2] = made[:share].astype(BF16)
            part[s, 1, lax.rem(zz, 2), zz // 2] = made[share:].astype(BF16)

    @pl.when(c == 0)
    def _():
        weight_part(0, aturned_ref, grow[:, :, pl.ds(pl.multiple_of(first * 128, 128), 384)].reshape(row_len, 384))

    @pl.when(c == 1)
    def _():
        right = grow[:, :, pl.ds(pl.multiple_of(first * 128, 128), 256)].reshape(row_len, 256)
        weight_part(0, aturned_ref, jnp.concatenate([right, jnp.zeros((row_len, 128), BF16)], axis=1))

    first_move(0, begin)
    normed.forward(3)
    to_sibling = []
    for kind, source, box in ((0, part_in, sib_in), (1, part_dn, sib_dn)):
        for yy in range(2):
            away = source.at[2 * yy + (1 - c)]
            to_sibling.append(remote(away, box.at[yy], sibs.at[kind, yy], sibr.at[kind, yy], sibling))
    to_y = (
        remote(ysend_in, yrecv_in, ysend.at[0], yrecv.at[0], ypeer),
        remote(ysend_dn, yrecv_dn, ysend.at[1], yrecv.at[1], ypeer),
    )

    over = 2 * (1 - y) + c

    @pl.loop(0, pairs)
    def _(j):
        keys[...] = jnp.zeros_like(keys)
        values[...] = jnp.zeros_like(values)

        @pl.loop(0, 2)
        def _(half):
            at = piece(half, both)
            same = same_cell(cls_ref, half * both, both, row_len)
            queries_grad = jnp.zeros((both, 128), F32)
            for head in range(2):
                query = half_of(qkv_ref[j, at, 0:128], head)
                key = half_of(qkv_ref[j, :, 128:256], head)
                grad = half_of(gatt[j, at, :], head)
                weigh = jnp.where(same, jnp.exp(mm(query, key, NT)), 0.0)
                total = jnp.sum(weigh, axis=-1, keepdims=True)
                scaled = (grad / total).astype(BF16)
                delta = jnp.sum(grad * att_ref[j, at, :], axis=-1, keepdims=True) / total
                spread = mm(scaled, qkv_ref[j, :, 256:384], NT)
                score = (weigh * (spread - delta)).astype(BF16)
                queries_grad = queries_grad + mm(score, key)
                keys[...] += mm(score, query, TN)
                values[...] += mm(weigh.astype(BF16), scaled, TN)
            low[j, at, 0:128] = (queries_grad * 0.125).astype(BF16)

        low[j, :, 128:256] = keys[...].astype(BF16)
        low[j, :, 256:384] = values[...].astype(BF16)
        for r, target in others:
            to_low(j, r, target).start()
        weight_part(j + 1, turned_ref, low[j])

        @pl.when(j == 0)
        def _():
            to_x(1).start()

        @pl.when(j == pairs - 1)
        def _():
            for half in range(2):
                normed.arrive(half)
                grads.arrive(half)
            to_x(2).start()

            @pl.when(c == 0)
            def _():
                to_x(3).start()

            makes(1, 4)
            first_a()

            @pl.loop(0, 2)
            def _(half):
                left = gx[:, :, :, piece(half, width // 2)].reshape(8 * tokens, width // 2)
                made = mm(left, gp[...], TN)
                for n in range(4):
                    for q in range(4):
                        at = n * share + q * rows
                        part_in[q, 4 * half + n] = made[at : at + rows].astype(BF16)

            to_sibling[0].start()
            to_sibling[1].start()
            every = gg[...].reshape(8 * tokens, width)

            @pl.loop(0, 4)
            def _(q):
                part_dn[q] = mm(ht[piece(q, owned), :], every).astype(BF16)

            to_sibling[2].start()
            to_sibling[3].start()
            to_sibling[0].wait()
            to_sibling[1].wait()
            ysend_in[...] = (part_in[over].astype(F32) + sib_in[1 - y].astype(F32)).astype(BF16)
            to_y[0].start()
            to_sibling[2].wait()
            to_sibling[3].wait()
            ysend_dn[...] = (part_dn[over].astype(F32) + sib_dn[1 - y].astype(F32)).astype(BF16)
            first_b()
            add_x(1)

    add_x(2)
    add_pair(1)

    mine = 2 * y + c
    to_q = []
    for k in range(1, 8):
        target = lax.rem(dp + k, 8)
        to_q.append(remote(slab.at[target], slab_in.at[dp], qsend.at[k], qrecv.at[k], (target, blk)))

    def start_q():
        to_y[0].wait()
        to_y[1].start()
        total = part_in[mine].astype(F32) + sib_in[y].astype(F32) + yrecv_in[...].astype(F32)
        slab[...] = total.astype(BF16)
        for copy in to_q:
            copy.start()
        slab_in[dp] = slab[dp]

    start_q()
    @pl.when(c == 0)
    def _():
        add_x(3)

    first_c()

    @pl.loop(0, pairs)
    def _(j):
        landing[0, j] = low[j, piece(blk, tokens), :]
        for r, target in others:
            to_low(j, r, target).wait_send()

    for r, target, count in received:

        @pl.loop(0, count)
        def _(j):
            to_low(j, r, target).wait_recv()

    gnorm[...] = jnp.zeros_like(gnorm)
    @pl.loop(0, 10)
    def _(p):
        @pl.when((p > 0) & (p + depth - 1 < 10))
        def _():
            for t in range(3):
                stream_qkv(p + depth - 1, t).start()

        for t in range(3):
            stream_qkv(p, t).wait()
        yy, pp = p // 5, lax.rem(p, 5)
        cc = pp // 3
        slot = 2 * flip(y, yy) + flip(c, cc)
        gnorm[...] += mm(landing[slot, pp - 3 * cc], st_in[lax.rem(p, depth), :, 0:384], NT)

    grad = gnorm[...]
    made, scale1 = centered(rows_all[y, piece(c, tokens), :].astype(F32))
    sums[0:1, :] = jnp.sum(grad * made, axis=0, keepdims=True)
    sums[1:2, :] = jnp.sum(grad, axis=0, keepdims=True)
    sbuf[...] = jnp.zeros_like(sbuf)
    for k in range(8):
        sbuf[k, :, 0:share] = sums[:, k * share : (k + 1) * share]
    to_u = []
    for k in range(1, 8):
        target = lax.rem(dp + k, 8)
        to_u.append(remote(sbuf.at[target], sbox.at[dp], usend.at[k], urecv.at[k], (target, blk)))
        to_u[-1].start()
    sbox[dp] = sbuf[dp]
    tgrad_ref[...] = (residual[...] + norm_back(grad * as_row(gain1_ref), made, scale1)).astype(BF16)
    outs.append(pltpu.make_async_copy(tgrad_ref, tgrad_out, outsem.at[1]))
    outs[-1].start()

    def end_down():
        to_y[1].wait()
        down_ref[...] = part_dn[mine].astype(F32) + sib_dn[y].astype(F32) + yrecv_dn[...].astype(F32)
        outs.append(pltpu.make_async_copy(down_ref, down_out, outsem.at[2]))
        outs[-1].start()

    def end_q():
        for copy in to_q:
            copy.wait()
        for s in range(8):
            in_ref[:, s * cut : (s + 1) * cut] = slab_in[s].astype(F32)
        outs.append(pltpu.make_async_copy(in_ref, in_out, outsem.at[3]))
        outs[-1].start()

    to_t = [remote(tbox.at[0], tbox.at[r], tsend.at[r], trecv.at[r], target) for r, target in others]

    def start_t():
        for copy in to_u:
            copy.wait()
        tbox[0] = jnp.sum(sbox[...], axis=0)
        for copy in to_t:
            copy.start()

    def end_t():
        for copy in to_t:
            copy.wait()
        total = (tbox[0] + tbox[1]) + (tbox[2] + tbox[3])
        for b in range(4):

            @pl.when(blk == b)
            def _():
                sums_ref[...] = total[:, b * rows : (b + 1) * rows]

    add_pair(2)
    add_half(1)

    @pl.when(c == 0)
    def _():
        add_pair(3)

    start_t()
    add_half(2)

    @pl.when(c == 0)
    def _():
        add_half(3)

    end_down()
    end_t()
    end_q()

    @pl.loop(0, pairs + 1)
    def _(s):
        for r, target in others:
            to_blk(s, r, target).wait_send()

    for r, target, count in received:

        @pl.loop(0, count + 1)
        def _(s):
            to_blk(s, r, target).wait_recv()

    for yy in range(2):
        for cc in range(2):
            slot = 2 * flip(y, yy) + flip(c, cc)
            p = 5 * yy + 3 * cc
            wide = 128 * (3 - cc)
            gout_ref[:, 128 * p : 128 * p + wide] = fin[slot, 0, :, :wide].astype(F32)
            for j in range(3 - cc):
                for t in range(3):
                    at = t * width + 128 * (p + j)
                    gqkv_ref[:, at : at + 128] = fin[slot, j + 1, :, 128 * t : 128 * t + 128].astype(F32)
    outs.append(pltpu.make_async_copy(gqkv_ref, gqkv_out, outsem.at[4]))
    outs[-1].start()
    outs.append(pltpu.make_async_copy(gout_ref, gout_out, outsem.at[5]))
    outs[-1].start()

    @pl.loop(0, pairs)
    def _(j):
        for r, target in others:
            to_own(j, r, target).wait_send()

    for gather in (row_tok, row_att, row, grads, normed):
        gather.drain()
    for copy in outs:
        copy.wait()


def finish_kernel(cells, sums_ref, *refs):
    count = 6
    arrays, (mean_ref, variance_ref, *grads), outs = refs[:count], refs[count : count + 6], refs[count + 6 : 2 * count + 6]
    held, isem, osem = refs[2 * count + 6 : -2], refs[-2], refs[-1]
    loads = [pltpu.make_async_copy(arrays[i], held[i], isem.at[i]) for i in range(count)]
    stores = [pltpu.make_async_copy(held[i], outs[i], osem.at[i]) for i in range(count)]
    for load in loads:
        load.start()
    for load, store in zip(loads, stores):
        load.wait()
        store.start()
    mean = sums_ref[4:5, :] / cells
    mean_ref[...] = mean
    variance_ref[...] = sums_ref[5:6, :] / cells - mean * mean
    for i in range(4):
        grads[i][...] = sums_ref[i : i + 1, :]
    for store in stores:
        store.wait()


def finish(cells, sums, *arrays):
    anywhere, v = pl.BlockSpec(memory_space=pl.ANY), pl.BlockSpec(memory_space=pltpu.VMEM)
    count = len(arrays)
    small = jax.ShapeDtypeStruct((1, sums.shape[1]), F32)
    return pl.pallas_call(
        functools.partial(finish_kernel, cells),
        out_shape=(small,) * 6 + tuple(jax.ShapeDtypeStruct(a.shape, a.dtype) for a in arrays),
        in_specs=[v] + [anywhere] * count,
        out_specs=(v,) * 6 + (anywhere,) * count,
        scratch_shapes=[pltpu.VMEM(a.shape, a.dtype) for a in arrays]
        + [pltpu.SemaphoreType.DMA((count,)), pltpu.SemaphoreType.DMA((count,))],
    )(sums, *arrays)


def whole_layer(cls_positions, tokens, grad, gain1, shift1, gain2, shift2, w_qkv, w_out, w_in, w_down):
    count, width = tokens.shape
    inner = w_in.shape[1]
    row_len, share = 4 * count, width // 8
    cut, owned, rows = inner // 8, inner // 32, width // 32
    block, depth = 512, 3
    v = pltpu.VMEM
    dma = pltpu.SemaphoreType.DMA
    anywhere = pl.BlockSpec(memory_space=pl.ANY)
    return pl.pallas_call(
        layer_kernel,
        out_shape=(
            jax.ShapeDtypeStruct((count, width), BF16),
            jax.ShapeDtypeStruct((count, width), BF16),
            jax.ShapeDtypeStruct((rows, 3 * width), F32),
            jax.ShapeDtypeStruct((rows, width), F32),
            jax.ShapeDtypeStruct((rows, inner), F32),
            jax.ShapeDtypeStruct((owned, width), F32),
            jax.ShapeDtypeStruct((8, rows), F32),
        ),
        in_specs=[pl.BlockSpec(memory_space=pltpu.SMEM)]
        + [anywhere] * 2
        + [pl.BlockSpec(memory_space=v)] * 4
        + [anywhere] * 4,
        out_specs=(anywhere,) * 6 + (pl.BlockSpec(memory_space=v),),
        scratch_shapes=[
            v((2, 4, count, width), BF16), v((2, 2 * count, width), BF16),
            v((3, row_len, 384), BF16), v((3, row_len, 128), F32), v((width, row_len), BF16), v((width, row_len), BF16),
            v((3, row_len, 128), BF16), v((4, 3, count, 128), BF16), v((2, 2 * count, width), BF16),
            v((count, width), BF16), v((count, width), BF16), v((rows, 3 * width), F32), v((rows, width), F32),
            v((rows, inner), F32), v((owned, width), F32),
            v((depth, width, block), BF16), v((depth, block, width), BF16),
            v((width, cut), BF16), v((cut, width), BF16), v((3, 128, width), BF16),
            v((2, 4, count, width), BF16), v((8 * count, cut), BF16), v((cut, 8 * count), BF16),
            v((4, 8, rows, cut), BF16), v((4, owned, width), BF16),
            v((2, 8, rows, cut), BF16), v((2, owned, width), BF16),
            v((8, rows, cut), BF16), v((owned, width), BF16), v((8, rows, cut), BF16), v((owned, width), BF16),
            v((8, rows, cut), BF16), v((8, rows, cut), BF16),
            v((count, width), F32), v((count, width), F32), v((count, width), F32),
            v((2, 2 * count, width), BF16), v((3, row_len, 128), F32), v((3, row_len, 384), BF16),
            v((row_len, 128), F32), v((row_len, 128), F32),
            v((4, 2, 2, 2, share, 384), BF16), v((3, 2, 2, share, 384), BF16), v((3, 2, 2, share, 384), BF16),
            v((3, 2, share, 384), BF16), v((3, 2, share, 384), BF16),
            v((2, 2, share, 384), BF16), v((2, 2, share, 384), BF16), v((2, share, 384), BF16),
            v((4, 4, share // 4, 384), BF16), v((4, 4, share // 4, 384), BF16),
            v((4, 3, count, 384), BF16),
            v((8, width), F32), v((8, 8, 256), F32), v((8, 8, 256), F32), v((4, 8, 256), F32),
            dma((2,)), dma((3, 3)), dma((3,)), dma((3,)), dma((3, 4)), dma((2, 4)), dma((4, 3)), dma((4, 3)),
            dma((3,)), dma((3,)), dma((6,)),
            dma((2 + 3 * depth,)), dma((2, depth)), dma((3,)), dma((3,)), dma((3,)), dma((3, 4)), dma((2, 4)),
            dma((2, 2)), dma((2, 2)), dma((2,)), dma((2,)), dma((8,)), dma((8,)),
            dma((4,)), dma((4,)), dma((4, 3)), dma((4, 3)), dma((4, 4)), dma((4, 4)), dma((4, 3)), dma((4, 3)),
            dma((8,)), dma((8,)), dma((4,)), dma((4,)),
        ],
        compiler_params=pltpu.CompilerParams(collective_id=1, has_side_effects=True, vmem_limit_bytes=64 * 2**20),
        cost_estimate=pl.CostEstimate(flops=40 * 2**30, bytes_accessed=50 * 2**20, transcendentals=0),
    )(cls_positions, tokens, grad, gain1, shift1, gain2, shift2, w_qkv, w_out, w_in, w_down)


def on_device(
    tokens,
    first_gain,
    first_shift,
    w_qkv,
    w_out,
    second_gain,
    second_shift,
    w_in,
    w_down,
    segment_ids,
    cls_positions,
    out_grad,
):
    tokens, out_grad = tokens[0], out_grad[0]
    layer, tokens_grad, grad_qkv, grad_out, grad_in, grad_down, sums = whole_layer(
        cls_positions, tokens, out_grad, first_gain, first_shift, second_gain, second_shift, w_qkv, w_out, w_in, w_down
    )
    mean, variance, gain1_grad, shift1_grad, gain2_grad, shift2_grad, *large = finish(
        cls_positions.size * lax.axis_size("dp"), sums, layer, tokens_grad, grad_qkv, grad_out, grad_in, grad_down
    )
    return (
        large[0][None],
        large[1][None],
        *large[2:],
        gain1_grad[0],
        shift1_grad[0],
        gain2_grad[0],
        shift2_grad[0],
        mean[0],
        variance[0],
    )


def solution(mesh):
    placed = (
        P("dp", "blk", None),
        P(),
        P(),
        P(),
        P(),
        P(),
        P(),
        P(),
        P(),
        P("dp", "blk"),
        P("dp", None),
        P("dp", "blk", None),
    )
    small = mesh.shape["dp"] == 8 and mesh.shape["blk"] == 4
    return jax.shard_map(
        on_device if small else on_device_general,
        mesh=mesh,
        in_specs=placed,
        out_specs=(
            P("dp", "blk", None),
            P("dp", "blk", None),
            P(("dp", "blk"), None),
            P(("dp", "blk"), None),
            P(("dp", "blk"), None),
            P(("dp", "blk"), None),
            P(("dp", "blk")),
            P(("dp", "blk")),
            P(("dp", "blk")),
            P(("dp", "blk")),
            P(("dp", "blk")),
            P(("dp", "blk")),
        ),
        check_vma=False,
    )
```

```python
import functools

import jax
import jax.numpy as jnp
from jax import lax
from jax.experimental import pallas as pl
from jax.experimental.pallas import tpu as pltpu
from jax.sharding import PartitionSpec as P

H = 20


EPSILON = 1e-05


def shifted(block, axis, distance):
    devices = range(lax.axis_size(axis))
    route = [((i - distance) % len(devices), i) for i in devices]
    return lax.ppermute(block, axis, route)


def layer_norm(values, gain, shift):
    center = values - jnp.mean(values, axis=-1, keepdims=True)
    spread = jnp.mean(center * center, axis=-1, keepdims=True)
    return center * lax.rsqrt(spread + EPSILON) * gain + shift


def exact_gelu(values):
    return jax.nn.gelu(values, approximate=False)


def same_cells(query_cells, key_cells):
    return query_cells[:, :, None] == key_cells[:, None, :]


def forward_block(queries, key_part, value_part, query_cells, key_cells, totals, weights):
    scores = jnp.einsum("sqhd,skhd->shqk", queries, key_part, preferred_element_type=jnp.float32)
    exp_scores = jnp.where(same_cells(query_cells, key_cells)[:, None], jnp.exp(scores), 0.0)
    weights = weights + jnp.sum(exp_scores, axis=-1)
    totals = totals + jnp.einsum(
        "shqk,skhd->sqhd",
        exp_scores.astype(jnp.bfloat16),
        value_part,
        preferred_element_type=jnp.float32,
    )
    return (totals, weights)


def backward_block(queries, scaled, deltas, query_cells, key_part, value_part, key_cells):
    scores = jnp.einsum("sqhd,skhd->shqk", queries, key_part, preferred_element_type=jnp.float32)
    exp_scores = jnp.where(same_cells(query_cells, key_cells)[:, None], jnp.exp(scores), 0.0)
    grad_exp = jnp.einsum("sqhd,skhd->shqk", scaled, value_part, preferred_element_type=jnp.float32)
    grad_scores = (exp_scores * (grad_exp - deltas[..., None])).astype(jnp.bfloat16)
    grad_queries = jnp.einsum(
        "shqk,skhd->sqhd", grad_scores, key_part, preferred_element_type=jnp.float32
    )
    grad_keys = jnp.einsum(
        "shqk,sqhd->skhd", grad_scores, queries, preferred_element_type=jnp.float32
    )
    grad_values = jnp.einsum(
        "shqk,sqhd->skhd",
        exp_scores.astype(jnp.bfloat16),
        scaled,
        preferred_element_type=jnp.float32,
    )
    return (grad_queries, grad_keys, grad_values)


def on_device_general(
    tokens,
    first_gain,
    first_shift,
    w_qkv,
    w_out,
    second_gain,
    second_shift,
    w_in,
    w_down,
    segment_ids,
    cls_positions,
    out_grad,
):
    seqs_here, block_len, width = tokens.shape
    head_count = H
    head_size = width // head_count
    blocks = lax.axis_size("blk")
    head_shape = (seqs_here, block_len, head_count, head_size)
    flat_shape = (seqs_here, block_len, width)
    tokens_wide = tokens.astype(jnp.float32)
    normed_low = layer_norm(tokens_wide, first_gain, first_shift).astype(jnp.bfloat16)
    projected = jnp.dot(normed_low, w_qkv, preferred_element_type=jnp.float32)
    queries = (projected[..., :width] * 0.125).astype(jnp.bfloat16).reshape(head_shape)
    key_part = projected[..., width : 2 * width].astype(jnp.bfloat16).reshape(head_shape)
    value_part = projected[..., 2 * width :].astype(jnp.bfloat16).reshape(head_shape)
    totals = jnp.zeros(head_shape, jnp.float32)
    weights = jnp.zeros((seqs_here, head_count, block_len), jnp.float32)
    totals, weights = forward_block(
        queries, key_part, value_part, segment_ids, segment_ids, totals, weights
    )

    def forward_step(position, loop_state):
        moving, totals_in, weights_in = loop_state
        moving = shifted((moving[0], moving[1], moving[2]), "blk", 1)
        totals_out, weights_out = forward_block(
            queries, moving[0], moving[1], segment_ids, moving[2], totals_in, weights_in
        )
        return (moving, totals_out, weights_out)

    moved_state, totals, weights = lax.fori_loop(
        0, blocks - 1, forward_step, ((key_part, value_part, segment_ids), totals, weights)
    )
    weights_rows = jnp.swapaxes(weights, 1, 2)[..., None]
    attended = totals / weights_rows
    attended_low = attended.reshape(flat_shape).astype(jnp.bfloat16)
    residual = tokens_wide + jnp.dot(attended_low, w_out, preferred_element_type=jnp.float32)
    normed_two_low = layer_norm(residual, second_gain, second_shift).astype(jnp.bfloat16)
    hidden_pre = jnp.dot(normed_two_low, w_in, preferred_element_type=jnp.float32)
    hidden_low = exact_gelu(hidden_pre).astype(jnp.bfloat16)
    layer = residual + jnp.dot(hidden_low, w_down, preferred_element_type=jnp.float32)
    offset = lax.axis_index("blk") * block_len
    places = (
        lax.broadcasted_iota(jnp.int32, (seqs_here, cls_positions.shape[1], block_len), 2) + offset
    )
    chosen = jnp.sum((places == cls_positions[:, :, None]).astype(jnp.float32), axis=1)
    cell_sums = jnp.sum(chosen[..., None] * layer, axis=(0, 1))
    cell_squares = jnp.sum(chosen[..., None] * layer * layer, axis=(0, 1))
    count = cls_positions.shape[0] * cls_positions.shape[1] * lax.axis_size("dp")
    share = width // (lax.axis_size("dp") * blocks)
    moment_sums = lax.psum((cell_sums, cell_squares), ("dp", "blk"))
    rank = lax.axis_index("dp") * blocks + lax.axis_index("blk")
    sum_share = lax.dynamic_slice_in_dim(moment_sums[0], rank * share, share)
    square_share = lax.dynamic_slice_in_dim(moment_sums[1], rank * share, share)
    grad_layer = out_grad.astype(jnp.float32)
    grad_down = jnp.einsum("sbf,sbd->fd", hidden_low, out_grad, preferred_element_type=jnp.float32)
    grad_hidden = jnp.einsum("sbd,fd->sbf", out_grad, w_down, preferred_element_type=jnp.float32)
    grad_pre = jax.vjp(exact_gelu, hidden_pre)[1](grad_hidden)[0].astype(jnp.bfloat16)
    grad_in = jnp.einsum(
        "sbd,sbf->df", normed_two_low, grad_pre, preferred_element_type=jnp.float32
    )
    grad_normed_two = jnp.einsum("sbf,df->sbd", grad_pre, w_in, preferred_element_type=jnp.float32)
    unused_two, pull_two = jax.vjp(layer_norm, residual, second_gain, second_shift)
    residual_part, second_gain_grad, second_shift_grad = pull_two(grad_normed_two)
    grad_residual = grad_layer + residual_part
    grad_proj = grad_residual.astype(jnp.bfloat16)
    grad_out = jnp.einsum(
        "sbd,sbe->de", attended_low, grad_proj, preferred_element_type=jnp.float32
    )
    grad_attended = jnp.einsum(
        "sbe,de->sbd", grad_proj, w_out, preferred_element_type=jnp.float32
    ).reshape(head_shape)
    scaled = (grad_attended / weights_rows).astype(jnp.bfloat16)
    deltas = jnp.swapaxes(jnp.sum(grad_attended * attended, axis=-1), 1, 2) / weights

    def key_step(position, loop_state):
        moving, key_sums, query_sum = loop_state
        grad_queries, grad_keys, grad_values = backward_block(
            queries, scaled, deltas, segment_ids, moving[0], moving[1], moving[2]
        )
        query_next = query_sum + grad_queries
        keys_next = key_sums[0] + grad_keys
        values_next = key_sums[1] + grad_values
        moving = shifted((moving[0], moving[1], moving[2]), "blk", 1)
        key_sums = (
            shifted(keys_next.astype(jnp.bfloat16), "blk", 1).astype(keys_next.dtype),
            shifted(values_next.astype(jnp.bfloat16), "blk", 1).astype(values_next.dtype),
        )
        return (moving, key_sums, query_next)

    zero_heads = jnp.zeros(head_shape, jnp.float32)
    moved_back, key_sums, query_total = lax.fori_loop(
        0,
        blocks,
        key_step,
        ((key_part, value_part, segment_ids), (zero_heads, zero_heads), zero_heads),
    )
    keys_total, values_total = (key_sums[0], key_sums[1])
    grad_qkv_low = jnp.concatenate(
        [
            (query_total * 0.125).reshape(flat_shape),
            keys_total.reshape(flat_shape),
            values_total.reshape(flat_shape),
        ],
        axis=-1,
    ).astype(jnp.bfloat16)
    grad_qkv = jnp.einsum(
        "sbd,sbe->de", normed_low, grad_qkv_low, preferred_element_type=jnp.float32
    )
    grad_normed_one = jnp.einsum(
        "sbe,de->sbd", grad_qkv_low, w_qkv, preferred_element_type=jnp.float32
    )
    unused_one, pull_one = jax.vjp(layer_norm, tokens_wide, first_gain, first_shift)
    tokens_part, first_gain_grad, first_shift_grad = pull_one(grad_normed_one)
    tokens_grad = (grad_residual + tokens_part).astype(jnp.bfloat16)
    summed = (
        lax.psum_scatter(grad_qkv, ("dp", "blk"), scatter_dimension=0, tiled=True),
        lax.psum_scatter(grad_out, ("dp", "blk"), scatter_dimension=0, tiled=True),
        lax.psum_scatter(grad_in, ("dp", "blk"), scatter_dimension=0, tiled=True),
        lax.psum_scatter(grad_down, ("dp", "blk"), scatter_dimension=0, tiled=True),
        lax.psum_scatter(first_gain_grad, ("dp", "blk"), scatter_dimension=0, tiled=True),
        lax.psum_scatter(first_shift_grad, ("dp", "blk"), scatter_dimension=0, tiled=True),
        lax.psum_scatter(second_gain_grad, ("dp", "blk"), scatter_dimension=0, tiled=True),
        lax.psum_scatter(second_shift_grad, ("dp", "blk"), scatter_dimension=0, tiled=True),
    )
    cls_mean = sum_share / count
    cls_variance = square_share / count - cls_mean * cls_mean
    return (
        layer.astype(jnp.bfloat16),
        tokens_grad,
        summed[0],
        summed[1],
        summed[2],
        summed[3],
        summed[4],
        summed[5],
        summed[6],
        summed[7],
        cls_mean,
        cls_variance,
    )


MESH = pl.DeviceIdType.MESH
F32 = jnp.float32
BF16 = jnp.bfloat16
NN = (((1,), (0,)), ((), ()))
NT = (((1,), (1,)), ((), ()))
TN = (((0,), (0,)), ((), ()))


def mm(left, right, dims=NN):
    return lax.dot_general(left, right, dims, preferred_element_type=F32)


def remote(src, dst, send, recv, target):
    return pltpu.make_async_remote_copy(
        src_ref=src, dst_ref=dst, send_sem=send, recv_sem=recv, device_id=target, device_id_type=MESH
    )


def greet(targets):
    barrier = pltpu.get_barrier_semaphore()
    for target in targets:
        pl.semaphore_signal(barrier, inc=1, device_id=target, device_id_type=MESH)
    pl.semaphore_wait(barrier, len(targets))


def place():
    dp, blk = lax.axis_index("dp"), lax.axis_index("blk")
    return dp, blk, dp // 2, lax.rem(dp, 2), blk // 2, lax.rem(blk, 2)


def piece(index, size):
    return pl.ds(pl.multiple_of(index * size, size), size)


def flip(mine, other):
    return mine + other - 2 * mine * other


class RowGather:
    def __init__(self, rows, size, y, c, sibling, ypeer, send, recv, source=None):
        near, far = rows.at[y, piece(c, size)], rows.at[1 - y, piece(c, size)]
        source = near if source is None else source
        self.core = remote(source, near, send.at[0], recv.at[0], sibling)
        self.over = remote(source, near, send.at[1], recv.at[1], ypeer)
        self.last = remote(far, far, send.at[2], recv.at[2], sibling)

    def start(self):
        self.over.start()
        self.core.start()

    def forward(self):
        self.over.wait_recv()
        self.last.start()

    def arrive(self):
        self.core.wait_recv()
        self.last.wait_recv()

    def drain(self):
        for copy in (self.core, self.over, self.last):
            copy.wait_send()


class DpGather:
    def __init__(self, slots, z, x, blk, send, recv):
        self.slots, self.z, self.x, self.send, self.recv = slots, z, x, send, recv
        above, below = lax.rem(z + 1, 4), lax.rem(z + 3, 4)
        self.targets = ((2 * above + x, blk), (2 * below + x, blk), (2 * z + 1 - x, blk))

    def hop(self, kind, zz):
        slot = self.slots.at[self.x, zz]
        return remote(slot, slot, self.send.at[kind, zz], self.recv.at[self.x, zz], self.targets[kind])

    def up(self, zz):
        @pl.when(self.z < 3)
        def _():
            self.hop(0, zz).start()

        self.hop(2, zz).start()

    def down(self, zz):
        @pl.when(self.z > 0)
        def _():
            self.hop(1, zz).start()

    def start(self):
        self.up(self.z)
        self.down(self.z)

    def forward(self, step):
        below, above = self.z - step, self.z + step

        @pl.when(below >= 0)
        def _():
            self.hop(0, below).wait_recv()
            self.up(below)

        @pl.when(above <= 3)
        def _():
            self.hop(1, above).wait_recv()
            self.down(above)
            self.hop(2, above).start()

    def arrive(self, half):
        for k in range(2):
            slot = self.slots.at[1 - self.x, 2 * half + k]
            done = self.recv.at[1 - self.x, 2 * half + k]
            remote(slot, slot, self.send.at[2, k], done, self.targets[2]).wait_recv()

    def drain(self):
        for zz in range(4):
            self.hop(2, zz).wait_send()

            @pl.when((self.z < 3) & (zz <= self.z))
            def _():
                self.hop(0, zz).wait_send()

            @pl.when((self.z > 0) & (zz >= self.z))
            def _():
                self.hop(1, zz).wait_send()


def centered(values):
    center = values - jnp.mean(values, axis=-1, keepdims=True)
    spread = jnp.mean(center * center, axis=-1, keepdims=True)
    scale = lax.rsqrt(spread + EPSILON)
    return center * scale, scale


def norm_back(grad, unit, scale):
    return scale * (
        grad - jnp.mean(grad, axis=-1, keepdims=True) - unit * jnp.mean(grad * unit, axis=-1, keepdims=True)
    )


def half_of(pair, head):
    lanes = lax.broadcasted_iota(jnp.int32, pair.shape, 1) // 64
    return jnp.where(lanes == head, pair, jnp.zeros_like(pair))


def cells_at(cls_ref, places):
    found = jnp.zeros(places.shape, jnp.int32)
    for n in range(cls_ref.shape[1]):
        found = found + (places >= cls_ref[0, n]).astype(jnp.int32)
    return found


def same_cell(cls_ref, start, count, row_len):
    mine = lax.broadcasted_iota(jnp.int32, (count, 1), 0) + start
    other = lax.broadcasted_iota(jnp.int32, (1, row_len), 1)
    return cells_at(cls_ref, mine) == cells_at(cls_ref, other)


def gelu_parts(pre):
    cdf = 0.5 * (1.0 + lax.erf(pre * 0.7071067811865476))
    return cdf, cdf + pre * (0.3989422804014327 * jnp.exp(-0.5 * pre * pre))


def as_row(ref):
    return ref[...].reshape(1, ref.shape[0])


def layer_kernel(
    cls_ref, tok_hbm, grad_hbm, gain1_ref, shift1_ref, gain2_ref, shift2_ref, wqkv_ref, wout_ref, win_ref, wdown_ref,
    layer_out, tgrad_out, gqkv_out, gout_out, in_out, down_out, sums_ref,
    gg, rows_all, qkv_ref, att_ref, turned_ref, aturned_ref, attlow, abox, arow,
    layer_ref, tgrad_ref, gqkv_ref, gout_ref, in_ref, down_ref,
    st_in, st_dn, wi, wd, wo, gx, gp, ht, part_in, part_dn, sib_in, sib_dn, ysend_in, ysend_dn, yrecv_in, yrecv_dn,
    slab, slab_in, residual, unit, gnorm, grow, gatt, low, keys, values, part, xin, zout, zin, zlast, zfirst, hfirst, xfirst, full, fin, landing,
    sums, sbuf, sbox, tbox,
    isem, lsem, rsend, rrecv, ogsend, ogrecv, bsend, brecv, arsend, arrecv, outsem,
    wsem, ssem, osem, gsend, grecv, dsend, drecv, sibs, sibr, ysend, yrecv, qsend, qrecv,
    xsend, xrecv, zsend, zrecv, fsend, frecv, asend, arecv, usend, urecv, tsend, trecv,
):
    dp, blk, z, x, y, c = place()
    tokens, width = tok_hbm.shape
    row_len, both = 4 * tokens, 2 * tokens
    first, pairs = 5 * y + 3 * c, 3 - c
    cut, owned, rows = wi.shape[1], down_ref.shape[0], in_ref.shape[0]
    share = width // 8
    block = st_in.shape[2]
    steps = win_ref.shape[1] // block
    depth = st_in.shape[0]
    sibling, ypeer, diag = (dp, 2 * y + 1 - c), (dp, 2 * (1 - y) + c), (dp, 2 * (1 - y) + 1 - c)
    xpeer = (2 * z + 1 - x, blk)
    others = ((1, sibling), (2, ypeer), (3, diag))
    received = ((1, sibling, 2 + c), (2, ypeer, pairs), (3, diag, 2 + c))

    tok_in = pltpu.make_async_copy(tok_hbm, rows_all.at[y, piece(c, tokens), :], isem.at[0])
    grad_in = pltpu.make_async_copy(grad_hbm, gg.at[x, z], isem.at[1])
    tok_in.start()
    grad_in.start()

    def load(j, t):
        source = wqkv_ref.at[:, pl.ds(pl.multiple_of(t * width + (first + j) * 128, 128), 128)]
        return pltpu.make_async_copy(source, st_in.at[j, :, pl.ds(t * 128, 128)], lsem.at[j, t])

    @pl.loop(0, pairs)
    def _(j):
        for t in range(3):
            load(j, t).start()

    def stream_in(i):
        slot = lax.rem(i, depth)
        return pltpu.make_async_copy(win_ref.at[:, piece(i, block)], st_in.at[slot], ssem.at[0, slot])

    def stream_dn(i):
        slot = lax.rem(i, depth)
        return pltpu.make_async_copy(wdown_ref.at[piece(i, block), :], st_dn.at[slot], ssem.at[1, slot])

    tails = ((0, block), (1, block), (2, width - 2 * block))

    def load_out(i, size):
        return pltpu.make_async_copy(
            wout_ref.at[pl.ds(i * block, size), :], st_dn.at[i, pl.ds(0, size), :], ssem.at[1, i]
        )

    def load_rows(j):
        return pltpu.make_async_copy(wout_ref.at[piece(first + j, 128), :], wo.at[j], osem.at[j])

    greet([sibling, ypeer, diag] + [(lax.rem(dp + k, 8), blk) for k in range(1, 8)])
    row_tok = RowGather(rows_all, tokens, y, c, sibling, ypeer, rsend, rrecv, tok_hbm)
    grads = DpGather(gg, z, x, blk, ogsend, ogrecv)
    row_tok.start()
    tok_in.wait()
    grad_in.wait()
    grads.start()
    for i, size in tails:
        load_out(i, size).start()

    @pl.loop(0, pairs)
    def _(j):
        load_rows(j).start()
        for t in range(3):
            load(j, t).wait()

    normed_rows = wd

    @pl.loop(0, 2)
    def _(step):
        @pl.when(step == 0)
        def _():
            row_tok.core.wait_recv()

        @pl.when(step == 1)
        def _():
            row_tok.forward()
            row_tok.last.wait_recv()
            grads.forward(1)

        chip = flip(y, step)
        at = piece(chip, both)
        normed_rows[at, :] = (centered(rows_all[chip].astype(F32))[0] * as_row(gain1_ref) + as_row(shift1_ref)).astype(BF16)

        @pl.loop(0, pairs)
        def _(j):
            made = mm(normed_rows[at, :], st_in[j, :, 0:384])
            qkv_ref[j, at, 0:128] = (made[:, 0:128] * 0.125).astype(BF16)
            qkv_ref[j, at, 128:384] = made[:, 128:384].astype(BF16)

    for i in range(depth - 1):
        stream_in(i).start()

    def to_own(j, r, target):
        return remote(attlow.at[j, piece(target[1], tokens), :], abox.at[r, j], bsend.at[r, j], brecv.at[r, j], target)

    @pl.loop(0, pairs)
    def _(j):
        @pl.loop(0, 2)
        def _(part):
            at = piece(part, both)
            same = same_cell(cls_ref, part * both, both, row_len)
            pair = jnp.zeros((both, 128), F32)
            for head in range(2):
                scores = mm(half_of(qkv_ref[j, at, 0:128], head), qkv_ref[j, :, 128:256], NT)
                weigh = jnp.where(same, jnp.exp(scores), 0.0)
                total = jnp.sum(weigh, axis=-1, keepdims=True)
                pair = pair + half_of(mm(weigh.astype(BF16), qkv_ref[j, :, 256:384]) / total, head)
            att_ref[j, at, :] = pair
            attlow[j, at, :] = pair.astype(BF16)

        for r, target in others:
            to_own(j, r, target).start()
        abox[0, j] = attlow[j, piece(blk, tokens), :]

        @pl.when(j == 1)
        def _():
            grads.forward(2)

    for b in range(4):
        at = slice(b * tokens, (b + 1) * tokens)
        turned_ref[:, at] = normed_rows[at, :].T

    for r, target, count in received:

        @pl.loop(0, count)
        def _(j):
            to_own(j, r, target).wait_recv()

    own_at = (y, piece(c, tokens))
    for p in range(10):
        yy, cc = p // 5, (p % 5) // 3
        slot = 2 * flip(y, yy) + flip(c, cc)
        arow[y, piece(c, tokens), 128 * p : 128 * p + 128] = abox[slot, p % 5 - 3 * cc]
    row_att = RowGather(arow, tokens, y, c, sibling, ypeer, arsend, arrecv)

    made = rows_all[y, piece(c, tokens), :].astype(F32)
    for i, size in tails:
        load_out(i, size).wait()
        made = made + mm(arow[y, piece(c, tokens), i * block : i * block + size], st_dn[i, :size, :])
    for i in range(depth - 1):
        stream_dn(i).start()
    residual[...] = made
    made, scale2 = centered(made)
    unit[...] = made
    gx[x, z] = (made * as_row(gain2_ref) + as_row(shift2_ref)).astype(BF16)
    normed = DpGather(gx, z, x, blk, dsend, drecv)
    normed.start()
    row_att.start()
    gnorm[...] = jnp.zeros_like(gnorm)

    @pl.loop(0, steps)
    def _(i):
        slot = lax.rem(i, depth)

        @pl.when(i + depth - 1 < steps)
        def _():
            stream_in(i + depth - 1).start()
            stream_dn(i + depth - 1).start()

        stream_in(i).wait()
        stream_dn(i).wait()
        pre = mm(gx[x, z], st_in[slot])
        cdf, slope = gelu_parts(pre)
        grad = (mm(gg[x, z], st_dn[slot], NT) * slope).astype(BF16)
        residual[...] += mm((pre * cdf).astype(BF16), st_dn[slot])
        gnorm[...] += mm(grad, st_in[slot], NT)

        @pl.when(i == 2)
        def _():
            grads.forward(3)

        @pl.when(i == 6)
        def _():
            row_att.forward()
            normed.forward(1)

    load_in = pltpu.make_async_copy(win_ref.at[:, piece(dp, cut)], wi, wsem.at[0])
    load_dn = pltpu.make_async_copy(wdown_ref.at[piece(dp, cut), :], wd, wsem.at[1])
    load_in.start()
    load_dn.start()
    layer = residual[...]
    layer_ref[...] = layer.astype(BF16)
    outs = [pltpu.make_async_copy(layer_ref, layer_out, outsem.at[0])]
    outs[0].start()
    sums[...] = jnp.zeros_like(sums)
    spots = lax.broadcasted_iota(jnp.int32, (tokens, 1), 0) + blk * tokens
    chosen = jnp.zeros((tokens, 1), F32)
    for n in range(cls_ref.shape[1]):
        chosen = chosen + (spots == cls_ref[0, n]).astype(F32)
    sums[4:5, :] = jnp.sum(chosen * layer, axis=0, keepdims=True)
    sums[5:6, :] = jnp.sum(chosen * layer * layer, axis=0, keepdims=True)
    grad = gnorm[...]
    sums[2:3, :] = jnp.sum(grad * unit[...], axis=0, keepdims=True)
    sums[3:4, :] = jnp.sum(grad, axis=0, keepdims=True)
    made = gg[x, z].astype(F32) + norm_back(grad * as_row(gain2_ref), unit[...], scale2)
    residual[...] = made
    grow[y, piece(c, tokens), :] = made.astype(BF16)
    row = RowGather(grow, tokens, y, c, sibling, ypeer, gsend, grecv)
    row.start()
    normed.forward(2)
    load_in.wait()
    load_dn.wait()

    def stream_qkv(p, t):
        slot = lax.rem(p, depth)
        source = wqkv_ref.at[:, pl.ds(pl.multiple_of(t * width + p * 128, 128), 128)]
        return pltpu.make_async_copy(source, st_in.at[slot, :, pl.ds(t * 128, 128)], wsem.at[2 + 3 * slot + t])

    for p in range(depth):
        for t in range(3):
            stream_qkv(p, t).start()
    near = z // 2

    def make(xx, half):
        at = piece(2 * xx + half, both)
        pre = mm(gx[xx, piece(half, 2)].reshape(both, width), wi[...])
        cdf, slope = gelu_parts(pre)
        ht[:, at] = (pre * cdf).astype(BF16).T
        gp[at, :] = (mm(gg[xx, piece(half, 2)].reshape(both, width), wd[...], NT) * slope).astype(BF16)

    def makes(first_step, last_step):
        @pl.loop(first_step, last_step)
        def _(step):
            make(flip(x, lax.rem(step, 2)), flip(near, step // 2))

    makes(0, 1)
    row_att.arrive()
    for b in range(4):
        aturned_ref[:, b * tokens : (b + 1) * tokens] = arow[b // 2, (b % 2) * tokens : (b % 2 + 1) * tokens, :].T
    row.forward()
    row.arrive()

    @pl.loop(0, pairs)
    def _(j):
        load_rows(j).wait()
        gatt[j] = mm(grow[...].reshape(row_len, width), wo[j], NT)

    even, pair_z, half_z = lax.rem(z, 2), z + 1 - 2 * lax.rem(z, 2), lax.rem(z + 2, 4)

    def to_x(s):
        return remote(part.at[s, 1 - x], xin.at[s - 1], xsend.at[s], xrecv.at[s], xpeer)

    def to_pair(s):
        return remote(zout.at[s - 1, 1 - even], zin.at[s - 1], zsend.at[s, 0], zrecv.at[s, 0], (2 * pair_z + x, blk))

    def to_half(s):
        return remote(zlast.at[s - 1, 0], zlast.at[s - 1, 1], zsend.at[s, 1], zrecv.at[s, 1], (2 * half_z + x, blk))

    other_half, my_half = 1 - z // 2, z // 2
    def first_moves(wide):
        lanes = pl.ds(0, wide)
        return (
            lambda: remote(
                part.at[0, :, 1 - even, :, :, lanes], zfirst.at[:, :, :, lanes], zsend.at[0, 0], zrecv.at[0, 0],
                (2 * pair_z + x, blk),
            ),
            lambda: remote(
                hfirst.at[0, :, :, lanes], hfirst.at[1, :, :, lanes], zsend.at[0, 1], zrecv.at[0, 1],
                (2 * half_z + x, blk),
            ),
            lambda: remote(xfirst.at[0, :, lanes], xfirst.at[1, :, lanes], xsend.at[0], xrecv.at[0], xpeer),
        )

    def first_move(stage, act):
        for core in range(2):

            @pl.when(c == core)
            def _():
                act(first_moves(128 * (3 - core))[stage]())

    def begin(copy):
        copy.start()

    def finish_copy(copy):
        copy.wait()

    def to_blk(s, r, target):
        return remote(full.at[s, target[1]], fin.at[r, s], fsend.at[r, s], frecv.at[r, s], target)

    def to_low(j, r, target):
        return remote(low.at[j, piece(target[1], tokens), :], landing.at[r, j], asend.at[r, j], arecv.at[r, j], target)

    def add_x(s):
        to_x(s).wait()
        for k in range(4):
            zout[s - 1, k // 2, k % 2] = (part[s, x, k // 2, k % 2].astype(F32) + xin[s - 1, k // 2, k % 2].astype(F32)).astype(BF16)
        to_pair(s).start()

    def add_pair(s):
        to_pair(s).wait()
        away = 1 - z // 2
        zlast[s - 1, 0] = (zout[s - 1, even, away].astype(F32) + zin[s - 1, away].astype(F32)).astype(BF16)
        to_half(s).start()

    def add_half(s):
        to_half(s).wait()
        mine = z // 2
        total = zout[s - 1, even, mine].astype(F32) + zin[s - 1, mine].astype(F32) + zlast[s - 1, 1].astype(F32)
        to_owners(s, total)

    def to_owners(s, total):
        for b in range(4):
            full[s, b] = total[b * rows : (b + 1) * rows].astype(BF16)
        for r, target in others:
            to_blk(s, r, target).start()
        fin[0, s] = full[s, blk]

    def first_a():
        first_move(0, finish_copy)
        for xx in range(2):
            hfirst[0, xx] = (part[0, xx, even, other_half].astype(F32) + zfirst[xx, other_half].astype(F32)).astype(BF16)
        first_move(1, begin)

    def first_sum(xx):
        return part[0, xx, even, my_half].astype(F32) + zfirst[xx, my_half].astype(F32) + hfirst[1, xx].astype(F32)

    def first_b():
        first_move(1, finish_copy)
        xfirst[0] = first_sum(1 - x).astype(BF16)
        first_move(2, begin)

    def first_c():
        first_move(2, finish_copy)
        to_owners(0, first_sum(x) + xfirst[1].astype(F32))

    def weight_part(s, left, right):
        @pl.loop(0, 4)
        def _(zz):
            made = mm(left[piece(zz, 2 * share), :], right)
            part[s, 0, lax.rem(zz, 2), zz // 2] = made[:share].astype(BF16)
            part[s, 1, lax.rem(zz, 2), zz // 2] = made[share:].astype(BF16)

    @pl.when(c == 0)
    def _():
        weight_part(0, aturned_ref, grow[:, :, pl.ds(pl.multiple_of(first * 128, 128), 384)].reshape(row_len, 384))

    @pl.when(c == 1)
    def _():
        right = grow[:, :, pl.ds(pl.multiple_of(first * 128, 128), 256)].reshape(row_len, 256)
        weight_part(0, aturned_ref, jnp.concatenate([right, jnp.zeros((row_len, 128), BF16)], axis=1))

    first_move(0, begin)
    normed.forward(3)
    to_sibling = []
    for kind, source, box in ((0, part_in, sib_in), (1, part_dn, sib_dn)):
        for yy in range(2):
            away = source.at[2 * yy + (1 - c)]
            to_sibling.append(remote(away, box.at[yy], sibs.at[kind, yy], sibr.at[kind, yy], sibling))
    to_y = (
        remote(ysend_in, yrecv_in, ysend.at[0], yrecv.at[0], ypeer),
        remote(ysend_dn, yrecv_dn, ysend.at[1], yrecv.at[1], ypeer),
    )

    over = 2 * (1 - y) + c

    @pl.loop(0, pairs)
    def _(j):
        keys[...] = jnp.zeros_like(keys)
        values[...] = jnp.zeros_like(values)

        @pl.loop(0, 2)
        def _(half):
            at = piece(half, both)
            same = same_cell(cls_ref, half * both, both, row_len)
            queries_grad = jnp.zeros((both, 128), F32)
            for head in range(2):
                query = half_of(qkv_ref[j, at, 0:128], head)
                key = half_of(qkv_ref[j, :, 128:256], head)
                grad = half_of(gatt[j, at, :], head)
                weigh = jnp.where(same, jnp.exp(mm(query, key, NT)), 0.0)
                total = jnp.sum(weigh, axis=-1, keepdims=True)
                scaled = (grad / total).astype(BF16)
                delta = jnp.sum(grad * att_ref[j, at, :], axis=-1, keepdims=True) / total
                spread = mm(scaled, qkv_ref[j, :, 256:384], NT)
                score = (weigh * (spread - delta)).astype(BF16)
                queries_grad = queries_grad + mm(score, key)
                keys[...] += mm(score, query, TN)
                values[...] += mm(weigh.astype(BF16), scaled, TN)
            low[j, at, 0:128] = (queries_grad * 0.125).astype(BF16)

        low[j, :, 128:256] = keys[...].astype(BF16)
        low[j, :, 256:384] = values[...].astype(BF16)
        for r, target in others:
            to_low(j, r, target).start()
        weight_part(j + 1, turned_ref, low[j])

        @pl.when(j == 0)
        def _():
            to_x(1).start()

        @pl.when(j == pairs - 1)
        def _():
            for half in range(2):
                normed.arrive(half)
                grads.arrive(half)
            to_x(2).start()

            @pl.when(c == 0)
            def _():
                to_x(3).start()

            makes(1, 4)
            first_a()

            @pl.loop(0, 2)
            def _(half):
                left = gx[:, :, :, piece(half, width // 2)].reshape(8 * tokens, width // 2)
                made = mm(left, gp[...], TN)
                for n in range(4):
                    for q in range(4):
                        at = n * share + q * rows
                        part_in[q, 4 * half + n] = made[at : at + rows].astype(BF16)

            to_sibling[0].start()
            to_sibling[1].start()
            every = gg[...].reshape(8 * tokens, width)

            @pl.loop(0, 4)
            def _(q):
                part_dn[q] = mm(ht[piece(q, owned), :], every).astype(BF16)

            to_sibling[2].start()
            to_sibling[3].start()
            to_sibling[0].wait()
            to_sibling[1].wait()
            ysend_in[...] = (part_in[over].astype(F32) + sib_in[1 - y].astype(F32)).astype(BF16)
            to_y[0].start()
            to_sibling[2].wait()
            to_sibling[3].wait()
            ysend_dn[...] = (part_dn[over].astype(F32) + sib_dn[1 - y].astype(F32)).astype(BF16)
            first_b()
            add_x(1)

    add_x(2)
    add_pair(1)

    mine = 2 * y + c
    to_q = []
    for k in range(1, 8):
        target = lax.rem(dp + k, 8)
        to_q.append(remote(slab.at[target], slab_in.at[dp], qsend.at[k], qrecv.at[k], (target, blk)))

    def start_q():
        to_y[0].wait()
        to_y[1].start()
        total = part_in[mine].astype(F32) + sib_in[y].astype(F32) + yrecv_in[...].astype(F32)
        slab[...] = total.astype(BF16)
        for copy in to_q:
            copy.start()
        slab_in[dp] = slab[dp]

    start_q()
    @pl.when(c == 0)
    def _():
        add_x(3)

    first_c()

    @pl.loop(0, pairs)
    def _(j):
        landing[0, j] = low[j, piece(blk, tokens), :]
        for r, target in others:
            to_low(j, r, target).wait_send()

    for r, target, count in received:

        @pl.loop(0, count)
        def _(j):
            to_low(j, r, target).wait_recv()

    gnorm[...] = jnp.zeros_like(gnorm)
    @pl.loop(0, 10)
    def _(p):
        @pl.when((p > 0) & (p + depth - 1 < 10))
        def _():
            for t in range(3):
                stream_qkv(p + depth - 1, t).start()

        for t in range(3):
            stream_qkv(p, t).wait()
        yy, pp = p // 5, lax.rem(p, 5)
        cc = pp // 3
        slot = 2 * flip(y, yy) + flip(c, cc)
        gnorm[...] += mm(landing[slot, pp - 3 * cc], st_in[lax.rem(p, depth), :, 0:384], NT)

    grad = gnorm[...]
    made, scale1 = centered(rows_all[y, piece(c, tokens), :].astype(F32))
    sums[0:1, :] = jnp.sum(grad * made, axis=0, keepdims=True)
    sums[1:2, :] = jnp.sum(grad, axis=0, keepdims=True)
    sbuf[...] = jnp.zeros_like(sbuf)
    for k in range(8):
        sbuf[k, :, 0:share] = sums[:, k * share : (k + 1) * share]
    to_u = []
    for k in range(1, 8):
        target = lax.rem(dp + k, 8)
        to_u.append(remote(sbuf.at[target], sbox.at[dp], usend.at[k], urecv.at[k], (target, blk)))
        to_u[-1].start()
    sbox[dp] = sbuf[dp]
    tgrad_ref[...] = (residual[...] + norm_back(grad * as_row(gain1_ref), made, scale1)).astype(BF16)
    outs.append(pltpu.make_async_copy(tgrad_ref, tgrad_out, outsem.at[1]))
    outs[-1].start()

    def end_down():
        to_y[1].wait()
        down_ref[...] = part_dn[mine].astype(F32) + sib_dn[y].astype(F32) + yrecv_dn[...].astype(F32)
        outs.append(pltpu.make_async_copy(down_ref, down_out, outsem.at[2]))
        outs[-1].start()

    def end_q():
        for copy in to_q:
            copy.wait()
        for s in range(8):
            in_ref[:, s * cut : (s + 1) * cut] = slab_in[s].astype(F32)
        outs.append(pltpu.make_async_copy(in_ref, in_out, outsem.at[3]))
        outs[-1].start()

    to_t = [remote(tbox.at[0], tbox.at[r], tsend.at[r], trecv.at[r], target) for r, target in others]

    def start_t():
        for copy in to_u:
            copy.wait()
        tbox[0] = jnp.sum(sbox[...], axis=0)
        for copy in to_t:
            copy.start()

    def end_t():
        for copy in to_t:
            copy.wait()
        total = (tbox[0] + tbox[1]) + (tbox[2] + tbox[3])
        for b in range(4):

            @pl.when(blk == b)
            def _():
                sums_ref[...] = total[:, b * rows : (b + 1) * rows]

    add_pair(2)
    add_half(1)

    @pl.when(c == 0)
    def _():
        add_pair(3)

    start_t()
    add_half(2)

    @pl.when(c == 0)
    def _():
        add_half(3)

    for r, target in others:
        to_blk(0, r, target).wait_recv()
    for yy in range(2):
        for cc in range(2):
            p, wide = 5 * yy + 3 * cc, 128 * (3 - cc)
            gout_ref[:, 128 * p : 128 * p + wide] = fin[2 * flip(y, yy) + flip(c, cc), 0, :, :wide].astype(F32)
    outs.append(pltpu.make_async_copy(gout_ref, gout_out, outsem.at[5]))
    outs[-1].start()
    end_down()
    end_t()
    end_q()

    @pl.loop(0, pairs + 1)
    def _(s):
        for r, target in others:
            to_blk(s, r, target).wait_send()

    for r, target, count in received:

        @pl.loop(1, count + 1)
        def _(s):
            to_blk(s, r, target).wait_recv()

    for yy in range(2):
        for cc in range(2):
            slot = 2 * flip(y, yy) + flip(c, cc)
            p = 5 * yy + 3 * cc
            for j in range(3 - cc):
                for t in range(3):
                    at = t * width + 128 * (p + j)
                    gqkv_ref[:, at : at + 128] = fin[slot, j + 1, :, 128 * t : 128 * t + 128].astype(F32)
    outs.append(pltpu.make_async_copy(gqkv_ref, gqkv_out, outsem.at[4]))
    outs[-1].start()

    @pl.loop(0, pairs)
    def _(j):
        for r, target in others:
            to_own(j, r, target).wait_send()

    for gather in (row_tok, row_att, row, grads, normed):
        gather.drain()
    for copy in outs:
        copy.wait()


def finish_kernel(cells, sums_ref, *refs):
    count = 6
    arrays, (mean_ref, variance_ref, *grads), outs = refs[:count], refs[count : count + 6], refs[count + 6 : 2 * count + 6]
    held, isem, osem = refs[2 * count + 6 : -2], refs[-2], refs[-1]
    loads = [pltpu.make_async_copy(arrays[i], held[i], isem.at[i]) for i in range(count)]
    stores = [pltpu.make_async_copy(held[i], outs[i], osem.at[i]) for i in range(count)]
    for load in loads:
        load.start()
    for load, store in zip(loads, stores):
        load.wait()
        store.start()
    mean = sums_ref[4:5, :] / cells
    mean_ref[...] = mean
    variance_ref[...] = sums_ref[5:6, :] / cells - mean * mean
    for i in range(4):
        grads[i][...] = sums_ref[i : i + 1, :]
    for store in stores:
        store.wait()


def finish(cells, sums, *arrays):
    anywhere, v = pl.BlockSpec(memory_space=pl.ANY), pl.BlockSpec(memory_space=pltpu.VMEM)
    count = len(arrays)
    small = jax.ShapeDtypeStruct((1, sums.shape[1]), F32)
    return pl.pallas_call(
        functools.partial(finish_kernel, cells),
        out_shape=(small,) * 6 + tuple(jax.ShapeDtypeStruct(a.shape, a.dtype) for a in arrays),
        in_specs=[v] + [anywhere] * count,
        out_specs=(v,) * 6 + (anywhere,) * count,
        scratch_shapes=[pltpu.VMEM(a.shape, a.dtype) for a in arrays]
        + [pltpu.SemaphoreType.DMA((count,)), pltpu.SemaphoreType.DMA((count,))],
    )(sums, *arrays)


def whole_layer(cls_positions, tokens, grad, gain1, shift1, gain2, shift2, w_qkv, w_out, w_in, w_down):
    count, width = tokens.shape
    inner = w_in.shape[1]
    row_len, share = 4 * count, width // 8
    cut, owned, rows = inner // 8, inner // 32, width // 32
    block, depth = 512, 3
    v = pltpu.VMEM
    dma = pltpu.SemaphoreType.DMA
    anywhere = pl.BlockSpec(memory_space=pl.ANY)
    return pl.pallas_call(
        layer_kernel,
        out_shape=(
            jax.ShapeDtypeStruct((count, width), BF16),
            jax.ShapeDtypeStruct((count, width), BF16),
            jax.ShapeDtypeStruct((rows, 3 * width), F32),
            jax.ShapeDtypeStruct((rows, width), F32),
            jax.ShapeDtypeStruct((rows, inner), F32),
            jax.ShapeDtypeStruct((owned, width), F32),
            jax.ShapeDtypeStruct((8, rows), F32),
        ),
        in_specs=[pl.BlockSpec(memory_space=pltpu.SMEM)]
        + [anywhere] * 2
        + [pl.BlockSpec(memory_space=v)] * 4
        + [anywhere] * 4,
        out_specs=(anywhere,) * 6 + (pl.BlockSpec(memory_space=v),),
        scratch_shapes=[
            v((2, 4, count, width), BF16), v((2, 2 * count, width), BF16),
            v((3, row_len, 384), BF16), v((3, row_len, 128), F32), v((width, row_len), BF16), v((width, row_len), BF16),
            v((3, row_len, 128), BF16), v((4, 3, count, 128), BF16), v((2, 2 * count, width), BF16),
            v((count, width), BF16), v((count, width), BF16), v((rows, 3 * width), F32), v((rows, width), F32),
            v((rows, inner), F32), v((owned, width), F32),
            v((depth, width, block), BF16), v((depth, block, width), BF16),
            v((width, cut), BF16), v((cut, width), BF16), v((3, 128, width), BF16),
            v((2, 4, count, width), BF16), v((8 * count, cut), BF16), v((cut, 8 * count), BF16),
            v((4, 8, rows, cut), BF16), v((4, owned, width), BF16),
            v((2, 8, rows, cut), BF16), v((2, owned, width), BF16),
            v((8, rows, cut), BF16), v((owned, width), BF16), v((8, rows, cut), BF16), v((owned, width), BF16),
            v((8, rows, cut), BF16), v((8, rows, cut), BF16),
            v((count, width), F32), v((count, width), F32), v((count, width), F32),
            v((2, 2 * count, width), BF16), v((3, row_len, 128), F32), v((3, row_len, 384), BF16),
            v((row_len, 128), F32), v((row_len, 128), F32),
            v((4, 2, 2, 2, share, 384), BF16), v((3, 2, 2, share, 384), BF16), v((3, 2, 2, share, 384), BF16),
            v((3, 2, share, 384), BF16), v((3, 2, share, 384), BF16),
            v((2, 2, share, 384), BF16), v((2, 2, share, 384), BF16), v((2, share, 384), BF16),
            v((4, 4, share // 4, 384), BF16), v((4, 4, share // 4, 384), BF16),
            v((4, 3, count, 384), BF16),
            v((8, width), F32), v((8, 8, 256), F32), v((8, 8, 256), F32), v((4, 8, 256), F32),
            dma((2,)), dma((3, 3)), dma((3,)), dma((3,)), dma((3, 4)), dma((2, 4)), dma((4, 3)), dma((4, 3)),
            dma((3,)), dma((3,)), dma((6,)),
            dma((2 + 3 * depth,)), dma((2, depth)), dma((3,)), dma((3,)), dma((3,)), dma((3, 4)), dma((2, 4)),
            dma((2, 2)), dma((2, 2)), dma((2,)), dma((2,)), dma((8,)), dma((8,)),
            dma((4,)), dma((4,)), dma((4, 3)), dma((4, 3)), dma((4, 4)), dma((4, 4)), dma((4, 3)), dma((4, 3)),
            dma((8,)), dma((8,)), dma((4,)), dma((4,)),
        ],
        compiler_params=pltpu.CompilerParams(collective_id=1, has_side_effects=True, vmem_limit_bytes=64 * 2**20),
        cost_estimate=pl.CostEstimate(flops=40 * 2**30, bytes_accessed=50 * 2**20, transcendentals=0),
    )(cls_positions, tokens, grad, gain1, shift1, gain2, shift2, w_qkv, w_out, w_in, w_down)


def on_device(
    tokens,
    first_gain,
    first_shift,
    w_qkv,
    w_out,
    second_gain,
    second_shift,
    w_in,
    w_down,
    segment_ids,
    cls_positions,
    out_grad,
):
    tokens, out_grad = tokens[0], out_grad[0]
    layer, tokens_grad, grad_qkv, grad_out, grad_in, grad_down, sums = whole_layer(
        cls_positions, tokens, out_grad, first_gain, first_shift, second_gain, second_shift, w_qkv, w_out, w_in, w_down
    )
    mean, variance, gain1_grad, shift1_grad, gain2_grad, shift2_grad, *large = finish(
        cls_positions.size * lax.axis_size("dp"), sums, layer, tokens_grad, grad_qkv, grad_out, grad_in, grad_down
    )
    return (
        large[0][None],
        large[1][None],
        *large[2:],
        gain1_grad[0],
        shift1_grad[0],
        gain2_grad[0],
        shift2_grad[0],
        mean[0],
        variance[0],
    )


def solution(mesh):
    placed = (
        P("dp", "blk", None),
        P(),
        P(),
        P(),
        P(),
        P(),
        P(),
        P(),
        P(),
        P("dp", "blk"),
        P("dp", None),
        P("dp", "blk", None),
    )
    small = mesh.shape["dp"] == 8 and mesh.shape["blk"] == 4
    return jax.shard_map(
        on_device if small else on_device_general,
        mesh=mesh,
        in_specs=placed,
        out_specs=(
            P("dp", "blk", None),
            P("dp", "blk", None),
            P(("dp", "blk"), None),
            P(("dp", "blk"), None),
            P(("dp", "blk"), None),
            P(("dp", "blk"), None),
            P(("dp", "blk")),
            P(("dp", "blk")),
            P(("dp", "blk")),
            P(("dp", "blk")),
            P(("dp", "blk")),
            P(("dp", "blk")),
        ),
        check_vma=False,
    )
```
